32 devices in a mesh: dp: 8 (over y, x, core), ctx: 4 (over z).
Axes of the slice: x: 2, y: 2, z: 4, core: 2. Of those that a mesh axis runs over, the one named last changes fastest.
Arguments:
- tokens: bfloat16 [8, 2048, 1024], P('dp', 'ctx'), may hold values from -6 to 6
- lengths: int32 [8], P('dp'), may hold values from 1 to 2048, 12288 in all
- cotangent: bfloat16 [8, 2048, 1024], P('dp', 'ctx'), may hold values from -6 to 6
- query_weight: bfloat16 [1024, 1024], P(('dp', 'ctx')), may hold values from -0.1875 to 0.1875
- key_weight: bfloat16 [1024, 1024], P(('dp', 'ctx')), may hold values from -0.1875 to 0.1875
- value_weight: bfloat16 [1024, 1024], P(('dp', 'ctx')), may hold values from -0.1875 to 0.1875
- output_weight: bfloat16 [1024, 1024], P(('dp', 'ctx')), may hold values from -4 to 4
- gate_weight: bfloat16 [1024, 4096], P(('dp', 'ctx')), may hold values from -0.1875 to 0.1875
- up_weight: bfloat16 [1024, 4096], P(('dp', 'ctx')), may hold values from -0.1875 to 0.1875
- down_weight: bfloat16 [4096, 1024], P(('dp', 'ctx')), may hold values from -0.09375 to 0.09375
- attention_gain: bfloat16 [1024], P(('dp', 'ctx')), may hold values from 0.099609375 to 1.8984375
- attention_shift: bfloat16 [1024], P(('dp', 'ctx')), may hold values from -1.5 to 1.5
- feed_gain: bfloat16 [1024], P(('dp', 'ctx')), may hold values from 0.099609375 to 1.8984375
- feed_shift: bfloat16 [1024], P(('dp', 'ctx')), may hold values from -1.5 to 1.5
Outputs:
- output: bfloat16 [8, 2048, 1024], P('dp', 'ctx')
- tokens_grad: bfloat16 [8, 2048, 1024], P('dp', 'ctx')
- query_grad: float32 [1024, 1024], P(('dp', 'ctx'))
- key_grad: float32 [1024, 1024], P(('dp', 'ctx'))
- value_grad: float32 [1024, 1024], P(('dp', 'ctx'))
- output_grad: float32 [1024, 1024], P(('dp', 'ctx'))
- gate_grad: float32 [1024, 4096], P(('dp', 'ctx'))
- up_grad: float32 [1024, 4096], P(('dp', 'ctx'))
- down_grad: float32 [4096, 1024], P(('dp', 'ctx'))
- attention_gain_grad: float32 [1024], P(('dp', 'ctx'))
- attention_shift_grad: float32 [1024], P(('dp', 'ctx'))
- feed_gain_grad: float32 [1024], P(('dp', 'ctx'))
- feed_shift_grad: float32 [1024], P(('dp', 'ctx'))
The draws below stay inside these ranges and needn't reach their ends.
Inputs may be any that keep to these rules, and one draw needn't show every extreme that they name: `lengths`: positions below a window's length are real, the rest padding; some window has length 2048.
All inputs are finite; a program needn't handle non-finite values. No bound on the sum of `lengths` on one device may be relied on, other than what follows from the above.
Results may differ from the reference program's by a relative error of at most 0.023.
Values may be sent and summed in bfloat16 or wider, within the bound.
No kernel may reach another device: no remote copies, remote signals or barrier semaphores. Data moves between devices by JAX's collectives and lax.ppermute only.
A program may use at most 192 MiB of HBM per device.

```python
import math
import jax
import jax.numpy as jnp
import numpy as np
from jax import lax

D = 1024
H = 16
HD = 64
FF = 4096
L = 2048
WINDOWS = 8


def steps_of(rng, dims, pieces, low, top_value):
    level = 1.0
    for dim, blocks in pieces:
        heights = jax.random.uniform(jax.random.fold_in(jax.random.fold_in(rng, 6), dim), (blocks,), jnp.float32, low / len(pieces), top_value / len(pieces))
        level = level * jnp.repeat(jnp.exp(heights), dims[dim] // blocks).reshape((-1,) + (1,) * (len(dims) - 1 - dim))
    return level


def profile(count, total, reach, lean):
    portions = [(1 << 20) // math.isqrt(rank ** lean) + 1 for rank in range(2, count + 1)]
    rest, counts = total - reach - (count - 1), [1] * (count - 1)
    while rest > 0:
        candidates = [i for i in range(count - 1) if counts[i] < reach]
        mass, left = sum([portions[i] for i in candidates]), rest
        for i in candidates:
            more = min(reach - counts[i], max(1, left * portions[i] // mass), rest)
            counts[i] = counts[i] + more
            rest = rest - more
    return np.array([reach] + counts)


def uneven(rng, count, total, bound, slope):
    if count == 2:
        one = jax.random.randint(rng, (), max(1, total - bound), min(bound, total - 1) + 1)
        return jnp.stack([one, total - one])
    sizes = jnp.asarray(profile(count, total, bound, slope), jnp.int32)
    twos = (count - 1) // 2
    donor, taker = sizes[1:1 + 2 * twos:2], sizes[2:2 + 2 * twos:2]
    room = jnp.minimum(donor - 1, bound - taker)
    passed = jax.random.randint(jax.random.fold_in(rng, 1), (twos,), 0, 1 << 20) % (room + 1)
    sizes = sizes.at[1:1 + 2 * twos:2].set(donor - passed).at[2:2 + 2 * twos:2].set(taker + passed)
    return sizes[jax.random.permutation(jax.random.fold_in(rng, 2), count)]


def bell_draw(stream_key, dims, width, bound, shards=(), kind=jnp.bfloat16):
    drawn = width * jax.random.normal(stream_key, dims, jnp.float32)
    if shards:
        drawn = drawn * steps_of(stream_key, dims, shards, -0.22, 0.18)
    return jnp.clip(drawn, -bound, bound).astype(kind)


def setup_inputs(seed: int = 0) -> dict:
    key_of = jax.random.split(jax.random.key(seed), 15)
    tokens = bell_draw(key_of[0], (WINDOWS, L, D), 1.0, 6.0, ((0, 8), (1, 4)))
    lengths = uneven(key_of[1], WINDOWS, WINDOWS * L * 3 // 4, L, 2).astype(jnp.int32)
    cotangent = bell_draw(key_of[2], (WINDOWS, L, D), 1.0, 6.0, ((0, 8), (1, 4)))
    query_weight = bell_draw(key_of[3], (D, D), D ** -0.5, 0.1875, ((0, 32),))
    key_weight = bell_draw(key_of[4], (D, D), D ** -0.5, 0.1875, ((0, 32),))
    value_weight = bell_draw(key_of[5], (D, D), D ** -0.5, 0.1875, ((0, 32),))
    output_weight = bell_draw(key_of[6], (D, D), (D * 4 // L) ** -0.5, 4.0, ((0, 32),))
    gate_weight = bell_draw(key_of[7], (D, FF), D ** -0.5, 0.1875, ((0, 32),))
    up_weight = bell_draw(key_of[8], (D, FF), D ** -0.5, 0.1875, ((0, 32),))
    down_weight = bell_draw(key_of[9], (FF, D), FF ** -0.5, 0.09375, ((0, 32),))
    attention_gain = jnp.clip(1.0 + 0.18 * jax.random.normal(key_of[10], (D,), jnp.float32), 0.099609375, 1.8984375).astype(jnp.bfloat16)
    attention_shift = bell_draw(key_of[11], (D,), 0.3, 1.5, ((0, 32),))
    feed_gain = jnp.clip(1.0 + 0.18 * jax.random.normal(key_of[12], (D,), jnp.float32), 0.099609375, 1.8984375).astype(jnp.bfloat16)
    feed_shift = bell_draw(key_of[13], (D,), 0.3, 1.5, ((0, 32),))
    return {"tokens": tokens, "lengths": lengths, "cotangent": cotangent, "query_weight": query_weight, "key_weight": key_weight, "value_weight": value_weight, "output_weight": output_weight, "gate_weight": gate_weight, "up_weight": up_weight, "down_weight": down_weight, "attention_gain": attention_gain, "attention_shift": attention_shift, "feed_gain": feed_gain, "feed_shift": feed_shift}


@jax.custom_vjp
def low(v):
    return lax.optimization_barrier(v.astype(jnp.bfloat16)).astype(jnp.float32)

@jax.custom_vjp
def low_back(v):
    return v

def low_keep(v):
    return (low(v), None)

def low_pass(kept, grad):
    return (grad,)

def back_keep(v):
    return (v, None)

def back_low(kept, grad):
    return (low(grad),)
low.defvjp(low_keep, low_pass)
low_back.defvjp(back_keep, back_low)
epsilon = 1e-05
masked_score = -1e+30

def layer_norm(values, gain, shift):
    centre = values - lax.optimization_barrier(jnp.mean(values, axis=-1, keepdims=True))
    spread = lax.optimization_barrier(jnp.mean(centre * centre, axis=-1, keepdims=True))
    return centre * lax.rsqrt(spread + epsilon) * gain + shift

def rotary_tables(positions):
    half = HD // 2
    freqs = jnp.exp(jnp.arange(half, dtype=jnp.float32) * (-2.0 * math.log(10000.0) / HD))
    angles = positions.astype(jnp.float32)[:, None] * freqs[None, :]
    cosine = jnp.concatenate([jnp.cos(angles), jnp.cos(angles)], axis=-1)
    sine = jnp.concatenate([jnp.sin(angles), jnp.sin(angles)], axis=-1)
    return (cosine, sine)

def rotate(values, cosine, sine):
    half = HD // 2
    turned = jnp.concatenate([-values[..., half:], values[..., :half]], axis=-1)
    return values * cosine[:, None, :] + turned * sine[:, None, :]

def matmul(left, right):
    return jnp.dot(left, right, precision=lax.Precision.HIGHEST)

def window_forward(params, inputs, valid):
    query_w, key_w, value_w, out_w, gate_w, up_w, down_w, gain_one, shift_one, gain_two, shift_two = params
    scale = 1.0 / math.sqrt(HD)
    cosine, sine = rotary_tables(jnp.arange(L, dtype=jnp.int32))
    normed = low(layer_norm(inputs, gain_one, shift_one))
    queries = low(rotate(low_back(matmul(normed, query_w)).reshape(L, H, HD), cosine, sine))
    keys_rot = low(rotate(low_back(matmul(normed, key_w)).reshape(L, H, HD), cosine, sine))
    values = low(low_back(matmul(normed, value_w))).reshape(L, H, HD)
    block_rows = min(512, L)

    def attend(query_block):
        scores = jnp.einsum('qhd,khd->hqk', query_block, keys_rot, precision=lax.Precision.HIGHEST) * scale
        scores = low_back(jnp.where(valid[None, None, :], scores, masked_score))
        probs = low(jax.nn.softmax(scores, axis=-1))
        return jnp.einsum('hqk,khd->qhd', probs, values, precision=lax.Precision.HIGHEST)
    attended = lax.map(jax.checkpoint(attend), queries.reshape(L // block_rows, block_rows, H, HD))
    attended = low(low_back(attended.reshape(L, H * HD)))
    resid = inputs + low_back(matmul(attended, out_w))
    normed_two = low(layer_norm(resid, gain_two, shift_two))
    gate_pre = low_back(matmul(normed_two, gate_w))
    up_pre = low_back(matmul(normed_two, up_w))
    hidden = low(jax.nn.silu(gate_pre) * up_pre)
    return resid + low_back(matmul(hidden, down_w))

def reference(tokens, lengths, cotangent, query_weight, key_weight, value_weight, output_weight, gate_weight, up_weight, down_weight, attention_gain, attention_shift, feed_gain, feed_shift):
    params = tuple((item.astype(jnp.float32) for item in (query_weight, key_weight, value_weight, output_weight, gate_weight, up_weight, down_weight, attention_gain, attention_shift, feed_gain, feed_shift)))
    positions = jnp.arange(L, dtype=jnp.int32)

    def per_window(totals, item):
        window, length, upstream = item
        valid = positions < length
        result, pull = jax.vjp(lambda chosen, inputs: window_forward(chosen, inputs, valid), params, window.astype(jnp.float32))
        masked_upstream = upstream.astype(jnp.float32) * valid[:, None].astype(jnp.float32)
        grads, input_grad = pull(masked_upstream)
        totals = jax.tree.map(lambda left, right: left + right, totals, grads)
        return (totals, (result.astype(jnp.bfloat16), input_grad.astype(jnp.bfloat16)))
    zeros = jax.tree.map(jnp.zeros_like, params)
    totals, stacked = lax.scan(per_window, zeros, (tokens, lengths, cotangent))
    return (stacked[0], stacked[1], totals[0], totals[1], totals[2], totals[3], totals[4], totals[5], totals[6], totals[7], totals[8], totals[9], totals[10])
```

```python
import functools
import math

import numpy as np

import jax
import jax.numpy as jnp
from jax import lax
from jax.experimental import pallas as pl
from jax.experimental.pallas import tpu as pltpu
from jax.sharding import PartitionSpec as P

H = 16
HD = 64
L = 2048


epsilon = 1e-05
masked_score = -1e30


def layer_norm(values, gain, shift):
    centre = values - jnp.mean(values, axis=-1, keepdims=True)
    spread = jnp.mean(centre * centre, axis=-1, keepdims=True)
    return centre * lax.rsqrt(spread + epsilon) * gain + shift


def rotary_tables(positions):
    half = HD // 2
    freqs = jnp.exp(jnp.arange(half, dtype=jnp.float32) * (-2.0 * math.log(10000.0) / HD))
    angles = positions.astype(jnp.float32)[:, None] * freqs[None, :]
    cosine = jnp.concatenate([jnp.cos(angles), jnp.cos(angles)], axis=-1)
    sine = jnp.concatenate([jnp.sin(angles), jnp.sin(angles)], axis=-1)
    return (cosine, sine)


def rotate(values, cosine, sine):
    half = HD // 2
    turned = jnp.concatenate([-values[..., half:], values[..., :half]], axis=-1)
    return values * cosine[:, None, :] + turned * sine[:, None, :]


AXES = ("dp", "ctx")
BF = jnp.bfloat16


class Plan:
    def __init__(self, mesh):
        self.dp, self.ctx = mesh.shape["dp"], mesh.shape["ctx"]
        self.stages = self.dp.bit_length() - 2
        self.ctx_bits = self.ctx.bit_length() - 1
        orders = (list(range(1, self.stages + 1)), list(range(self.stages, 0, -1)))
        self.core = self.pairs(lambda d, z: (d ^ 1, z))
        self.stage = [
            self.pairs(lambda d, z, t=t: (d ^ (1 << orders[d & 1][t]), z)) for t in range(self.stages)
        ]
        self.along = [self.pairs(lambda d, z, b=b: (d, z ^ (1 << b))) for b in range(self.ctx_bits)]
        half = self.dp // 2
        table = np.zeros((self.dp, self.dp), np.int32)
        for d in range(self.dp):
            for j in range(self.dp):
                owner = d ^ 1 if j >= half else d
                block = owner
                for t in range(self.stages):
                    if (j % half) >> (self.stages - 1 - t) & 1:
                        block ^= 1 << orders[owner & 1][t]
                table[d, j] = block
        self.table = table

    def pairs(self, target):
        found = []
        for d in range(self.dp):
            for z in range(self.ctx):
                other, place = target(d, z)
                found.append((d * self.ctx + z, other * self.ctx + place))
        return found

    def slots(self):
        return jnp.asarray(self.table)[lax.axis_index("dp")]


def assemble(slots, pieces, rows):
    blocks = slots.shape[0]
    width = pieces[0].shape[1]
    sizes = [piece.shape[0] // rows for piece in pieces]
    starts = [sum(sizes[:i]) for i in range(len(sizes))]

    def body(order, *refs):
        slot = pl.program_id(0)
        out = refs[-1]
        for piece, start, size in zip(refs, starts, sizes):

            @pl.when((slot >= start) & (slot < start + size))
            def _(piece=piece):
                out[...] = piece[...]

    specs = [
        pl.BlockSpec(
            (rows, width),
            lambda j, order, start=start, size=size: (jnp.clip(j - start, 0, size - 1), 0),
        )
        for start, size in zip(starts, sizes)
    ]
    return pl.pallas_call(
        body,
        out_shape=jax.ShapeDtypeStruct((blocks * rows, width), pieces[0].dtype),
        grid_spec=pltpu.PrefetchScalarGridSpec(
            num_scalar_prefetch=1,
            grid=(blocks,),
            in_specs=specs,
            out_specs=pl.BlockSpec((rows, width), lambda j, order: (order[j], 0)),
        ),
        name="assemble",
    )(slots, *pieces)


def gather_rows(plan, slots, shard):
    place = lax.axis_index("ctx")
    run = shard
    for bit, pairs in enumerate(plan.along):
        other = lax.ppermute(run, AXES, pairs)
        upper = (place >> bit) & 1 == 1
        run = jnp.where(upper, jnp.concatenate([other, run]), jnp.concatenate([run, other]))
    rows = run.shape[0]
    pieces = [run]
    for pairs in reversed(plan.stage):
        other = lax.ppermute(run, AXES, pairs)
        pieces.append(other)
        run = jnp.concatenate([run, other])
    pieces.append(lax.ppermute(run, AXES, plan.core))
    return assemble(slots, pieces, rows)


def to_slots(slots, values):
    blocks = slots.shape[0]
    rows, width = values.shape
    part = width // blocks
    if part % 128:
        cut = values.reshape(rows, blocks, part)
        return jnp.take(cut, slots, axis=1).reshape(rows, width)

    def body(order, source, out):
        out[...] = source[...]

    return pl.pallas_call(
        body,
        out_shape=jax.ShapeDtypeStruct((rows, width), values.dtype),
        grid_spec=pltpu.PrefetchScalarGridSpec(
            num_scalar_prefetch=1,
            grid=(blocks,),
            in_specs=[pl.BlockSpec((rows, part), lambda j, order: (0, order[j]))],
            out_specs=pl.BlockSpec((rows, part), lambda j, order: (0, j)),
        ),
        name="to_slots",
    )(slots, values)


def sum_rows(plan, left, right):
    place = lax.axis_index("ctx")
    rows = left.shape[1] // plan.dp
    half = plan.dp // 2

    def product(start, end, add=None):
        part = lax.slice_in_dim(left, start * rows, end * rows, axis=1)
        found = jnp.dot(part.T, right, preferred_element_type=jnp.float32)
        if add is not None:
            found = found + add.astype(jnp.float32)
        return found.astype(BF)

    def total(a, b):
        return (a.astype(jnp.float32) + b.astype(jnp.float32)).astype(BF)

    other = lax.ppermute(product(half, plan.dp), AXES, plan.core)
    size = half // 2
    upper = product(size, half, other[size * rows :])
    other_upper = lax.ppermute(upper, AXES, plan.stage[0])
    held = total(product(0, size, other[: size * rows]), other_upper)
    for pairs in plan.stage[1:]:
        size //= 2
        other = lax.ppermute(held[size * rows :], AXES, pairs)
        held = total(held[: size * rows], other)
    for bit in reversed(range(plan.ctx_bits)):
        cut = held.shape[0] // 2
        above = (place >> bit) & 1 == 1
        low, high = held[:cut], held[cut:]
        other = lax.ppermute(jnp.where(above, low, high), AXES, plan.along[bit])
        held = jnp.where(above, high, low).astype(jnp.float32) + other.astype(jnp.float32)
        if bit:
            held = held.astype(BF)
    return held


def sum_vectors(plan, vectors):
    count = plan.dp * plan.ctx
    packed = jnp.stack(vectors).reshape(len(vectors), count, -1).transpose(1, 0, 2)
    part = packed.shape[2]
    packed = packed.reshape(count, len(vectors) * part)
    came = lax.all_to_all(packed, AXES, split_axis=0, concat_axis=0, tiled=True)
    whole = jnp.sum(came, axis=0)
    return [whole[i * part : (i + 1) * part] for i in range(len(vectors))]


def shards(
    plan,
    tokens,
    lengths,
    cotangent,
    query_weight,
    key_weight,
    value_weight,
    output_weight,
    gate_weight,
    up_weight,
    down_weight,
    attention_gain,
    attention_shift,
    feed_gain,
    feed_shift,
):
    slots = plan.slots()
    edge = jnp.stack([attention_gain, attention_shift, feed_gain, feed_shift], axis=1)
    edge = jnp.pad(edge, ((0, 0), (0, 124)))
    mixed = jnp.concatenate([query_weight, key_weight, value_weight, output_weight, edge], axis=1)
    mixed = gather_rows(plan, slots, mixed)
    vectors = mixed[:, 4096:4100].T
    weights = (
        mixed[:, :1024],
        mixed[:, 1024:2048],
        mixed[:, 2048:3072],
        mixed[:, 3072:4096],
        gather_rows(plan, slots, gate_weight),
        gather_rows(plan, slots, up_weight),
        gather_rows(plan, slots, down_weight),
        vectors[0],
        vectors[1],
        vectors[2],
        vectors[3],
    )
    windows, local_len, width = tokens.shape
    total_rows = windows * local_len
    scale = 1.0 / math.sqrt(HD)
    local_pos = lax.axis_index("ctx") * local_len + jnp.arange(local_len, dtype=jnp.int32)
    row_valid = (local_pos[None, :] < lengths[:, None]).astype(jnp.float32)
    cosine, sine = rotary_tables(local_pos)
    inputs = tokens.astype(jnp.float32).reshape(total_rows, width)
    gain_one = weights[7].astype(jnp.float32)
    shift_one = weights[8].astype(jnp.float32)
    gain_two = weights[9].astype(jnp.float32)
    shift_two = weights[10].astype(jnp.float32)
    normed_one = layer_norm(inputs, gain_one, shift_one)
    normed_low = normed_one.astype(jnp.bfloat16)
    query_raw = jnp.dot(normed_low, weights[0], preferred_element_type=jnp.float32)
    key_raw = jnp.dot(normed_low, weights[1], preferred_element_type=jnp.float32)
    value_flat = (
        jnp.dot(normed_low, weights[2], preferred_element_type=jnp.float32)
        .astype(jnp.bfloat16)
        .reshape(windows, local_len, width)
    )
    queries = rotate(query_raw.reshape(windows, local_len, H, HD), cosine, sine).astype(
        jnp.bfloat16
    )
    keys_flat = (
        rotate(key_raw.reshape(windows, local_len, H, HD), cosine, sine)
        .astype(jnp.bfloat16)
        .reshape(windows, local_len, width)
    )
    start_state = (
        jnp.full((windows, H, local_len), masked_score, jnp.float32),
        jnp.zeros((windows, H, local_len), jnp.float32),
        jnp.zeros((windows, local_len, H, HD), jnp.float32),
    )
    key_piece = lax.all_gather(keys_flat, "ctx", axis=1, tiled=True)
    value_piece = lax.all_gather(value_flat, "ctx", axis=1, tiled=True)
    piece_len = key_piece.shape[1]
    attend_block = math.gcd(piece_len, 256)

    def one_block(inner, index):
        maxima, totals, accum = inner
        offset = index * attend_block
        key_block = lax.dynamic_slice_in_dim(key_piece, offset, attend_block, 1).reshape(
            windows, attend_block, H, HD
        )
        value_block = lax.dynamic_slice_in_dim(value_piece, offset, attend_block, 1).reshape(
            windows, attend_block, H, HD
        )
        key_pos = offset + jnp.arange(attend_block, dtype=jnp.int32)
        allowed = (key_pos[None, :] < lengths[:, None])[:, None, None, :]
        scores = (
            jnp.einsum("wqhd,wkhd->whqk", queries, key_block, preferred_element_type=jnp.float32)
            * scale
        )
        scores = jnp.where(allowed, scores, masked_score)
        new_max = jnp.maximum(maxima, jnp.max(scores, axis=-1))
        expo = jnp.where(allowed, jnp.exp(scores - new_max[..., None]), 0.0)
        factor = jnp.exp(maxima - new_max)
        totals = totals * factor + jnp.sum(expo, axis=-1)
        update = jnp.einsum(
            "whqk,wkhd->wqhd",
            expo.astype(jnp.bfloat16),
            value_block,
            preferred_element_type=jnp.float32,
        )
        accum = accum * jnp.transpose(factor, (0, 2, 1))[..., None] + update
        return ((new_max, totals, accum), None)

    result, unused = lax.scan(one_block, start_state, jnp.arange(piece_len // attend_block))
    maxima, totals, accum = result
    log_total = maxima + jnp.log(totals)
    attended = accum / jnp.transpose(totals, (0, 2, 1))[..., None]
    attn_low = attended.reshape(total_rows, width).astype(jnp.bfloat16)
    resid = inputs + jnp.dot(attn_low, weights[3], preferred_element_type=jnp.float32)
    normed_two = layer_norm(resid, gain_two, shift_two)
    two_low = normed_two.astype(jnp.bfloat16)
    gate_pre = jnp.dot(two_low, weights[4], preferred_element_type=jnp.float32)
    up_pre = jnp.dot(two_low, weights[5], preferred_element_type=jnp.float32)
    sigma = jax.nn.sigmoid(gate_pre)
    activ = gate_pre * sigma
    hidden = (activ * up_pre).astype(jnp.bfloat16)
    result_rows = resid + jnp.dot(hidden, weights[6], preferred_element_type=jnp.float32)
    output = result_rows.astype(jnp.bfloat16).reshape(windows, local_len, width)
    back_weights = weights
    upstream = cotangent.astype(jnp.float32).reshape(total_rows, width) * row_valid.reshape(
        total_rows, 1
    )
    upstream_low = upstream.astype(jnp.bfloat16)
    grad_down = sum_rows(plan, to_slots(slots, hidden), upstream_low)
    grad_hidden = jnp.dot(upstream_low, back_weights[6].T, preferred_element_type=jnp.float32)
    grad_gate = (grad_hidden * up_pre * sigma * (1.0 + gate_pre * (1.0 - sigma))).astype(
        jnp.bfloat16
    )
    grad_up = (grad_hidden * activ).astype(jnp.bfloat16)
    two_slots = to_slots(slots, two_low)
    grad_gate_w = sum_rows(plan, two_slots, grad_gate)
    grad_up_w = sum_rows(plan, two_slots, grad_up)
    grad_normed_two = jnp.dot(
        grad_gate, back_weights[4].T, preferred_element_type=jnp.float32
    ) + jnp.dot(grad_up, back_weights[5].T, preferred_element_type=jnp.float32)
    unused_two, pull_two = jax.vjp(layer_norm, resid, gain_two, shift_two)
    grad_resid_norm, grad_gain_two, grad_shift_two = pull_two(grad_normed_two)
    grad_resid = upstream + grad_resid_norm
    branch_low = grad_resid.astype(jnp.bfloat16)
    grad_out_w = sum_rows(plan, to_slots(slots, attn_low), branch_low)
    grad_attn = (
        jnp.dot(branch_low, back_weights[3].T, preferred_element_type=jnp.float32)
        .astype(jnp.bfloat16)
        .reshape(windows, local_len, H, HD)
    )
    delta = jnp.transpose(jnp.sum(grad_attn.astype(jnp.float32) * attended, axis=-1), (0, 2, 1))
    key_all, value_all = (
        lax.all_gather(keys_flat, "ctx", axis=1, tiled=True),
        lax.all_gather(value_flat, "ctx", axis=1, tiled=True),
    )
    block = min(256, L)

    def back_block(carry, index):
        grad_query, kv_grads = carry
        offset = index * block
        key_block = lax.dynamic_slice_in_dim(key_all, offset, block, 1).reshape(
            windows, block, H, HD
        )
        value_block = lax.dynamic_slice_in_dim(value_all, offset, block, 1).reshape(
            windows, block, H, HD
        )
        key_pos = offset + jnp.arange(block, dtype=jnp.int32)
        allowed = (key_pos[None, :] < lengths[:, None])[:, None, None, :]
        scores = (
            jnp.einsum("wqhd,wkhd->whqk", queries, key_block, preferred_element_type=jnp.float32)
            * scale
        )
        probs = jnp.where(allowed, jnp.exp(scores - log_total[..., None]), 0.0)
        grad_probs = jnp.einsum(
            "wqhd,wkhd->whqk", grad_attn, value_block, preferred_element_type=jnp.float32
        )
        grad_scores = (probs * (grad_probs - delta[..., None])).astype(jnp.bfloat16)
        grad_query = (
            grad_query
            + jnp.einsum(
                "whqk,wkhd->wqhd", grad_scores, key_block, preferred_element_type=jnp.float32
            )
            * scale
        )
        grad_key_blk = (
            jnp.einsum("whqk,wqhd->wkhd", grad_scores, queries, preferred_element_type=jnp.float32)
            * scale
        )
        grad_value_blk = jnp.einsum(
            "whqk,wqhd->wkhd",
            probs.astype(jnp.bfloat16),
            grad_attn,
            preferred_element_type=jnp.float32,
        )
        joined = jnp.concatenate(
            [
                grad_key_blk.reshape(windows, block, width),
                grad_value_blk.reshape(windows, block, width),
            ],
            axis=-1,
        )
        kv_grads = lax.dynamic_update_slice_in_dim(kv_grads, joined, offset, 1)
        return ((grad_query, kv_grads), None)

    start_back = (
        jnp.zeros((windows, local_len, H, HD), jnp.float32),
        jnp.zeros((windows, L, 2 * width), jnp.float32),
    )
    back_state, unused = lax.scan(back_block, start_back, jnp.arange(L // block))
    grad_query, kv_grads = back_state
    kv_share = lax.psum_scatter(
        kv_grads.astype(jnp.bfloat16), "ctx", scatter_dimension=1, tiled=True
    ).astype(jnp.float32)
    grad_key = kv_share[..., :width].reshape(windows, local_len, H, HD)
    grad_value = kv_share[..., width:].reshape(total_rows, width).astype(jnp.bfloat16)
    grad_query_raw = (
        rotate(grad_query, cosine, -sine).reshape(total_rows, width).astype(jnp.bfloat16)
    )
    grad_key_raw = rotate(grad_key, cosine, -sine).reshape(total_rows, width).astype(jnp.bfloat16)
    raw = jnp.concatenate([grad_query_raw, grad_key_raw, grad_value], axis=1)
    grad_raw_w = sum_rows(plan, to_slots(slots, normed_low), raw)
    grad_query_w = grad_raw_w[:, :width]
    grad_key_w = grad_raw_w[:, width : 2 * width]
    grad_value_w = grad_raw_w[:, 2 * width :]
    grad_normed_one = jnp.dot(grad_query_raw, back_weights[0].T, preferred_element_type=jnp.float32)
    grad_normed_one = grad_normed_one + jnp.dot(
        grad_key_raw, back_weights[1].T, preferred_element_type=jnp.float32
    )
    grad_normed_one = grad_normed_one + jnp.dot(
        grad_value, back_weights[2].T, preferred_element_type=jnp.float32
    )
    unused_one, pull_one = jax.vjp(layer_norm, inputs, gain_one, shift_one)
    grad_inputs_norm, grad_gain_one, grad_shift_one = pull_one(grad_normed_one)
    tokens_grad = (
        (grad_resid + grad_inputs_norm).astype(jnp.bfloat16).reshape(windows, local_len, width)
    )
    vectors_grad = sum_vectors(
        plan, (grad_gain_one, grad_shift_one, grad_gain_two, grad_shift_two)
    )
    summed = (
        grad_query_w,
        grad_key_w,
        grad_value_w,
        grad_out_w,
        grad_gate_w,
        grad_up_w,
        grad_down,
        *vectors_grad,
    )
    return (
        output,
        tokens_grad,
        summed[0],
        summed[1],
        summed[2],
        summed[3],
        summed[4],
        summed[5],
        summed[6],
        summed[7],
        summed[8],
        summed[9],
        summed[10],
    )


def solution(mesh):
    return jax.shard_map(
        functools.partial(shards, Plan(mesh)),
        mesh=mesh,
        in_specs=(
            P("dp", "ctx", None),
            P("dp"),
            P("dp", "ctx", None),
            P(("dp", "ctx"), None),
            P(("dp", "ctx"), None),
            P(("dp", "ctx"), None),
            P(("dp", "ctx"), None),
            P(("dp", "ctx"), None),
            P(("dp", "ctx"), None),
            P(("dp", "ctx"), None),
            P(("dp", "ctx")),
            P(("dp", "ctx")),
            P(("dp", "ctx")),
            P(("dp", "ctx")),
        ),
        out_specs=(
            P("dp", "ctx", None),
            P("dp", "ctx", None),
            P(("dp", "ctx"), None),
            P(("dp", "ctx"), None),
            P(("dp", "ctx"), None),
            P(("dp", "ctx"), None),
            P(("dp", "ctx"), None),
            P(("dp", "ctx"), None),
            P(("dp", "ctx"), None),
            P(("dp", "ctx")),
            P(("dp", "ctx")),
            P(("dp", "ctx")),
            P(("dp", "ctx")),
        ),
        check_vma=False,
    )
```

```python
import functools
import math

import numpy as np

import jax
import jax.numpy as jnp
from jax import lax
from jax.experimental import pallas as pl
from jax.experimental.pallas import tpu as pltpu
from jax.sharding import PartitionSpec as P

H = 16
HD = 64
L = 2048


epsilon = 1e-05
masked_score = -1e30


def layer_norm(values, gain, shift):
    centre = values - jnp.mean(values, axis=-1, keepdims=True)
    spread = jnp.mean(centre * centre, axis=-1, keepdims=True)
    return centre * lax.rsqrt(spread + epsilon) * gain + shift


def rotary_tables(positions):
    half = HD // 2
    turns = jnp.arange(2 * HD, dtype=jnp.int32) % half
    freqs = jnp.exp(turns.astype(jnp.float32) * (-2.0 * math.log(10000.0) / HD))
    angles = positions.astype(jnp.float32)[:, None] * freqs[None, :]
    return (jnp.cos(angles), jnp.sin(angles))


AXES = ("dp", "ctx")
BF = jnp.bfloat16


class Plan:
    def __init__(self, mesh):
        self.dp, self.ctx = mesh.shape["dp"], mesh.shape["ctx"]
        self.stages = self.dp.bit_length() - 2
        self.ctx_bits = self.ctx.bit_length() - 1
        orders = (list(range(1, self.stages + 1)), list(range(self.stages, 0, -1)))
        self.core = self.pairs(lambda d, z: (d ^ 1, z))
        self.stage = [
            self.pairs(lambda d, z, t=t: (d ^ (1 << orders[d & 1][t]), z)) for t in range(self.stages)
        ]
        self.across = [self.pairs(lambda d, z, k=k: (d, z ^ k)) for k in range(self.ctx)]
        half = self.dp // 2
        table = np.zeros((self.dp, self.dp), np.int32)
        for d in range(self.dp):
            for j in range(self.dp):
                owner = d ^ 1 if j >= half else d
                block = owner
                for t in range(self.stages):
                    if (j % half) >> (self.stages - 1 - t) & 1:
                        block ^= 1 << orders[owner & 1][t]
                table[d, j] = block
        self.table = table

    def pairs(self, target):
        found = []
        for d in range(self.dp):
            for z in range(self.ctx):
                other, place = target(d, z)
                found.append((d * self.ctx + z, other * self.ctx + place))
        return found

    def slots(self):
        return jnp.asarray(self.table)[lax.axis_index("dp")]


def assemble(slots, pieces, rows):
    blocks = slots.shape[0]
    width = pieces[0].shape[1]
    sizes = [piece.shape[0] // rows for piece in pieces]
    starts = [sum(sizes[:i]) for i in range(len(sizes))]

    def body(order, *refs):
        slot = pl.program_id(0)
        out = refs[-1]
        for piece, start, size in zip(refs, starts, sizes):

            @pl.when((slot >= start) & (slot < start + size))
            def _(piece=piece):
                out[...] = piece[...]

    specs = [
        pl.BlockSpec(
            (rows, width),
            lambda j, order, start=start, size=size: (jnp.clip(j - start, 0, size - 1), 0),
        )
        for start, size in zip(starts, sizes)
    ]
    return pl.pallas_call(
        body,
        out_shape=jax.ShapeDtypeStruct((blocks * rows, width), pieces[0].dtype),
        grid_spec=pltpu.PrefetchScalarGridSpec(
            num_scalar_prefetch=1,
            grid=(blocks,),
            in_specs=specs,
            out_specs=pl.BlockSpec((rows, width), lambda j, order: (order[j], 0)),
        ),
        name="assemble",
    )(slots, *pieces)


def tie(values, others):
    leaves, tree = jax.tree.flatten((values, others))
    return jax.tree.unflatten(tree, lax.optimization_barrier(leaves))


class Chain:
    def __init__(self, steps):
        self.steps = steps
        self.flying, self.sent = next(steps)
        self.done = False
        self.value = None

    def land(self, came):
        if self.done:
            return
        try:
            self.flying, self.sent = self.steps.send(came)
        except StopIteration as stop:
            self.flying, self.sent, self.done, self.value = [], [], True, stop.value


def step(main, *chains):
    main, came = tie(main, [chain.flying for chain in chains])
    for chain, arrays in zip(chains, came):
        chain.land(arrays)
    return tie(main, [chain.sent for chain in chains])[0]


def begin(main, steps):
    chain = Chain(steps)
    return tie(main, chain.sent)[0], chain


def finish(main, *chains):
    while not all(chain.done for chain in chains):
        main = step(main, *chains)
    return main


def gather_steps(plan, shard):
    place = lax.axis_index("ctx")
    blocks = yield (
        [lax.ppermute(shard, AXES, plan.across[k]) for k in range(1, plan.ctx)],
        [shard],
    )
    blocks = [shard, *blocks]
    for bit in range(plan.ctx_bits):
        upper = (place >> bit) & 1 == 1
        blocks = [
            jnp.where(upper, jnp.concatenate([b, a]), jnp.concatenate([a, b]))
            for a, b in zip(blocks[::2], blocks[1::2])
        ]
    run = blocks[0]
    pieces = [run]
    for pairs in reversed(plan.stage):
        (other,) = yield [lax.ppermute(run, AXES, pairs)], [run]
        pieces.append(other)
        run = jnp.concatenate([run, other])
    (other,) = yield [lax.ppermute(run, AXES, plan.core)], [run]
    pieces.append(other)
    return run, pieces


def sum_steps(plan, product):
    place = lax.axis_index("ctx")
    half = plan.dp // 2

    def total(a, b):
        return (a.astype(jnp.float32) + b.astype(jnp.float32)).astype(BF)

    send = product(half, plan.dp)
    (other,) = yield [lax.ppermute(send, AXES, plan.core)], [send]
    rows = other.shape[0] // half
    size = half // 2
    send = product(size, half, other[size * rows :])
    flying = [lax.ppermute(send, AXES, plan.stage[0])]
    keep = product(0, size, other[: size * rows])
    (other,) = yield flying, [send, keep]
    held = total(keep, other)
    for pairs in plan.stage[1:]:
        size //= 2
        send = held[size * rows :]
        (other,) = yield [lax.ppermute(send, AXES, pairs)], [send]
        held = total(held[: size * rows], other)
    cut = held.shape[0] // plan.ctx
    parts = [lax.dynamic_slice_in_dim(held, (place ^ k) * cut, cut, 0) for k in range(plan.ctx)]
    others = yield (
        [lax.ppermute(parts[k], AXES, plan.across[k]) for k in range(1, plan.ctx)],
        parts[1:],
    )
    return sum((other.astype(jnp.float32) for other in others), parts[0].astype(jnp.float32))


def sum_vectors(plan, vectors):
    count = plan.dp * plan.ctx
    packed = jnp.stack(vectors).reshape(len(vectors), count, -1).transpose(1, 0, 2)
    part = packed.shape[2]
    packed = packed.reshape(count, len(vectors) * part)
    came = lax.all_to_all(packed, AXES, split_axis=0, concat_axis=0, tiled=True)
    whole = jnp.sum(came, axis=0)
    return [whole[i * part : (i + 1) * part] for i in range(len(vectors))]


def nt(a, b):
    return lax.dot_general(a, b, (((1,), (1,)), ((), ())), preferred_element_type=jnp.float32)


def turn(values, cosine, sine):
    lane = lax.broadcasted_iota(jnp.int32, values.shape, 1)
    ahead = pltpu.roll(values, 128 - HD // 2, 1)
    behind = pltpu.roll(values, HD // 2, 1)
    turned = jnp.where(lane % HD < HD // 2, -ahead, behind)
    return values * cosine + turned * sine


def head_parts(values):
    lane = lax.broadcasted_iota(jnp.int32, values.shape, 1)
    zero = jnp.zeros_like(values)
    return [jnp.where(lane < HD, values, zero), jnp.where(lane < HD, zero, values)]


def product_of(plan, groups):
    def product(start, end, add=None):
        columns = []
        low = 0
        for terms in groups:
            found = 0.0
            for flipped, right in terms:
                rows = flipped.shape[0] // plan.dp
                part = flipped[start * rows : end * rows]
                found = found + jnp.dot(part, right, preferred_element_type=jnp.float32)
            high = low + found.shape[1]
            if add is not None:
                found = found + add[:, low:high].astype(jnp.float32)
            columns.append(found.astype(BF))
            low = high
        return columns[0] if len(columns) == 1 else jnp.concatenate(columns, axis=1)

    return product


def whole(shape):
    return pl.BlockSpec(shape, lambda *at: (0,) * len(shape))


def call(body, order, grid, ins, outs, operands, name, flops, scratch=(), transcendentals=0):
    size = lambda a: math.prod(a.shape) * jnp.dtype(a.dtype).itemsize
    out_shape = [shape for spec, shape in outs]
    return pl.pallas_call(
        body,
        out_shape=out_shape,
        grid_spec=pltpu.PrefetchScalarGridSpec(
            num_scalar_prefetch=1,
            grid=grid,
            in_specs=ins,
            out_specs=[spec for spec, shape in outs],
            scratch_shapes=list(scratch),
        ),
        cost_estimate=pl.CostEstimate(
            flops=flops,
            bytes_accessed=sum(size(a) for a in [*operands, *out_shape]),
            transcendentals=transcendentals,
        ),
        name=name,
    )(order, *operands)


def array(shape, dtype=BF):
    return jax.ShapeDtypeStruct(shape, dtype)


def spread(order, source, target, rows):
    blocks = order.shape[0]
    part = source.shape[1] // blocks
    for j in range(blocks):
        at = pl.multiple_of(order[j] * part, 128)
        target[rows, j * part : (j + 1) * part] = source[rows, pl.ds(at, part)].astype(target.dtype)


def collect(order, source, target):
    blocks = order.shape[0]
    part = source.shape[1] // blocks
    for j in range(blocks):
        at = pl.multiple_of(order[j] * part, 128)
        target[:, pl.ds(at, part)] = source[:, j * part : (j + 1) * part].astype(target.dtype)


def by_pieces(left, pieces):
    found, low = 0.0, 0
    for piece in pieces:
        high = low + piece.shape[0]
        found = found + jnp.dot(left[:, low:high], piece[...], preferred_element_type=jnp.float32)
        low = high
    return found


def project(order, source, gain, shift, mixed, cosine, sine, block):
    rows, width = source.shape
    tile = 512
    tiles = width // tile
    skip = 0 if block == 0 else tiles
    count = len(mixed)
    scale = 1.0 / math.sqrt(HD)

    def body(order_ref, source_ref, gain_ref, shift_ref, cos_ref, sin_ref, *refs):
        weights = refs[:count]
        outs, normed = refs[count:-1], refs[-1]
        at = pl.program_id(0) + skip

        @pl.when(at == skip)
        def _():
            spread(order_ref, source_ref, normed, slice(None))
            chunk = math.gcd(rows, 128)

            def one(i, unused):
                here = pl.ds(pl.multiple_of(i * chunk, chunk), chunk)
                found = normed[here, :].astype(jnp.float32)
                normed[here, :] = layer_norm(found, gain_ref[...], shift_ref[...]).astype(BF)
                return unused

            lax.fori_loop(0, rows // chunk, one, 0)
            outs[0][...] = normed[...].T

        found = by_pieces(normed, weights)

        def turned(c):
            return turn(found[:, c : c + 128], cos_ref[...], sin_ref[...]).astype(BF)

        if block == 0:

            @pl.when(at < tiles)
            def _():
                for c in range(0, tile, 128):
                    outs[1][:, c : c + 128] = (turned(c).astype(jnp.float32) * scale).astype(BF)

        @pl.when(at >= tiles)
        def _():
            for c in range(0, tile, 256):
                outs[-1][:, c : c + 128] = turned(c)
                outs[-1][:, c + 128 : c + 256] = found[:, c + 128 : c + 256].astype(BF)

    table = pl.BlockSpec((rows, 128), lambda j, order: (block, 0))
    outs = [(whole((width, rows)), array((width, rows)))]
    if block == 0:
        outs.append(
            (
                pl.BlockSpec((rows, tile), lambda j, order: (0, jnp.minimum(j, tiles - 1))),
                array((rows, width)),
            )
        )
    outs.append(
        (
            pl.BlockSpec((rows, tile), lambda j, order: (0, jnp.maximum(j + skip - tiles, 0))),
            array((rows, 2 * width)),
        )
    )
    return call(
        body,
        order,
        (3 * tiles - skip,),
        [whole((rows, width)), whole((1, width)), whole((1, width)), table, table]
        + [
            pl.BlockSpec((piece.shape[0], tile), lambda j, order: (0, j + skip)) for piece in mixed
        ],
        outs,
        (source, gain[None, :], shift[None, :], cosine, sine, *mixed),
        f"project{block}",
        2 * rows * width * width * (2 if block else 3),
        scratch=[pltpu.VMEM((rows, width), BF)],
    )


def attend(order, valid, block, state, last, queries, both):
    rows, width = queries.shape
    pairs = width // 128
    first = state is None

    def body(order_ref, valid_ref, q_ref, kv_ref, *refs):
        outs = refs if first else refs[2:]
        parts = head_parts(q_ref[...])
        keys = kv_ref[:, :128]
        flipped = kv_ref[:, 128:].T
        tops, masses, sums = [], [], []
        for head in range(2):
            scores = nt(keys, parts[head])
            seat = lax.broadcasted_iota(jnp.int32, scores.shape, 0)
            scores = jnp.where(seat < valid_ref[block], scores, masked_score)
            top = jnp.max(scores, axis=0, keepdims=True)
            if not first:
                top = jnp.maximum(top, refs[0][0, head : head + 1, :])
            expo = jnp.exp(scores - top)
            mass = jnp.sum(expo, axis=0, keepdims=True)
            held = jnp.dot(
                flipped[head * HD : (head + 1) * HD, :],
                expo.astype(BF),
                preferred_element_type=jnp.float32,
            )
            if not first:
                factor = jnp.exp(refs[0][0, head : head + 1, :] - top)
                mass = mass + refs[0][0, head + 2 : head + 3, :] * factor
                held = held + refs[1][head * HD : (head + 1) * HD, :] * factor
            tops.append(top)
            masses.append(mass)
            sums.append(held)
        blank = jnp.zeros((4, rows), jnp.float32)
        if last:
            found = jnp.concatenate([s / m for s, m in zip(sums, masses)], axis=0)
            outs[1][...] = found.astype(BF)
            found = found.T
            outs[0][...] = found.astype(BF)
            outs[2][...] = found
            lse = [t + jnp.log(m) for t, m in zip(tops, masses)]
            outs[3][...] = jnp.concatenate(lse + masses + [blank], axis=0)[None]
        else:
            outs[0][...] = jnp.concatenate(tops + masses + [blank], axis=0)[None]
            outs[1][...] = jnp.concatenate(sums, axis=0)

    column = pl.BlockSpec((rows, 128), lambda j, order: (0, j))
    stats = pl.BlockSpec((1, 8, rows), lambda j, order: (j, 0, 0))
    carried = pl.BlockSpec((128, rows), lambda j, order: (j, 0))
    stats_shape = array((pairs, 8, rows), jnp.float32)
    if last:
        outs = [
            (column, array((rows, width))),
            (carried, array((width, rows))),
            (column, array((rows, width), jnp.float32)),
            (stats, stats_shape),
        ]
    else:
        outs = [(stats, stats_shape), (carried, array((width, rows), jnp.float32))]
    return call(
        body,
        order,
        (pairs,),
        [
            pl.BlockSpec(memory_space=pltpu.SMEM),
            pl.BlockSpec((rows, 128), lambda j, order: (0, order[j])),
            pl.BlockSpec((rows, 256), lambda j, order: (0, order[j])),
        ]
        + ([] if first else [stats, carried]),
        outs,
        (valid, queries, both, *(() if first else state)),
        f"attend{block}",
        16 * rows * rows * width,
        transcendentals=16 * rows * rows,
    )


def attend_back(order, valid, block, held, last, queries, both, go, attended, lse, cosine, sine):
    rows, width = queries.shape
    pairs = width // 128
    scale = 1.0 / math.sqrt(HD)
    first = held is None

    def body(order_ref, valid_ref, q_ref, kv_ref, go_ref, o_ref, lse_ref, cos_ref, sin_ref, *refs):
        dq_ref, dkv_ref = refs[-2:]
        keys = kv_ref[:, :128]
        values = kv_ref[:, 128:]
        go_all = go_ref[...]
        q_parts = head_parts(q_ref[...])
        go_parts = head_parts(go_all)
        crossed = (go_all.astype(jnp.float32) * o_ref[...]).T
        flipped = keys.T
        dk = jnp.zeros((rows, 128), jnp.float32)
        dv = jnp.zeros((rows, 128), jnp.float32)
        dq = []
        for head in range(2):
            delta = jnp.sum(crossed[head * HD : (head + 1) * HD, :], axis=0, keepdims=True)
            scores = nt(keys, q_parts[head])
            seat = lax.broadcasted_iota(jnp.int32, scores.shape, 0)
            scores = jnp.where(seat < valid_ref[block], scores, masked_score)
            probs = jnp.exp(scores - lse_ref[0, head : head + 1, :])
            grad_probs = nt(values, go_parts[head])
            grad_scores = (probs * (grad_probs - delta)).astype(BF)
            dv = dv + jnp.dot(probs.astype(BF), go_parts[head], preferred_element_type=jnp.float32)
            dk = dk + jnp.dot(grad_scores, q_parts[head], preferred_element_type=jnp.float32)
            dq.append(
                jnp.dot(
                    flipped[head * HD : (head + 1) * HD, :],
                    grad_scores,
                    preferred_element_type=jnp.float32,
                )
            )
        dkv_ref[:, :128] = turn(dk, cos_ref[...], -sin_ref[...]).astype(BF)
        dkv_ref[:, 128:] = dv.astype(BF)
        found = jnp.concatenate(dq, axis=0)
        if not first:
            found = found + refs[0][...]
        if last:
            dq_ref[...] = turn(found.T * scale, cos_ref[...], -sin_ref[...]).astype(BF)
        else:
            dq_ref[...] = found

    column = pl.BlockSpec((rows, 128), lambda j, order: (0, j))
    natural = pl.BlockSpec((rows, 128), lambda j, order: (0, order[j]))
    natural_both = pl.BlockSpec((rows, 256), lambda j, order: (0, order[j]))
    carried = pl.BlockSpec((128, rows), lambda j, order: (j, 0))
    table = pl.BlockSpec((rows, 128), lambda j, order: (block, 0))
    return call(
        body,
        order,
        (pairs,),
        [
            pl.BlockSpec(memory_space=pltpu.SMEM),
            natural,
            natural_both,
            column,
            column,
            pl.BlockSpec((1, 8, rows), lambda j, order: (j, 0, 0)),
            table,
            table,
        ]
        + ([] if first else [carried]),
        [
            (natural, array((rows, width))) if last else (carried, array((width, rows), jnp.float32)),
            (natural_both, array((rows, 2 * width))),
        ],
        (valid, queries, both, go, attended, lse, cosine, sine, *(() if first else (held,))),
        f"attend_back{block}",
        40 * rows * rows * width,
        transcendentals=16 * rows * rows,
    )


def middle(order, attended, mixed, tokens, gain, shift):
    rows, width = tokens.shape
    count = len(mixed)
    chunk = math.gcd(rows, 256)

    def body(order_ref, o_ref, x_ref, gain_ref, shift_ref, *refs):
        weights = refs[:count]
        resid_ref, two_ref, flipped_ref, held = refs[count:]
        found = x_ref[...].astype(jnp.float32) + by_pieces(o_ref, weights)
        resid_ref[...] = found
        spread(order_ref, resid_ref, held, slice(None))
        two = layer_norm(held[...], gain_ref[...], shift_ref[...]).astype(BF)
        two_ref[...] = two
        flipped_ref[...] = two.T

    line = pl.BlockSpec((chunk, width), lambda i, order: (i, 0))
    return call(
        body,
        order,
        (rows // chunk,),
        [line, line, whole((1, width)), whole((1, width))]
        + [pl.BlockSpec((piece.shape[0], width), lambda i, order: (0, 3)) for piece in mixed],
        [
            (line, array((rows, width), jnp.float32)),
            (line, array((rows, width))),
            (pl.BlockSpec((width, chunk), lambda i, order: (0, i)), array((width, rows))),
        ],
        (attended, tokens, gain[None, :], shift[None, :], *mixed),
        "middle",
        2 * rows * width * width,
        scratch=[pltpu.VMEM((chunk, width), jnp.float32)],
    )


def feed(order, two, pair):
    rows, width = two.shape
    blocks = order.shape[0]
    hidden = pair[0].shape[1] // 2
    part = hidden // blocks
    count = len(pair)

    def body(order_ref, two_ref, *refs):
        gate_ref, up_ref, hidden_ref, flipped_ref = refs[count:]
        found = by_pieces(two_ref, refs[:count])
        gate, up = found[:, :part], found[:, part:]
        made = (gate / (1.0 + jnp.exp(-gate)) * up).astype(BF)
        gate_ref[...] = gate.astype(BF)
        up_ref[...] = up.astype(BF)
        hidden_ref[...] = made
        flipped_ref[...] = made.T

    tile = pl.BlockSpec((rows, part), lambda j, order: (0, j))
    shape = array((rows, hidden))
    return call(
        body,
        order,
        (blocks,),
        [whole((rows, width))]
        + [
            pl.BlockSpec((piece.shape[0], 2 * part), lambda j, order: (0, order[j]))
            for piece in pair
        ],
        [
            (tile, shape),
            (tile, shape),
            (tile, shape),
            (pl.BlockSpec((part, rows), lambda j, order: (j, 0)), array((hidden, rows))),
        ],
        (two, *pair),
        "feed",
        4 * rows * width * hidden,
        transcendentals=rows * hidden,
    )


def feed_back(order, upstream, gate, up, made, resid, pair, down):
    rows, width = upstream.shape
    blocks = order.shape[0]
    hidden = gate.shape[1]
    part = hidden // blocks
    count, downs = len(pair), len(down)
    each = blocks // downs

    def body(order_ref, m_ref, gate_ref, up_ref, made_ref, resid_ref, *refs):
        pairs, lows = refs[:count], refs[count : count + downs]
        out_ref, grads_ref, two_ref, total, result = refs[count + downs :]
        at = pl.program_id(0)

        @pl.when(at == 0)
        def _():
            total[...] = jnp.zeros_like(total)
            result[...] = resid_ref[...]

        def one(low):
            gate_all = gate_ref[...].astype(jnp.float32)
            up_all = up_ref[...].astype(jnp.float32)
            sigma = 1.0 / (1.0 + jnp.exp(-gate_all))
            made_grad = nt(m_ref[...], low[...])
            result[...] += jnp.dot(made_ref[...], low[...], preferred_element_type=jnp.float32)
            gate_grad = made_grad * up_all * sigma * (1.0 + gate_all * (1.0 - sigma))
            grads_ref[:, :part] = gate_grad.astype(BF)
            grads_ref[:, part:] = (made_grad * gate_all * sigma).astype(BF)

        for i in range(downs):

            @pl.when((at >= i * each) & (at < (i + 1) * each))
            def _(i=i):
                one(lows[i])

        grads = grads_ref[...]
        low = 0
        for piece in pairs:
            high = low + piece.shape[0]
            total[:, low:high] += nt(grads, piece[...])
            low = high

        @pl.when(at == blocks - 1)
        def _():
            out_ref[...] = result[...].astype(BF)
            collect(order_ref, total, two_ref)

    tile = pl.BlockSpec((rows, part), lambda j, order: (0, j))
    return call(
        body,
        order,
        (blocks,),
        [whole((rows, width)), tile, tile, tile, whole((rows, width))]
        + [
            pl.BlockSpec((piece.shape[0], 2 * part), lambda j, order: (0, order[j]))
            for piece in pair
        ]
        + [
            pl.BlockSpec(
                (part, width), lambda j, order, i=i: (jnp.clip(j - i * each, 0, each - 1), 0)
            )
            for i in range(downs)
        ],
        [
            (whole((rows, width)), array((rows, width))),
            (
                pl.BlockSpec((rows, 2 * part), lambda j, order: (0, order[j])),
                array((rows, 2 * hidden)),
            ),
            (whole((rows, width)), array((rows, width), jnp.float32)),
        ],
        (upstream, gate, up, made, resid, *pair, *down),
        "feed_back",
        8 * rows * width * hidden,
        scratch=[pltpu.VMEM((rows, width), jnp.float32), pltpu.VMEM((rows, width), jnp.float32)],
        transcendentals=rows * hidden,
    )


def norm_back(values, grads, gain):
    centre = values - jnp.mean(values, axis=-1, keepdims=True)
    scale = lax.rsqrt(jnp.mean(centre * centre, axis=-1, keepdims=True) + epsilon)
    normed = centre * scale
    scaled = grads * gain
    inner = jnp.mean(scaled * normed, axis=-1, keepdims=True)
    found = (scaled - jnp.mean(scaled, axis=-1, keepdims=True) - normed * inner) * scale
    return (
        found,
        jnp.sum(grads * normed, axis=0, keepdims=True),
        jnp.sum(grads, axis=0, keepdims=True),
    )


def middle_back(order, grads, resid, upstream, mixed, gain):
    rows, width = resid.shape
    count = len(mixed)
    chunk = math.gcd(rows, 256)

    def body(order_ref, grads_ref, resid_ref, m_ref, gain_ref, *refs):
        weights = refs[:count]
        y_ref, a_ref, go_ref, edge_ref = refs[count:]

        @pl.when(pl.program_id(0) == 0)
        def _():
            edge_ref[...] = jnp.zeros_like(edge_ref)

        found, gain_grad, shift_grad = norm_back(resid_ref[...], grads_ref[...], gain_ref[...])
        found = m_ref[...].astype(jnp.float32) + found
        edge_ref[0:1, :] += gain_grad
        edge_ref[1:2, :] += shift_grad
        y_ref[...] = found
        a_ref[...] = found.astype(BF)
        low = 0
        for weight in weights:
            high = low + weight.shape[0]
            go_ref[:, low:high] = nt(a_ref[...], weight[...]).astype(BF)
            low = high

    line = pl.BlockSpec((chunk, width), lambda i, order: (i, 0))
    return call(
        body,
        order,
        (rows // chunk,),
        [line, line, line, whole((1, width))]
        + [pl.BlockSpec((piece.shape[0], width), lambda i, order: (0, 3)) for piece in mixed],
        [
            (line, array((rows, width), jnp.float32)),
            (line, array((rows, width))),
            (line, array((rows, width))),
            (whole((8, width)), array((8, width), jnp.float32)),
        ],
        (grads, resid, upstream, gain[None, :], *mixed),
        "middle_back",
        2 * rows * width * width,
    )


def pull(order, dq, both, mixed, block):
    rows, width = both.shape[0], both.shape[1] // 2
    tile = 512
    tiles = width // tile
    count = len(mixed)
    skip = 0 if block == 0 else tiles
    steps = 3 * tiles - skip
    dtype = BF if block else jnp.float32

    def body(order_ref, *refs):
        lefts = refs[: 1 if block else 2]
        weights = refs[len(lefts) : len(lefts) + count]
        out_ref, total = refs[len(lefts) + count :]
        at = pl.program_id(0)

        @pl.when(at == 0)
        def _():
            total[...] = jnp.zeros_like(total)

        def one(left):
            low = 0
            for weight in weights:
                high = low + weight.shape[0]
                total[:, low:high] += nt(left[...], weight[...])
                low = high

        if block:
            one(lefts[0])
        else:

            @pl.when(at < tiles)
            def _():
                one(lefts[0])

            @pl.when(at >= tiles)
            def _():
                one(lefts[1])

        @pl.when(at == steps - 1)
        def _():
            out_ref[...] = total[...].astype(dtype)

    lefts = [] if block else [pl.BlockSpec((rows, tile), lambda j, order: (0, jnp.minimum(j, tiles - 1)))]
    lefts.append(pl.BlockSpec((rows, tile), lambda j, order: (0, jnp.maximum(j + skip - tiles, 0))))
    return call(
        body,
        order,
        (steps,),
        lefts
        + [
            pl.BlockSpec((piece.shape[0], tile), lambda j, order: (0, j + skip)) for piece in mixed
        ],
        [(whole((rows, width)), array((rows, width), dtype))],
        ((both,) if block else (dq, both)) + tuple(mixed),
        f"pull{block}",
        2 * rows * width * width * (2 if block else 3),
        scratch=[pltpu.VMEM((rows, width), jnp.float32)],
    )[0]


def end_back(order, parts, tokens, grads, gain):
    rows, width = tokens.shape
    count = len(parts)
    chunk = math.gcd(rows, 256)

    def body(order_ref, x_ref, y_ref, gain_ref, *refs):
        sources = refs[:count]
        out_ref, edge_ref, held, total = refs[count:]

        @pl.when(pl.program_id(0) == 0)
        def _():
            edge_ref[...] = jnp.zeros_like(edge_ref)

        held[...] = sum(source[...].astype(jnp.float32) for source in sources)
        collect(order_ref, held, total)
        found, gain_grad, shift_grad = norm_back(
            x_ref[...].astype(jnp.float32), total[...], gain_ref[...]
        )
        edge_ref[0:1, :] += gain_grad
        edge_ref[1:2, :] += shift_grad
        out_ref[...] = (y_ref[...] + found).astype(BF)

    line = pl.BlockSpec((chunk, width), lambda i, order: (i, 0))
    return call(
        body,
        order,
        (rows // chunk,),
        [line, line, whole((1, width))] + [line] * count,
        [(line, array((rows, width))), (whole((8, width)), array((8, width), jnp.float32))],
        (tokens, grads, gain[None, :], *parts),
        "end_back",
        0,
        scratch=[pltpu.VMEM((chunk, width), jnp.float32), pltpu.VMEM((chunk, width), jnp.float32)],
    )


def join(first, second, part):
    rows, width = first.shape
    stacked = jnp.stack([first.reshape(rows, -1, part), second.reshape(rows, -1, part)], axis=2)
    return stacked.reshape(rows, 2 * width)


def part_ways(both, part):
    rows, width = both.shape
    cut = both.reshape(rows, -1, 2, part)
    return cut[:, :, 0].reshape(rows, width // 2), cut[:, :, 1].reshape(rows, width // 2)


def shards(
    plan,
    tokens,
    lengths,
    cotangent,
    query_weight,
    key_weight,
    value_weight,
    output_weight,
    gate_weight,
    up_weight,
    down_weight,
    attention_gain,
    attention_shift,
    feed_gain,
    feed_shift,
):
    slots = plan.slots()
    windows, local_len, width = tokens.shape
    rows = windows * local_len
    hidden = gate_weight.shape[1]
    place = lax.axis_index("ctx")
    exact = (width // plan.dp) % 128 == 0
    order = slots if exact else jnp.arange(8, dtype=jnp.int32)
    part = hidden // order.shape[0]

    def pieces_of(chain, shard):
        run, pieces = chain.value
        if exact:
            return [run, pieces[-1]]
        return [assemble(slots, pieces, shard.shape[0] * plan.ctx)]

    def in_slots(flipped):
        if exact:
            return flipped
        cut = flipped.reshape(plan.dp, -1, flipped.shape[1])
        return jnp.take(cut, slots, axis=0).reshape(flipped.shape)

    edge = jnp.stack([attention_gain, attention_shift, feed_gain, feed_shift], axis=1)
    edge = jnp.pad(edge, ((0, 0), (0, 124)))
    both = join(key_weight, value_weight, 128)
    mixed = jnp.concatenate([query_weight, both, output_weight, edge], axis=1)
    mix = Chain(gather_steps(plan, mixed))

    seats = jnp.arange(local_len, dtype=jnp.int32)
    starts = (place ^ jnp.arange(plan.ctx, dtype=jnp.int32)) * local_len
    valid = jnp.clip(lengths[0] - starts, 0, local_len)
    cosine, sine = rotary_tables((starts[:, None] + seats[None, :]).reshape(-1))
    real = (place * local_len + seats < lengths[0])[:, None]
    upstream = jnp.where(real, cotangent.reshape(rows, width), 0)
    own = tokens.reshape(rows, width)

    pair_own = join(gate_weight, up_weight, part)
    pair_own = step(pair_own, mix)
    pair = Chain(gather_steps(plan, pair_own))
    own = step(own, mix)
    own = step(own, mix)
    own = step(own, pair)
    came = {k: lax.ppermute(own, AXES, plan.across[k]) for k in range(1, plan.ctx)}
    own = finish(own, mix)
    mixed_w = pieces_of(mix, mixed)
    cols = jnp.concatenate([piece[:, 4 * width : 4 * width + 4] for piece in mixed_w])
    cols = cols.T.astype(jnp.float32)
    back = jnp.argsort(order)
    natural = cols.reshape(4, order.shape[0], -1)[:, back].reshape(4, width)

    flipped, both = {}, {}
    flipped[0], queries, both[0] = project(order, own, cols[0], cols[1], mixed_w, cosine, sine, 0)
    state = attend(order, valid, 0, None, plan.ctx == 1, queries, both[0])
    down = None
    for k in range(1, plan.ctx):
        state, came[k] = tie(state, came[k])
        if k == 1:
            state = step(state, pair)
        if k == 2:
            down_own, state = tie(down_weight, state)
            down = Chain(gather_steps(plan, down_own))
        if k == 3:
            state = step(state, pair, down)
        flipped[k], both[k] = project(
            order, came[k], cols[0], cols[1], mixed_w, cosine, sine, k
        )
        state = attend(order, valid, k, state, k == plan.ctx - 1, queries, both[k])
    state = step(state, down)
    low, low_flipped, attended, lse = state
    resid, two, two_flipped = middle(order, low, mixed_w, own, cols[2], cols[3])
    two = finish(two, pair)
    two = step(two, down)
    pair_w = pieces_of(pair, pair_own)
    gate, up, made, made_flipped = feed(order, two, pair_w)
    made, down_sum = begin(
        made, sum_steps(plan, product_of(plan, [[(in_slots(made_flipped), upstream)]]))
    )
    made = finish(made, down)
    down_w = pieces_of(down, down_weight)
    output, pair_grads, two_grads = feed_back(
        order, upstream, gate, up, made, resid, pair_w, down_w
    )
    output = output.reshape(windows, local_len, width)

    two_grads = step(two_grads, down_sum)
    two_grads, pair_sum = begin(
        two_grads, sum_steps(plan, product_of(plan, [[(in_slots(two_flipped), pair_grads)]]))
    )
    y_grads, low_grads, go, edge_two = middle_back(
        order, two_grads, resid, upstream, mixed_w, natural[2]
    )
    go = step(go, pair_sum)
    go, output_sum = begin(
        go, sum_steps(plan, product_of(plan, [[(in_slots(low_flipped), low_grads)]]))
    )
    held = None
    grads, sends = {}, []
    for k in reversed(range(plan.ctx)):
        held, grads[k] = attend_back(
            order, valid, k, held, k == 0, queries, both[k], go, attended, lse, cosine, sine
        )
        if k == plan.ctx - 1:
            held = step(held, down_sum, output_sum)
        elif k == plan.ctx - 2:
            held = step(held, down_sum, output_sum, pair_sum)
        elif k:
            held = step(held, down_sum, output_sum, pair_sum)
        else:
            held = step(held, output_sum, pair_sum)
        part_grads = pull(order, held, grads[k], mixed_w, k)
        if k:
            held, part_grads = tie(held, part_grads)
            sends.append(lax.ppermute(part_grads, AXES, plan.across[k]))
    flipped = {k: in_slots(flipped[k]) for k in flipped}
    last = product_of(
        plan, [[(flipped[0], held)], [(flipped[k], grads[k]) for k in range(plan.ctx)]]
    )
    part_grads, last_sum = begin(part_grads, sum_steps(plan, last))
    part_grads = finish(part_grads, down_sum, output_sum, pair_sum)
    part_grads = step(part_grads, last_sum)
    tokens_grad, edge_one = end_back(
        order, [part_grads, *sends], own, y_grads, natural[0]
    )
    vectors = sum_vectors(plan, (edge_one[0], edge_one[1], edge_two[0], edge_two[1]))
    finish((), last_sum)
    gate_grad, up_grad = part_ways(pair_sum.value, part)
    key_grad, value_grad = part_ways(last_sum.value[:, width:], 128)
    return (
        output,
        tokens_grad.reshape(windows, local_len, width),
        last_sum.value[:, :width],
        key_grad,
        value_grad,
        output_sum.value,
        gate_grad,
        up_grad,
        down_sum.value,
        *vectors,
    )


def solution(mesh):
    return jax.shard_map(
        functools.partial(shards, Plan(mesh)),
        mesh=mesh,
        in_specs=(
            P("dp", "ctx", None),
            P("dp"),
            P("dp", "ctx", None),
            P(("dp", "ctx"), None),
            P(("dp", "ctx"), None),
            P(("dp", "ctx"), None),
            P(("dp", "ctx"), None),
            P(("dp", "ctx"), None),
            P(("dp", "ctx"), None),
            P(("dp", "ctx"), None),
            P(("dp", "ctx")),
            P(("dp", "ctx")),
            P(("dp", "ctx")),
            P(("dp", "ctx")),
        ),
        out_specs=(
            P("dp", "ctx", None),
            P("dp", "ctx", None),
            P(("dp", "ctx"), None),
            P(("dp", "ctx"), None),
            P(("dp", "ctx"), None),
            P(("dp", "ctx"), None),
            P(("dp", "ctx"), None),
            P(("dp", "ctx"), None),
            P(("dp", "ctx"), None),
            P(("dp", "ctx")),
            P(("dp", "ctx")),
            P(("dp", "ctx")),
            P(("dp", "ctx")),
        ),
        check_vma=False,
    )
```

```python
import functools
import math

import numpy as np

import jax
import jax.numpy as jnp
from jax import lax
from jax.experimental import pallas as pl
from jax.experimental.pallas import tpu as pltpu
from jax.sharding import PartitionSpec as P

H = 16
HD = 64
L = 2048


epsilon = 1e-05
masked_score = -1e30


def layer_norm(values, gain, shift):
    centre = values - jnp.mean(values, axis=-1, keepdims=True)
    spread = jnp.mean(centre * centre, axis=-1, keepdims=True)
    return centre * lax.rsqrt(spread + epsilon) * gain + shift


def rotary_tables(positions):
    half = HD // 2
    turns = jnp.arange(2 * HD, dtype=jnp.int32) % half
    freqs = jnp.exp(turns.astype(jnp.float32) * (-2.0 * math.log(10000.0) / HD))
    angles = positions.astype(jnp.float32)[:, None] * freqs[None, :]
    return (jnp.cos(angles), jnp.sin(angles))


AXES = ("dp", "ctx")
BF = jnp.bfloat16


class Plan:
    def __init__(self, mesh):
        self.dp, self.ctx = mesh.shape["dp"], mesh.shape["ctx"]
        self.stages = self.dp.bit_length() - 2
        self.ctx_bits = self.ctx.bit_length() - 1
        orders = (list(range(1, self.stages + 1)), list(range(self.stages, 0, -1)))
        self.core = self.pairs(lambda d, z: (d ^ 1, z))
        self.stage = [
            self.pairs(lambda d, z, t=t: (d ^ (1 << orders[d & 1][t]), z)) for t in range(self.stages)
        ]
        self.across = [self.pairs(lambda d, z, k=k: (d, z ^ k)) for k in range(self.ctx)]
        self.line = self.ctx == 4
        self.inner = self.pairs(lambda d, z: (d, z ^ 3), (1, 2))
        self.outward = self.pairs(lambda d, z: (d, z ^ 1), (1, 2))
        self.inward = self.pairs(lambda d, z: (d, z ^ 1), (0, 3))
        self.blocks = np.arange(self.ctx)[:, None] ^ np.arange(self.ctx)[None, :]
        if self.line:
            self.blocks = np.array([[0, 1, 2, 3], [1, 0, 2, 3], [2, 3, 1, 0], [3, 2, 1, 0]])
        self.blocks = self.blocks.astype(np.int32)
        half = self.dp // 2
        table = np.zeros((self.dp, self.dp), np.int32)
        for d in range(self.dp):
            for j in range(self.dp):
                owner = d ^ 1 if j >= half else d
                block = owner
                for t in range(self.stages):
                    if (j % half) >> (self.stages - 1 - t) & 1:
                        block ^= 1 << orders[owner & 1][t]
                table[d, j] = block
        self.table = table
        self.back = np.argsort(table, axis=1).astype(np.int32)

    def pairs(self, target, places=None):
        found = []
        for d in range(self.dp):
            for z in range(self.ctx) if places is None else places:
                other, place = target(d, z)
                found.append((d * self.ctx + z, other * self.ctx + place))
        return found

    def slots(self):
        return jnp.asarray(self.table)[lax.axis_index("dp")]


def assemble(slots, pieces, rows):
    blocks = slots.shape[0]
    width = pieces[0].shape[1]
    sizes = [piece.shape[0] // rows for piece in pieces]
    starts = [sum(sizes[:i]) for i in range(len(sizes))]

    def body(order, *refs):
        slot = pl.program_id(0)
        out = refs[-1]
        for piece, start, size in zip(refs, starts, sizes):

            @pl.when((slot >= start) & (slot < start + size))
            def _(piece=piece):
                out[...] = piece[...]

    specs = [
        pl.BlockSpec(
            (rows, width),
            lambda j, order, start=start, size=size: (jnp.clip(j - start, 0, size - 1), 0),
        )
        for start, size in zip(starts, sizes)
    ]
    return pl.pallas_call(
        body,
        out_shape=jax.ShapeDtypeStruct((blocks * rows, width), pieces[0].dtype),
        grid_spec=pltpu.PrefetchScalarGridSpec(
            num_scalar_prefetch=1,
            grid=(blocks,),
            in_specs=specs,
            out_specs=pl.BlockSpec((rows, width), lambda j, order: (order[j], 0)),
        ),
        name="assemble",
    )(slots, *pieces)


def tie(values, others):
    leaves, tree = jax.tree.flatten((values, others))
    return jax.tree.unflatten(tree, lax.optimization_barrier(leaves))


class Chain:
    def __init__(self, steps):
        self.steps = steps
        self.flying, self.sent = next(steps)
        self.done = False
        self.value = None

    def land(self, came):
        if self.done:
            return
        try:
            self.flying, self.sent = self.steps.send(came)
        except StopIteration as stop:
            self.flying, self.sent, self.done, self.value = [], [], True, stop.value


def step(main, *chains):
    main, came = tie(main, [chain.flying for chain in chains])
    for chain, arrays in zip(chains, came):
        chain.land(arrays)
    return tie(main, [chain.sent for chain in chains])[0]


def begin(main, steps):
    chain = Chain(steps)
    return tie(main, chain.sent)[0], chain


def finish(main, *chains):
    while not all(chain.done for chain in chains):
        main = step(main, *chains)
    return main


def gather_steps(plan, shard):
    place = lax.axis_index("ctx")
    blocks = yield (
        [lax.ppermute(shard, AXES, plan.across[k]) for k in range(1, plan.ctx)],
        [shard],
    )
    blocks = [shard, *blocks]
    for bit in range(plan.ctx_bits):
        upper = (place >> bit) & 1 == 1
        blocks = [
            jnp.where(upper, jnp.concatenate([b, a]), jnp.concatenate([a, b]))
            for a, b in zip(blocks[::2], blocks[1::2])
        ]
    run = blocks[0]
    pieces = [run]
    for pairs in reversed(plan.stage):
        (other,) = yield [lax.ppermute(run, AXES, pairs)], [run]
        pieces.append(other)
        run = jnp.concatenate([run, other])
    (other,) = yield [lax.ppermute(run, AXES, plan.core)], [run]
    pieces.append(other)
    return run, pieces


def add(a, b):
    return (a.astype(jnp.float32) + b.astype(jnp.float32)).astype(BF)


def window_steps(plan, own, came):
    if not plan.line:
        others = yield [lax.ppermute(own, AXES, plan.across[k]) for k in range(1, plan.ctx)], [own]
        came.update(enumerate(others, 1))
        return
    near, middle = yield (
        [lax.ppermute(own, AXES, plan.across[1]), lax.ppermute(own, AXES, plan.inner)],
        [own],
    )
    came[1] = near
    far, cross = yield (
        [lax.ppermute(middle, AXES, plan.outward), lax.ppermute(near, AXES, plan.inner)],
        [middle, near],
    )
    came[2] = middle + far
    (last,) = yield [lax.ppermute(cross, AXES, plan.outward)], [cross]
    came[3] = cross + last


def return_steps(plan, parts):
    (came,) = yield [lax.ppermute(parts[3], AXES, plan.inward)], [parts[3]]
    run = add(parts[3], came)
    near, cross = yield (
        [lax.ppermute(parts[2], AXES, plan.inward), lax.ppermute(run, AXES, plan.inner)],
        [parts[2], run],
    )
    run, last = add(parts[2], near), add(parts[1], cross)
    return (
        yield (
            [
                lax.ppermute(run, AXES, plan.inner),
                lax.ppermute(last, AXES, plan.across[1]),
            ],
            [run, last],
        )
    )


def sum_steps(plan, product):
    place = lax.axis_index("ctx")
    half = plan.dp // 2

    send = product(half, plan.dp)
    (other,) = yield [lax.ppermute(send, AXES, plan.core)], [send]
    rows = other.shape[0] // half
    size = half // 2
    send = product(size, half, other[size * rows :])
    flying = [lax.ppermute(send, AXES, plan.stage[0])]
    keep = product(0, size, other[: size * rows])
    (other,) = yield flying, [send, keep]
    held = add(keep, other)
    for pairs in plan.stage[1:]:
        size //= 2
        send = held[size * rows :]
        (other,) = yield [lax.ppermute(send, AXES, pairs)], [send]
        held = add(held[: size * rows], other)
    for bit in reversed(range(plan.ctx_bits)):
        cut = held.shape[0] // 2
        upper = (place >> bit) & 1
        send = lax.dynamic_slice_in_dim(held, (1 - upper) * cut, cut, 0)
        keep = lax.dynamic_slice_in_dim(held, upper * cut, cut, 0)
        (other,) = yield [lax.ppermute(send, AXES, plan.across[1 << bit])], [send]
        held = add(keep, other) if bit else keep.astype(jnp.float32) + other.astype(jnp.float32)
    return held


def sum_vectors(plan, vectors):
    count = plan.dp * plan.ctx
    packed = jnp.stack(vectors).reshape(len(vectors), count, -1).transpose(1, 0, 2)
    part = packed.shape[2]
    packed = packed.reshape(count, len(vectors) * part)
    came = lax.all_to_all(packed, AXES, split_axis=0, concat_axis=0, tiled=True)
    whole = jnp.sum(came, axis=0)
    return [whole[i * part : (i + 1) * part] for i in range(len(vectors))]


def nt(a, b):
    return lax.dot_general(a, b, (((1,), (1,)), ((), ())), preferred_element_type=jnp.float32)


def turn(values, cosine, sine):
    lane = lax.broadcasted_iota(jnp.int32, values.shape, 1)
    ahead = pltpu.roll(values, 128 - HD // 2, 1)
    behind = pltpu.roll(values, HD // 2, 1)
    turned = jnp.where(lane % HD < HD // 2, -ahead, behind)
    return values * cosine + turned * sine


def head_parts(values):
    lane = lax.broadcasted_iota(jnp.int32, values.shape, 1)
    zero = jnp.zeros_like(values)
    return [jnp.where(lane < HD, values, zero), jnp.where(lane < HD, zero, values)]


def product_of(plan, groups):
    def product(start, end, more=None):
        columns = []
        low = 0
        for terms in groups:
            found = 0.0
            for flipped, right in terms:
                rows = flipped.shape[0] // plan.dp
                part = flipped[start * rows : end * rows]
                found = found + jnp.dot(part, right, preferred_element_type=jnp.float32)
            high = low + found.shape[1]
            if more is not None:
                found = found + more[:, low:high].astype(jnp.float32)
            columns.append(found.astype(BF))
            low = high
        return columns[0] if len(columns) == 1 else jnp.concatenate(columns, axis=1)

    return product


def whole(shape):
    return pl.BlockSpec(shape, lambda *at: (0,) * len(shape))


def call(body, order, grid, ins, outs, operands, name, flops, scratch=(), transcendentals=0):
    size = lambda a: math.prod(a.shape) * jnp.dtype(a.dtype).itemsize
    out_shape = [shape for spec, shape in outs]
    return pl.pallas_call(
        body,
        out_shape=out_shape,
        grid_spec=pltpu.PrefetchScalarGridSpec(
            num_scalar_prefetch=1,
            grid=grid,
            in_specs=ins,
            out_specs=[spec for spec, shape in outs],
            scratch_shapes=list(scratch),
        ),
        cost_estimate=pl.CostEstimate(
            flops=flops,
            bytes_accessed=sum(size(a) for a in [*operands, *out_shape]),
            transcendentals=transcendentals,
        ),
        name=name,
    )(order, *operands)


def array(shape, dtype=BF):
    return jax.ShapeDtypeStruct(shape, dtype)


def spread(order, source, target, rows):
    blocks = order.shape[0]
    part = source.shape[1] // blocks
    for j in range(blocks):
        at = pl.multiple_of(order[j] * part, 128)
        target[rows, j * part : (j + 1) * part] = source[rows, pl.ds(at, part)].astype(target.dtype)


def collect(order, source, target):
    blocks = order.shape[0]
    part = source.shape[1] // blocks
    for j in range(blocks):
        at = pl.multiple_of(order[j] * part, 128)
        target[:, pl.ds(at, part)] = source[:, j * part : (j + 1) * part].astype(target.dtype)


def by_pieces(left, pieces):
    found, low = 0.0, 0
    for piece in pieces:
        high = low + piece.shape[0]
        found = found + jnp.dot(left[:, low:high], piece[...], preferred_element_type=jnp.float32)
        low = high
    return found


def project(order, source, gain, shift, mixed, cosine, sine, block):
    rows, width = source.shape
    tile = 512
    tiles = width // tile
    skip = 0 if block == 0 else tiles
    count = len(mixed)
    scale = 1.0 / math.sqrt(HD)

    def body(order_ref, source_ref, gain_ref, shift_ref, cos_ref, sin_ref, *refs):
        weights = refs[:count]
        outs, normed = refs[count:-1], refs[-1]
        at = pl.program_id(0) + skip

        @pl.when(at == skip)
        def _():
            spread(order_ref, source_ref, normed, slice(None))
            chunk = math.gcd(rows, 128)

            def one(i, unused):
                here = pl.ds(pl.multiple_of(i * chunk, chunk), chunk)
                found = normed[here, :].astype(jnp.float32)
                normed[here, :] = layer_norm(found, gain_ref[...], shift_ref[...]).astype(BF)
                return unused

            lax.fori_loop(0, rows // chunk, one, 0)
            outs[0][...] = normed[...].T

        found = by_pieces(normed, weights)

        def turned(c):
            return turn(found[:, c : c + 128], cos_ref[...], sin_ref[...]).astype(BF)

        if block == 0:

            @pl.when(at < tiles)
            def _():
                for c in range(0, tile, 128):
                    outs[1][:, c : c + 128] = (turned(c).astype(jnp.float32) * scale).astype(BF)

        @pl.when(at >= tiles)
        def _():
            for c in range(0, tile, 256):
                outs[-1][:, c : c + 128] = turned(c)
                outs[-1][:, c + 128 : c + 256] = found[:, c + 128 : c + 256].astype(BF)

    table = pl.BlockSpec((rows, 128), lambda j, order: (block, 0))
    outs = [(whole((width, rows)), array((width, rows)))]
    if block == 0:
        outs.append(
            (
                pl.BlockSpec((rows, tile), lambda j, order: (0, jnp.minimum(j, tiles - 1))),
                array((rows, width)),
            )
        )
    outs.append(
        (
            pl.BlockSpec((rows, tile), lambda j, order: (0, jnp.maximum(j + skip - tiles, 0))),
            array((rows, 2 * width)),
        )
    )
    return call(
        body,
        order,
        (3 * tiles - skip,),
        [whole((rows, width)), whole((1, width)), whole((1, width)), table, table]
        + [
            pl.BlockSpec((piece.shape[0], tile), lambda j, order: (0, j + skip)) for piece in mixed
        ],
        outs,
        (source, gain[None, :], shift[None, :], cosine, sine, *mixed),
        f"project{block}",
        2 * rows * width * width * (2 if block else 3),
        scratch=[pltpu.VMEM((rows, width), BF)],
    )


def attend(order, valid, block, state, last, queries, both):
    rows, width = queries.shape
    pairs = width // 128
    first = state is None

    def body(order_ref, valid_ref, q_ref, kv_ref, *refs):
        outs = refs if first else refs[2:]
        parts = head_parts(q_ref[...])
        keys = kv_ref[:, :128]
        flipped = kv_ref[:, 128:].T
        tops, masses, sums = [], [], []
        for head in range(2):
            scores = nt(keys, parts[head])
            seat = lax.broadcasted_iota(jnp.int32, scores.shape, 0)
            scores = jnp.where(seat < valid_ref[block], scores, masked_score)
            top = jnp.max(scores, axis=0, keepdims=True)
            if not first:
                top = jnp.maximum(top, refs[0][0, head : head + 1, :])
            expo = jnp.exp(scores - top)
            mass = jnp.sum(expo, axis=0, keepdims=True)
            held = jnp.dot(
                flipped[head * HD : (head + 1) * HD, :],
                expo.astype(BF),
                preferred_element_type=jnp.float32,
            )
            if not first:
                factor = jnp.exp(refs[0][0, head : head + 1, :] - top)
                mass = mass + refs[0][0, head + 2 : head + 3, :] * factor
                held = held + refs[1][head * HD : (head + 1) * HD, :] * factor
            tops.append(top)
            masses.append(mass)
            sums.append(held)
        blank = jnp.zeros((4, rows), jnp.float32)
        if last:
            found = jnp.concatenate([s / m for s, m in zip(sums, masses)], axis=0)
            outs[1][...] = found.astype(BF)
            found = found.T
            outs[0][...] = found.astype(BF)
            outs[2][...] = found
            lse = [t + jnp.log(m) for t, m in zip(tops, masses)]
            outs[3][...] = jnp.concatenate(lse + masses + [blank], axis=0)[None]
        else:
            outs[0][...] = jnp.concatenate(tops + masses + [blank], axis=0)[None]
            outs[1][...] = jnp.concatenate(sums, axis=0)

    column = pl.BlockSpec((rows, 128), lambda j, order: (0, j))
    stats = pl.BlockSpec((1, 8, rows), lambda j, order: (j, 0, 0))
    carried = pl.BlockSpec((128, rows), lambda j, order: (j, 0))
    stats_shape = array((pairs, 8, rows), jnp.float32)
    if last:
        outs = [
            (column, array((rows, width))),
            (carried, array((width, rows))),
            (column, array((rows, width), jnp.float32)),
            (stats, stats_shape),
        ]
    else:
        outs = [(stats, stats_shape), (carried, array((width, rows), jnp.float32))]
    return call(
        body,
        order,
        (pairs,),
        [
            pl.BlockSpec(memory_space=pltpu.SMEM),
            pl.BlockSpec((rows, 128), lambda j, order: (0, order[j])),
            pl.BlockSpec((rows, 256), lambda j, order: (0, order[j])),
        ]
        + ([] if first else [stats, carried]),
        outs,
        (valid, queries, both, *(() if first else state)),
        f"attend{block}",
        16 * rows * rows * width,
        transcendentals=16 * rows * rows,
    )


def attend_back(order, valid, block, held, last, queries, both, go, attended, lse, cosine, sine):
    rows, width = queries.shape
    pairs = width // 128
    scale = 1.0 / math.sqrt(HD)
    first = held is None

    def body(order_ref, valid_ref, q_ref, kv_ref, go_ref, o_ref, lse_ref, cos_ref, sin_ref, *refs):
        dq_ref, dkv_ref = refs[-2:]
        keys = kv_ref[:, :128]
        values = kv_ref[:, 128:]
        go_all = go_ref[...]
        q_parts = head_parts(q_ref[...])
        go_parts = head_parts(go_all)
        crossed = (go_all.astype(jnp.float32) * o_ref[...]).T
        flipped = keys.T
        dk = jnp.zeros((rows, 128), jnp.float32)
        dv = jnp.zeros((rows, 128), jnp.float32)
        dq = []
        for head in range(2):
            delta = jnp.sum(crossed[head * HD : (head + 1) * HD, :], axis=0, keepdims=True)
            scores = nt(keys, q_parts[head])
            seat = lax.broadcasted_iota(jnp.int32, scores.shape, 0)
            scores = jnp.where(seat < valid_ref[block], scores, masked_score)
            probs = jnp.exp(scores - lse_ref[0, head : head + 1, :])
            grad_probs = nt(values, go_parts[head])
            grad_scores = (probs * (grad_probs - delta)).astype(BF)
            dv = dv + jnp.dot(probs.astype(BF), go_parts[head], preferred_element_type=jnp.float32)
            dk = dk + jnp.dot(grad_scores, q_parts[head], preferred_element_type=jnp.float32)
            dq.append(
                jnp.dot(
                    flipped[head * HD : (head + 1) * HD, :],
                    grad_scores,
                    preferred_element_type=jnp.float32,
                )
            )
        dkv_ref[:, :128] = turn(dk, cos_ref[...], -sin_ref[...]).astype(BF)
        dkv_ref[:, 128:] = dv.astype(BF)
        found = jnp.concatenate(dq, axis=0)
        if not first:
            found = found + refs[0][...]
        if last:
            dq_ref[...] = turn(found.T * scale, cos_ref[...], -sin_ref[...]).astype(BF)
        else:
            dq_ref[...] = found

    column = pl.BlockSpec((rows, 128), lambda j, order: (0, j))
    natural = pl.BlockSpec((rows, 128), lambda j, order: (0, order[j]))
    natural_both = pl.BlockSpec((rows, 256), lambda j, order: (0, order[j]))
    carried = pl.BlockSpec((128, rows), lambda j, order: (j, 0))
    table = pl.BlockSpec((rows, 128), lambda j, order: (block, 0))
    return call(
        body,
        order,
        (pairs,),
        [
            pl.BlockSpec(memory_space=pltpu.SMEM),
            natural,
            natural_both,
            column,
            column,
            pl.BlockSpec((1, 8, rows), lambda j, order: (j, 0, 0)),
            table,
            table,
        ]
        + ([] if first else [carried]),
        [
            (natural, array((rows, width))) if last else (carried, array((width, rows), jnp.float32)),
            (natural_both, array((rows, 2 * width))),
        ],
        (valid, queries, both, go, attended, lse, cosine, sine, *(() if first else (held,))),
        f"attend_back{block}",
        40 * rows * rows * width,
        transcendentals=16 * rows * rows,
    )


def middle(order, attended, mixed, tokens, gain, shift):
    rows, width = tokens.shape
    count = len(mixed)
    chunk = math.gcd(rows, 256)

    def body(order_ref, o_ref, x_ref, gain_ref, shift_ref, *refs):
        weights = refs[:count]
        resid_ref, two_ref, flipped_ref, held = refs[count:]
        found = x_ref[...].astype(jnp.float32) + by_pieces(o_ref, weights)
        resid_ref[...] = found
        spread(order_ref, resid_ref, held, slice(None))
        two = layer_norm(held[...], gain_ref[...], shift_ref[...]).astype(BF)
        two_ref[...] = two
        flipped_ref[...] = two.T

    line = pl.BlockSpec((chunk, width), lambda i, order: (i, 0))
    return call(
        body,
        order,
        (rows // chunk,),
        [line, line, whole((1, width)), whole((1, width))]
        + [pl.BlockSpec((piece.shape[0], width), lambda i, order: (0, 3)) for piece in mixed],
        [
            (line, array((rows, width), jnp.float32)),
            (line, array((rows, width))),
            (pl.BlockSpec((width, chunk), lambda i, order: (0, i)), array((width, rows))),
        ],
        (attended, tokens, gain[None, :], shift[None, :], *mixed),
        "middle",
        2 * rows * width * width,
        scratch=[pltpu.VMEM((chunk, width), jnp.float32)],
    )


def feed(order, two, pair):
    rows, width = two.shape
    blocks = order.shape[0]
    hidden = pair[0].shape[1] // 2
    part = hidden // blocks
    count = len(pair)

    def body(order_ref, two_ref, *refs):
        gate_ref, up_ref, hidden_ref, flipped_ref = refs[count:]
        found = by_pieces(two_ref, refs[:count])
        gate, up = found[:, :part], found[:, part:]
        made = (gate / (1.0 + jnp.exp(-gate)) * up).astype(BF)
        gate_ref[...] = gate.astype(BF)
        up_ref[...] = up.astype(BF)
        hidden_ref[...] = made
        flipped_ref[...] = made.T

    tile = pl.BlockSpec((rows, part), lambda j, order: (0, j))
    shape = array((rows, hidden))
    return call(
        body,
        order,
        (blocks,),
        [whole((rows, width))]
        + [
            pl.BlockSpec((piece.shape[0], 2 * part), lambda j, order: (0, order[j]))
            for piece in pair
        ],
        [
            (tile, shape),
            (tile, shape),
            (tile, shape),
            (pl.BlockSpec((part, rows), lambda j, order: (j, 0)), array((hidden, rows))),
        ],
        (two, *pair),
        "feed",
        4 * rows * width * hidden,
        transcendentals=rows * hidden,
    )


def feed_back(order, upstream, gate, up, made, resid, pair, down):
    rows, width = upstream.shape
    blocks = order.shape[0]
    hidden = gate.shape[1]
    part = hidden // blocks
    count, downs = len(pair), len(down)
    each = blocks // downs

    def body(order_ref, m_ref, gate_ref, up_ref, made_ref, resid_ref, *refs):
        pairs, lows = refs[:count], refs[count : count + downs]
        out_ref, grads_ref, two_ref, total, result = refs[count + downs :]
        at = pl.program_id(0)

        @pl.when(at == 0)
        def _():
            total[...] = jnp.zeros_like(total)
            result[...] = resid_ref[...]

        def one(low):
            gate_all = gate_ref[...].astype(jnp.float32)
            up_all = up_ref[...].astype(jnp.float32)
            sigma = 1.0 / (1.0 + jnp.exp(-gate_all))
            made_grad = nt(m_ref[...], low[...])
            result[...] += jnp.dot(made_ref[...], low[...], preferred_element_type=jnp.float32)
            gate_grad = made_grad * up_all * sigma * (1.0 + gate_all * (1.0 - sigma))
            grads_ref[:, :part] = gate_grad.astype(BF)
            grads_ref[:, part:] = (made_grad * gate_all * sigma).astype(BF)

        for i in range(downs):

            @pl.when((at >= i * each) & (at < (i + 1) * each))
            def _(i=i):
                one(lows[i])

        grads = grads_ref[...]
        low = 0
        for piece in pairs:
            high = low + piece.shape[0]
            total[:, low:high] += nt(grads, piece[...])
            low = high

        @pl.when(at == blocks - 1)
        def _():
            out_ref[...] = result[...].astype(BF)
            collect(order_ref, total, two_ref)

    tile = pl.BlockSpec((rows, part), lambda j, order: (0, j))
    return call(
        body,
        order,
        (blocks,),
        [whole((rows, width)), tile, tile, tile, whole((rows, width))]
        + [
            pl.BlockSpec((piece.shape[0], 2 * part), lambda j, order: (0, order[j]))
            for piece in pair
        ]
        + [
            pl.BlockSpec(
                (part, width), lambda j, order, i=i: (jnp.clip(j - i * each, 0, each - 1), 0)
            )
            for i in range(downs)
        ],
        [
            (whole((rows, width)), array((rows, width))),
            (
                pl.BlockSpec((rows, 2 * part), lambda j, order: (0, order[j])),
                array((rows, 2 * hidden)),
            ),
            (whole((rows, width)), array((rows, width), jnp.float32)),
        ],
        (upstream, gate, up, made, resid, *pair, *down),
        "feed_back",
        8 * rows * width * hidden,
        scratch=[pltpu.VMEM((rows, width), jnp.float32), pltpu.VMEM((rows, width), jnp.float32)],
        transcendentals=rows * hidden,
    )


def norm_back(values, grads, gain):
    centre = values - jnp.mean(values, axis=-1, keepdims=True)
    scale = lax.rsqrt(jnp.mean(centre * centre, axis=-1, keepdims=True) + epsilon)
    normed = centre * scale
    scaled = grads * gain
    inner = jnp.mean(scaled * normed, axis=-1, keepdims=True)
    found = (scaled - jnp.mean(scaled, axis=-1, keepdims=True) - normed * inner) * scale
    return (
        found,
        jnp.sum(grads * normed, axis=0, keepdims=True),
        jnp.sum(grads, axis=0, keepdims=True),
    )


def middle_back(order, grads, resid, upstream, mixed, gain):
    rows, width = resid.shape
    count = len(mixed)
    chunk = math.gcd(rows, 256)

    def body(order_ref, grads_ref, resid_ref, m_ref, gain_ref, *refs):
        weights = refs[:count]
        y_ref, a_ref, go_ref, edge_ref = refs[count:]

        @pl.when(pl.program_id(0) == 0)
        def _():
            edge_ref[...] = jnp.zeros_like(edge_ref)

        found, gain_grad, shift_grad = norm_back(resid_ref[...], grads_ref[...], gain_ref[...])
        found = m_ref[...].astype(jnp.float32) + found
        edge_ref[0:1, :] += gain_grad
        edge_ref[1:2, :] += shift_grad
        y_ref[...] = found
        a_ref[...] = found.astype(BF)
        low = 0
        for weight in weights:
            high = low + weight.shape[0]
            go_ref[:, low:high] = nt(a_ref[...], weight[...]).astype(BF)
            low = high

    line = pl.BlockSpec((chunk, width), lambda i, order: (i, 0))
    return call(
        body,
        order,
        (rows // chunk,),
        [line, line, line, whole((1, width))]
        + [pl.BlockSpec((piece.shape[0], width), lambda i, order: (0, 3)) for piece in mixed],
        [
            (line, array((rows, width), jnp.float32)),
            (line, array((rows, width))),
            (line, array((rows, width))),
            (whole((8, width)), array((8, width), jnp.float32)),
        ],
        (grads, resid, upstream, gain[None, :], *mixed),
        "middle_back",
        2 * rows * width * width,
    )


def pull(order, dq, both, mixed, block):
    rows, width = both.shape[0], both.shape[1] // 2
    tile = 512
    tiles = width // tile
    count = len(mixed)
    skip = 0 if block == 0 else tiles
    steps = 3 * tiles - skip
    dtype = BF if block else jnp.float32

    def body(order_ref, *refs):
        lefts = refs[: 1 if block else 2]
        weights = refs[len(lefts) : len(lefts) + count]
        out_ref, total = refs[len(lefts) + count :]
        at = pl.program_id(0)

        @pl.when(at == 0)
        def _():
            total[...] = jnp.zeros_like(total)

        def one(left):
            low = 0
            for weight in weights:
                high = low + weight.shape[0]
                total[:, low:high] += nt(left[...], weight[...])
                low = high

        if block:
            one(lefts[0])
        else:

            @pl.when(at < tiles)
            def _():
                one(lefts[0])

            @pl.when(at >= tiles)
            def _():
                one(lefts[1])

        @pl.when(at == steps - 1)
        def _():
            out_ref[...] = total[...].astype(dtype)

    lefts = [] if block else [pl.BlockSpec((rows, tile), lambda j, order: (0, jnp.minimum(j, tiles - 1)))]
    lefts.append(pl.BlockSpec((rows, tile), lambda j, order: (0, jnp.maximum(j + skip - tiles, 0))))
    return call(
        body,
        order,
        (steps,),
        lefts
        + [
            pl.BlockSpec((piece.shape[0], tile), lambda j, order: (0, j + skip)) for piece in mixed
        ],
        [(whole((rows, width)), array((rows, width), dtype))],
        ((both,) if block else (dq, both)) + tuple(mixed),
        f"pull{block}",
        rows * width,
        scratch=[pltpu.VMEM((rows, width), jnp.float32)],
    )[0]


def end_back(order, parts, tokens, grads, gain):
    rows, width = tokens.shape
    count = len(parts)
    chunk = math.gcd(rows, 256)

    def body(order_ref, x_ref, y_ref, gain_ref, *refs):
        sources = refs[:count]
        out_ref, edge_ref, held, total = refs[count:]

        @pl.when(pl.program_id(0) == 0)
        def _():
            edge_ref[...] = jnp.zeros_like(edge_ref)

        held[...] = sum(source[...].astype(jnp.float32) for source in sources)
        collect(order_ref, held, total)
        found, gain_grad, shift_grad = norm_back(
            x_ref[...].astype(jnp.float32), total[...], gain_ref[...]
        )
        edge_ref[0:1, :] += gain_grad
        edge_ref[1:2, :] += shift_grad
        out_ref[...] = (y_ref[...] + found).astype(BF)

    line = pl.BlockSpec((chunk, width), lambda i, order: (i, 0))
    return call(
        body,
        order,
        (rows // chunk,),
        [line, line, whole((1, width))] + [line] * count,
        [(line, array((rows, width))), (whole((8, width)), array((8, width), jnp.float32))],
        (tokens, grads, gain[None, :], *parts),
        "end_back",
        0,
        scratch=[pltpu.VMEM((chunk, width), jnp.float32), pltpu.VMEM((chunk, width), jnp.float32)],
    )


def join(first, second, part):
    rows, width = first.shape
    stacked = jnp.stack([first.reshape(rows, -1, part), second.reshape(rows, -1, part)], axis=2)
    return stacked.reshape(rows, 2 * width)


def part_ways(both, part):
    rows, width = both.shape
    cut = both.reshape(rows, -1, 2, part)
    return cut[:, :, 0].reshape(rows, width // 2), cut[:, :, 1].reshape(rows, width // 2)


def shards(
    plan,
    tokens,
    lengths,
    cotangent,
    query_weight,
    key_weight,
    value_weight,
    output_weight,
    gate_weight,
    up_weight,
    down_weight,
    attention_gain,
    attention_shift,
    feed_gain,
    feed_shift,
):
    slots = plan.slots()
    windows, local_len, width = tokens.shape
    rows = windows * local_len
    hidden = gate_weight.shape[1]
    place = lax.axis_index("ctx")
    exact = (width // plan.dp) % 128 == 0
    order = slots if exact else jnp.arange(8, dtype=jnp.int32)
    part = hidden // order.shape[0]

    def pieces_of(chain, shard):
        run, pieces = chain.value
        if exact:
            return [run, pieces[-1]]
        return [assemble(slots, pieces, shard.shape[0] * plan.ctx)]

    def in_slots(flipped):
        if exact:
            return flipped
        cut = flipped.reshape(plan.dp, -1, flipped.shape[1])
        return jnp.take(cut, slots, axis=0).reshape(flipped.shape)

    edge = jnp.stack([attention_gain, attention_shift, feed_gain, feed_shift], axis=1)
    edge = jnp.pad(edge, ((0, 0), (0, 124)))
    both = join(key_weight, value_weight, 128)
    mixed = jnp.concatenate([query_weight, both, output_weight, edge], axis=1)
    mix = Chain(gather_steps(plan, mixed))

    seats = jnp.arange(local_len, dtype=jnp.int32)
    starts = jnp.asarray(plan.blocks)[place] * local_len
    valid = jnp.clip(lengths[0] - starts, 0, local_len)
    cosine, sine = rotary_tables((starts[:, None] + seats[None, :]).reshape(-1))
    real = (place * local_len + seats < lengths[0])[:, None]
    upstream = jnp.where(real, cotangent.reshape(rows, width), 0)
    own = tokens.reshape(rows, width)

    pair_own = join(gate_weight, up_weight, part)
    early = (pair_own, cosine, sine, upstream)
    pair_own, cosine, sine, upstream = step(early, mix)
    pair = Chain(gather_steps(plan, pair_own))
    own = step(own, mix)
    came = {}
    own, window = begin(own, window_steps(plan, own, came))
    own = step(own, mix)
    own = step(own, pair)
    own = finish(own, mix)
    mixed_w = pieces_of(mix, mixed)
    cols = jnp.concatenate([piece[:, 4 * width : 4 * width + 4] for piece in mixed_w])
    cols = cols.T.astype(jnp.float32)
    back = jnp.asarray(plan.back)[lax.axis_index("dp")] if exact else order
    natural = cols.reshape(4, order.shape[0], -1)[:, back].reshape(4, width)

    flipped, both = {}, {}
    flipped[0], queries, both[0] = project(order, own, cols[0], cols[1], mixed_w, cosine, sine, 0)
    state = attend(order, valid, 0, None, plan.ctx == 1, queries, both[0])
    down = None
    for k in range(1, plan.ctx):
        while k not in came:
            state = step(state, window, pair) if k == 1 else step(state, window)
        if k == 2:
            down_own, state = tie(down_weight, state)
            down = Chain(gather_steps(plan, down_own))
        if k == 3:
            state = step(state, pair)
        flipped[k], both[k] = project(
            order, came[k], cols[0], cols[1], mixed_w, cosine, sine, k
        )
        state = attend(order, valid, k, state, k == plan.ctx - 1, queries, both[k])
    state = step(state, down)
    low, low_flipped, attended, lse = state
    resid, two, two_flipped = middle(order, low, mixed_w, own, cols[2], cols[3])
    two = finish(two, pair)
    two = step(two, down)
    pair_w = pieces_of(pair, pair_own)
    gate, up, made, made_flipped = feed(order, two, pair_w)
    made, down_sum = begin(
        made, sum_steps(plan, product_of(plan, [[(in_slots(made_flipped), upstream)]]))
    )
    made = finish(made, down)
    down_w = pieces_of(down, down_weight)
    output, pair_grads, two_grads = feed_back(
        order, upstream, gate, up, made, resid, pair_w, down_w
    )
    output = output.reshape(windows, local_len, width)

    two_grads, pair_grads = step((two_grads, pair_grads), down_sum)
    two_grads, pair_sum = begin(
        two_grads, sum_steps(plan, product_of(plan, [[(in_slots(two_flipped), pair_grads)]]))
    )
    y_grads, low_grads, go, edge_two = middle_back(
        order, two_grads, resid, upstream, mixed_w, natural[2]
    )
    go = step(go, pair_sum)
    go, output_sum = begin(
        go, sum_steps(plan, product_of(plan, [[(in_slots(low_flipped), low_grads)]]))
    )
    held, back_way = None, None
    grads, parts = {}, {}
    flipped = {k: in_slots(flipped[k]) for k in flipped}
    for k in reversed(range(plan.ctx)):
        held, grads[k] = attend_back(
            order, valid, k, held, k == 0, queries, both[k], go, attended, lse, cosine, sine
        )
        if k:
            held = step(held, down_sum, output_sum, *([] if k == plan.ctx - 1 else [pair_sum]))
            parts[k] = pull(order, held, grads[k], mixed_w, k)
            held, parts[k] = tie(held, parts[k])
            if plan.line:
                if back_way is None:
                    held, back_way = begin(held, return_steps(plan, parts))
                else:
                    held = step(held, back_way)
    groups = [[(flipped[0], held)], [(flipped[k], grads[k]) for k in range(plan.ctx)]]
    held, last_sum = begin(held, sum_steps(plan, product_of(plan, groups)))
    held = step(held, output_sum, pair_sum)
    part_grads = pull(order, held, grads[0], mixed_w, 0)
    part_grads = step(part_grads, last_sum)
    if plan.line:
        part_grads = finish(part_grads, back_way)
        sends = back_way.value
    else:
        sends = [lax.ppermute(parts[k], AXES, plan.across[k]) for k in range(1, plan.ctx)]
    tokens_grad, edge_one = end_back(
        order, [part_grads, *sends], own, y_grads, natural[0]
    )
    vectors = sum_vectors(plan, (edge_one[0], edge_one[1], edge_two[0], edge_two[1]))
    finish((), last_sum)
    finish((), down_sum, output_sum, pair_sum)
    gate_grad, up_grad = part_ways(pair_sum.value, part)
    key_grad, value_grad = part_ways(last_sum.value[:, width:], 128)
    return (
        output,
        tokens_grad.reshape(windows, local_len, width),
        last_sum.value[:, :width],
        key_grad,
        value_grad,
        output_sum.value,
        gate_grad,
        up_grad,
        down_sum.value,
        *vectors,
    )


def solution(mesh):
    return jax.shard_map(
        functools.partial(shards, Plan(mesh)),
        mesh=mesh,
        in_specs=(
            P("dp", "ctx", None),
            P("dp"),
            P("dp", "ctx", None),
            P(("dp", "ctx"), None),
            P(("dp", "ctx"), None),
            P(("dp", "ctx"), None),
            P(("dp", "ctx"), None),
            P(("dp", "ctx"), None),
            P(("dp", "ctx"), None),
            P(("dp", "ctx"), None),
            P(("dp", "ctx")),
            P(("dp", "ctx")),
            P(("dp", "ctx")),
            P(("dp", "ctx")),
        ),
        out_specs=(
            P("dp", "ctx", None),
            P("dp", "ctx", None),
            P(("dp", "ctx"), None),
            P(("dp", "ctx"), None),
            P(("dp", "ctx"), None),
            P(("dp", "ctx"), None),
            P(("dp", "ctx"), None),
            P(("dp", "ctx"), None),
            P(("dp", "ctx"), None),
            P(("dp", "ctx")),
            P(("dp", "ctx")),
            P(("dp", "ctx")),
            P(("dp", "ctx")),
        ),
        check_vma=False,
    )
```

```python
import functools
import math

import numpy as np

import jax
import jax.numpy as jnp
from jax import lax
from jax.experimental import pallas as pl
from jax.experimental.pallas import tpu as pltpu
from jax.sharding import PartitionSpec as P

H = 16
HD = 64
L = 2048


epsilon = 1e-05
masked_score = -1e30


def layer_norm(values, gain, shift):
    centre = values - jnp.mean(values, axis=-1, keepdims=True)
    spread = jnp.mean(centre * centre, axis=-1, keepdims=True)
    return centre * lax.rsqrt(spread + epsilon) * gain + shift


def rotary_tables(positions):
    half = HD // 2
    turns = jnp.arange(2 * HD, dtype=jnp.int32) % half
    freqs = jnp.exp(turns.astype(jnp.float32) * (-2.0 * math.log(10000.0) / HD))
    angles = positions.astype(jnp.float32)[:, None] * freqs[None, :]
    return (jnp.cos(angles), jnp.sin(angles))


AXES = ("dp", "ctx")
BF = jnp.bfloat16


class Plan:
    def __init__(self, mesh):
        self.dp, self.ctx = mesh.shape["dp"], mesh.shape["ctx"]
        self.stages = self.dp.bit_length() - 2
        self.ctx_bits = self.ctx.bit_length() - 1
        orders = (list(range(1, self.stages + 1)), list(range(self.stages, 0, -1)))
        self.core = self.pairs(lambda d, z: (d ^ 1, z))
        self.stage = [
            self.pairs(lambda d, z, t=t: (d ^ (1 << orders[d & 1][t]), z)) for t in range(self.stages)
        ]
        self.across = [self.pairs(lambda d, z, k=k: (d, z ^ k)) for k in range(self.ctx)]
        self.line = self.ctx == 4
        self.inner = self.pairs(lambda d, z: (d, z ^ 3), (1, 2))
        self.outward = self.pairs(lambda d, z: (d, z ^ 1), (1, 2))
        self.inward = self.pairs(lambda d, z: (d, z ^ 1), (0, 3))
        self.blocks = np.arange(self.ctx)[:, None] ^ np.arange(self.ctx)[None, :]
        if self.line:
            self.blocks = np.array([[0, 1, 2, 3], [1, 0, 2, 3], [2, 3, 1, 0], [3, 2, 1, 0]])
        self.blocks = self.blocks.astype(np.int32)
        half = self.dp // 2
        table = np.zeros((self.dp, self.dp), np.int32)
        for d in range(self.dp):
            for j in range(self.dp):
                owner = d ^ 1 if j >= half else d
                block = owner
                for t in range(self.stages):
                    if (j % half) >> (self.stages - 1 - t) & 1:
                        block ^= 1 << orders[owner & 1][t]
                table[d, j] = block
        self.table = table
        self.back = np.argsort(table, axis=1).astype(np.int32)

    def pairs(self, target, places=None):
        found = []
        for d in range(self.dp):
            for z in range(self.ctx) if places is None else places:
                other, place = target(d, z)
                found.append((d * self.ctx + z, other * self.ctx + place))
        return found

    def slots(self):
        return jnp.asarray(self.table)[lax.axis_index("dp")]


def assemble(slots, pieces, rows):
    blocks = slots.shape[0]
    width = pieces[0].shape[1]
    sizes = [piece.shape[0] // rows for piece in pieces]
    starts = [sum(sizes[:i]) for i in range(len(sizes))]

    def body(order, *refs):
        slot = pl.program_id(0)
        out = refs[-1]
        for piece, start, size in zip(refs, starts, sizes):

            @pl.when((slot >= start) & (slot < start + size))
            def _(piece=piece):
                out[...] = piece[...]

    specs = [
        pl.BlockSpec(
            (rows, width),
            lambda j, order, start=start, size=size: (jnp.clip(j - start, 0, size - 1), 0),
        )
        for start, size in zip(starts, sizes)
    ]
    return pl.pallas_call(
        body,
        out_shape=jax.ShapeDtypeStruct((blocks * rows, width), pieces[0].dtype),
        grid_spec=pltpu.PrefetchScalarGridSpec(
            num_scalar_prefetch=1,
            grid=(blocks,),
            in_specs=specs,
            out_specs=pl.BlockSpec((rows, width), lambda j, order: (order[j], 0)),
        ),
        name="assemble",
    )(slots, *pieces)


def tie(values, others):
    leaves, tree = jax.tree.flatten((values, others))
    return jax.tree.unflatten(tree, lax.optimization_barrier(leaves))


class Chain:
    def __init__(self, steps):
        self.steps = steps
        self.flying, self.sent = next(steps)
        self.done = False
        self.value = None

    def land(self, came):
        if self.done:
            return
        try:
            self.flying, self.sent = self.steps.send(came)
        except StopIteration as stop:
            self.flying, self.sent, self.done, self.value = [], [], True, stop.value


def step(main, *chains):
    main, came = tie(main, [chain.flying for chain in chains])
    for chain, arrays in zip(chains, came):
        chain.land(arrays)
    return tie(main, [chain.sent for chain in chains])[0]


def wait(main, *chains):
    main, came = tie(main, [chain.flying for chain in chains])
    for chain, arrays in zip(chains, came):
        chain.came = arrays
    return main


def go_on(main, *chains):
    main, came = tie(main, [chain.came for chain in chains])
    for chain, arrays in zip(chains, came):
        chain.land(arrays)
    return tie(main, [chain.sent for chain in chains])[0]


def begin(main, steps):
    chain = Chain(steps)
    return tie(main, chain.sent)[0], chain


def finish(main, *chains):
    while not all(chain.done for chain in chains):
        main = step(main, *chains)
    return main


def gather_steps(plan, shard, line=False):
    place = lax.axis_index("ctx")
    if line and plan.line:
        near, middle = yield (
            [lax.ppermute(shard, AXES, plan.across[1]), lax.ppermute(shard, AXES, plan.inner)],
            [shard],
        )
        far, cross = yield (
            [lax.ppermute(middle, AXES, plan.outward), lax.ppermute(near, AXES, plan.inner)],
            [middle, near],
        )
        (last,) = yield [lax.ppermute(cross, AXES, plan.outward)], [cross]
        two, three = middle + far, cross + last
        upper = place >= 2
        blocks = [shard, near, jnp.where(upper, three, two), jnp.where(upper, two, three)]
        odd = place % 2 == 1
        run = jnp.where(
            upper,
            jnp.concatenate(blocks[2:] + [jnp.where(odd, near, shard), jnp.where(odd, shard, near)]),
            jnp.concatenate([jnp.where(odd, near, shard), jnp.where(odd, shard, near)] + blocks[2:]),
        )
    else:
        blocks = yield (
            [lax.ppermute(shard, AXES, plan.across[k]) for k in range(1, plan.ctx)],
            [shard],
        )
        blocks = [shard, *blocks]
        for bit in range(plan.ctx_bits):
            upper = (place >> bit) & 1 == 1
            blocks = [
                jnp.where(upper, jnp.concatenate([b, a]), jnp.concatenate([a, b]))
                for a, b in zip(blocks[::2], blocks[1::2])
            ]
        run = blocks[0]
    *early, final = reversed(plan.stage)
    for pairs in early:
        (other,) = yield [lax.ppermute(run, AXES, pairs)], [run]
        run = jnp.concatenate([run, other])
    other, far = yield [lax.ppermute(run, AXES, final), lax.ppermute(run, AXES, plan.core)], [run]
    (last,) = yield [lax.ppermute(other, AXES, plan.core)], [other]
    return [run, other, far, last]


def add(a, b):
    return (a.astype(jnp.float32) + b.astype(jnp.float32)).astype(BF)


def window_steps(plan, own, came):
    if not plan.line:
        others = yield [lax.ppermute(own, AXES, plan.across[k]) for k in range(1, plan.ctx)], [own]
        came.update(enumerate(others, 1))
        return
    near, middle = yield (
        [lax.ppermute(own, AXES, plan.across[1]), lax.ppermute(own, AXES, plan.inner)],
        [own],
    )
    came[1] = near
    far, cross = yield (
        [lax.ppermute(middle, AXES, plan.outward), lax.ppermute(near, AXES, plan.inner)],
        [middle, near],
    )
    came[2] = middle + far
    (last,) = yield [lax.ppermute(cross, AXES, plan.outward)], [cross]
    came[3] = cross + last


def return_steps(plan, parts):
    (came,) = yield [lax.ppermute(parts[3], AXES, plan.inward)], [parts[3]]
    run = add(parts[3], came)
    near, cross = yield (
        [lax.ppermute(parts[2], AXES, plan.inward), lax.ppermute(run, AXES, plan.inner)],
        [parts[2], run],
    )
    run, last = add(parts[2], near), add(parts[1], cross)
    return (
        yield (
            [
                lax.ppermute(run, AXES, plan.inner),
                lax.ppermute(last, AXES, plan.across[1]),
            ],
            [run, last],
        )
    )


def sum_steps(plan, product, send=None):
    place = lax.axis_index("ctx")
    half = plan.dp // 2

    if send is None:
        send = product(half, plan.dp)
    (other,) = yield [lax.ppermute(send, AXES, plan.core)], [send]
    rows = other.shape[0] // half
    size = half // 2
    send = product(size, half, other[size * rows :])
    flying = [lax.ppermute(send, AXES, plan.stage[0])]
    keep = product(0, size, other[: size * rows])
    (other,) = yield flying, [send, keep]
    held = add(keep, other)
    for pairs in plan.stage[1:]:
        size //= 2
        send = held[size * rows :]
        (other,) = yield [lax.ppermute(send, AXES, pairs)], [send]
        held = add(held[: size * rows], other)
    width = held.shape[1]
    for bit in range(plan.ctx_bits):
        left = 1 << (plan.ctx_bits - bit - 1)
        lower = (place >> bit) & 1
        cut = held.reshape(left, 2, -1, width)
        send = lax.dynamic_index_in_dim(cut, 1 - lower, 1, False).reshape(-1, width)
        keep = lax.dynamic_index_in_dim(cut, lower, 1, False).reshape(-1, width)
        (other,) = yield [lax.ppermute(send, AXES, plan.across[1 << bit])], [send]
        if left > 1:
            held = add(keep, other)
        else:
            held = keep.astype(jnp.float32) + other.astype(jnp.float32)
    return held


def sum_vectors(plan, vectors):
    count = plan.dp * plan.ctx
    packed = jnp.stack(vectors).reshape(len(vectors), count, -1).transpose(1, 0, 2)
    part = packed.shape[2]
    packed = packed.reshape(count, len(vectors) * part)
    came = lax.all_to_all(packed, AXES, split_axis=0, concat_axis=0, tiled=True)
    whole = jnp.sum(came, axis=0)
    return [whole[i * part : (i + 1) * part] for i in range(len(vectors))]


def nt(a, b):
    return lax.dot_general(a, b, (((1,), (1,)), ((), ())), preferred_element_type=jnp.float32)


def turn(values, cosine, sine):
    lane = lax.broadcasted_iota(jnp.int32, values.shape, 1)
    ahead = pltpu.roll(values, 128 - HD // 2, 1)
    behind = pltpu.roll(values, HD // 2, 1)
    turned = jnp.where(lane % HD < HD // 2, -ahead, behind)
    return values * cosine + turned * sine


def head_parts(values):
    lane = lax.broadcasted_iota(jnp.int32, values.shape, 1)
    zero = jnp.zeros_like(values)
    return [jnp.where(lane < HD, values, zero), jnp.where(lane < HD, zero, values)]


def product_of(plan, groups):
    def product(start, end, more=None):
        columns = []
        low = 0
        for terms in groups:
            found = 0.0
            for flipped, right in terms:
                rows = flipped.shape[0] // plan.dp
                part = flipped[start * rows : end * rows]
                found = found + jnp.dot(part, right, preferred_element_type=jnp.float32)
            high = low + found.shape[1]
            if more is not None:
                found = found + more[:, low:high].astype(jnp.float32)
            columns.append(found.astype(BF))
            low = high
        return columns[0] if len(columns) == 1 else jnp.concatenate(columns, axis=1)

    return product


def whole(shape):
    return pl.BlockSpec(shape, lambda *at: (0,) * len(shape))


def call(body, order, grid, ins, outs, operands, name, flops, scratch=(), transcendentals=0):
    size = lambda a: math.prod(a.shape) * jnp.dtype(a.dtype).itemsize
    out_shape = [shape for spec, shape in outs]
    return pl.pallas_call(
        body,
        out_shape=out_shape,
        grid_spec=pltpu.PrefetchScalarGridSpec(
            num_scalar_prefetch=1,
            grid=grid,
            in_specs=ins,
            out_specs=[spec for spec, shape in outs],
            scratch_shapes=list(scratch),
        ),
        cost_estimate=pl.CostEstimate(
            flops=flops,
            bytes_accessed=sum(size(a) for a in [*operands, *out_shape]),
            transcendentals=transcendentals,
        ),
        name=name,
    )(order, *operands)


def array(shape, dtype=BF):
    return jax.ShapeDtypeStruct(shape, dtype)


def spread(order, source, target, rows):
    blocks = order.shape[0]
    part = source.shape[1] // blocks
    for j in range(blocks):
        at = pl.multiple_of(order[j] * part, 128)
        target[rows, j * part : (j + 1) * part] = source[rows, pl.ds(at, part)].astype(target.dtype)


def collect(order, source, target):
    blocks = order.shape[0]
    part = source.shape[1] // blocks
    for j in range(blocks):
        at = pl.multiple_of(order[j] * part, 128)
        target[:, pl.ds(at, part)] = source[:, j * part : (j + 1) * part].astype(target.dtype)


def by_pieces(left, pieces):
    found, low = 0.0, 0
    for piece in pieces:
        high = low + piece.shape[0]
        found = found + jnp.dot(left[:, low:high], piece[...], preferred_element_type=jnp.float32)
        low = high
    return found


def project(order, source, cols, mixed, cosine, sine, block):
    rows, width = source.shape
    tile = 512
    tiles = width // tile
    skip = 0 if block == 0 else tiles
    count = len(mixed)
    scale = 1.0 / math.sqrt(HD)

    def body(order_ref, source_ref, cos_ref, sin_ref, *refs):
        weights, edges = refs[:count], refs[count : -1 - found_outs]
        outs, normed = refs[-1 - found_outs : -1], refs[-1]
        cols_ref = outs[-1] if block == 0 else edges[0]
        at = pl.program_id(0) + skip

        @pl.when(at == skip)
        def _():
            if block == 0:
                low = 0
                for edge in edges:
                    high = low + edge.shape[0]
                    cols_ref[:, low:high] = edge[...].astype(jnp.float32).T[:8]
                    low = high
            spread(order_ref, source_ref, normed, slice(None))
            chunk = math.gcd(rows, 128)

            def one(i, unused):
                here = pl.ds(pl.multiple_of(i * chunk, chunk), chunk)
                found = normed[here, :].astype(jnp.float32)
                normed[here, :] = layer_norm(found, cols_ref[0:1, :], cols_ref[1:2, :]).astype(BF)
                return unused

            lax.fori_loop(0, rows // chunk, one, 0)
            outs[0][...] = normed[...].T

        found = by_pieces(normed, weights)

        def turned(c):
            return turn(found[:, c : c + 128], cos_ref[...], sin_ref[...]).astype(BF)

        if block == 0:

            @pl.when(at < tiles)
            def _():
                for c in range(0, tile, 128):
                    outs[1][:, c : c + 128] = (turned(c).astype(jnp.float32) * scale).astype(BF)

        @pl.when(at >= tiles)
        def _():
            both_ref = outs[2] if block == 0 else outs[1]
            for c in range(0, tile, 256):
                both_ref[:, c : c + 128] = turned(c)
                both_ref[:, c + 128 : c + 256] = found[:, c + 128 : c + 256].astype(BF)

    table = pl.BlockSpec((rows, 128), lambda j, order: (block, 0))
    outs = [(whole((width, rows)), array((width, rows)))]
    if block == 0:
        outs.append(
            (
                pl.BlockSpec((rows, tile), lambda j, order: (0, jnp.minimum(j, tiles - 1))),
                array((rows, width)),
            )
        )
    outs.append(
        (
            pl.BlockSpec((rows, tile), lambda j, order: (0, jnp.maximum(j + skip - tiles, 0))),
            array((rows, 2 * width)),
        )
    )
    if block == 0:
        outs.append((whole((8, width)), array((8, width), jnp.float32)))
        edges = [
            pl.BlockSpec((piece.shape[0], 128), lambda j, order: (0, 3 * width // 128))
            for piece in mixed
        ]
    else:
        edges = [whole((8, width))]
    found_outs = len(outs)
    return call(
        body,
        order,
        (3 * tiles - skip,),
        [whole((rows, width)), table, table]
        + [
            pl.BlockSpec((piece.shape[0], tile), lambda j, order: (0, j + skip)) for piece in mixed
        ]
        + edges,
        outs,
        (source, cosine, sine, *mixed, *(mixed if block == 0 else [cols])),
        f"project{block}",
        32 * rows * width * width * (2 if block else 3),
        scratch=[pltpu.VMEM((rows, width), BF)],
    )


def attend(order, valid, block, state, last, queries, both):
    rows, width = queries.shape
    pairs = width // 128
    first = state is None

    def body(order_ref, valid_ref, q_ref, kv_ref, *refs):
        outs = refs if first else refs[2:]
        parts = head_parts(q_ref[...])
        keys = kv_ref[:, :128]
        flipped = kv_ref[:, 128:].T
        tops, masses, sums = [], [], []
        for head in range(2):
            scores = nt(keys, parts[head])
            seat = lax.broadcasted_iota(jnp.int32, scores.shape, 0)
            scores = jnp.where(seat < valid_ref[block], scores, masked_score)
            top = jnp.max(scores, axis=0, keepdims=True)
            if not first:
                top = jnp.maximum(top, refs[0][0, head : head + 1, :])
            expo = jnp.exp(scores - top)
            mass = jnp.sum(expo, axis=0, keepdims=True)
            held = jnp.dot(
                flipped[head * HD : (head + 1) * HD, :],
                expo.astype(BF),
                preferred_element_type=jnp.float32,
            )
            if not first:
                factor = jnp.exp(refs[0][0, head : head + 1, :] - top)
                mass = mass + refs[0][0, head + 2 : head + 3, :] * factor
                held = held + refs[1][head * HD : (head + 1) * HD, :] * factor
            tops.append(top)
            masses.append(mass)
            sums.append(held)
        blank = jnp.zeros((4, rows), jnp.float32)
        if last:
            found = jnp.concatenate([s / m for s, m in zip(sums, masses)], axis=0)
            outs[1][...] = found.astype(BF)
            found = found.T
            outs[0][...] = found.astype(BF)
            outs[2][...] = found
            lse = [t + jnp.log(m) for t, m in zip(tops, masses)]
            outs[3][...] = jnp.concatenate(lse + masses + [blank], axis=0)[None]
        else:
            outs[0][...] = jnp.concatenate(tops + masses + [blank], axis=0)[None]
            outs[1][...] = jnp.concatenate(sums, axis=0)

    column = pl.BlockSpec((rows, 128), lambda j, order: (0, j))
    stats = pl.BlockSpec((1, 8, rows), lambda j, order: (j, 0, 0))
    carried = pl.BlockSpec((128, rows), lambda j, order: (j, 0))
    stats_shape = array((pairs, 8, rows), jnp.float32)
    if last:
        outs = [
            (column, array((rows, width))),
            (carried, array((width, rows))),
            (column, array((rows, width), jnp.float32)),
            (stats, stats_shape),
        ]
    else:
        outs = [(stats, stats_shape), (carried, array((width, rows), jnp.float32))]
    return call(
        body,
        order,
        (pairs,),
        [
            pl.BlockSpec(memory_space=pltpu.SMEM),
            pl.BlockSpec((rows, 128), lambda j, order: (0, order[j])),
            pl.BlockSpec((rows, 256), lambda j, order: (0, order[j])),
        ]
        + ([] if first else [stats, carried]),
        outs,
        (valid, queries, both, *(() if first else state)),
        f"attend{block}",
        256 * rows * rows * width,
        transcendentals=16 * rows * rows,
    )


def attend_back(order, valid, block, held, last, queries, both, go, attended, lse, cosine, sine):
    rows, width = queries.shape
    pairs = width // 128
    scale = 1.0 / math.sqrt(HD)
    first = held is None

    def body(order_ref, valid_ref, q_ref, kv_ref, go_ref, o_ref, lse_ref, cos_ref, sin_ref, *refs):
        dq_ref, dkv_ref = refs[-2:]
        keys = kv_ref[:, :128]
        values = kv_ref[:, 128:]
        go_all = go_ref[...]
        q_parts = head_parts(q_ref[...])
        go_parts = head_parts(go_all)
        crossed = (go_all.astype(jnp.float32) * o_ref[...]).T
        flipped = keys.T
        dk = jnp.zeros((rows, 128), jnp.float32)
        dv = jnp.zeros((rows, 128), jnp.float32)
        dq = []
        for head in range(2):
            delta = jnp.sum(crossed[head * HD : (head + 1) * HD, :], axis=0, keepdims=True)
            scores = nt(keys, q_parts[head])
            seat = lax.broadcasted_iota(jnp.int32, scores.shape, 0)
            scores = jnp.where(seat < valid_ref[block], scores, masked_score)
            probs = jnp.exp(scores - lse_ref[0, head : head + 1, :])
            grad_probs = nt(values, go_parts[head])
            grad_scores = (probs * (grad_probs - delta)).astype(BF)
            dv = dv + jnp.dot(probs.astype(BF), go_parts[head], preferred_element_type=jnp.float32)
            dk = dk + jnp.dot(grad_scores, q_parts[head], preferred_element_type=jnp.float32)
            dq.append(
                jnp.dot(
                    flipped[head * HD : (head + 1) * HD, :],
                    grad_scores,
                    preferred_element_type=jnp.float32,
                )
            )
        dkv_ref[:, :128] = turn(dk, cos_ref[...], -sin_ref[...]).astype(BF)
        dkv_ref[:, 128:] = dv.astype(BF)
        found = jnp.concatenate(dq, axis=0)
        if not first:
            found = found + refs[0][...]
        if last:
            dq_ref[...] = turn(found.T * scale, cos_ref[...], -sin_ref[...]).astype(BF)
        else:
            dq_ref[...] = found

    column = pl.BlockSpec((rows, 128), lambda j, order: (0, j))
    natural = pl.BlockSpec((rows, 128), lambda j, order: (0, order[j]))
    natural_both = pl.BlockSpec((rows, 256), lambda j, order: (0, order[j]))
    carried = pl.BlockSpec((128, rows), lambda j, order: (j, 0))
    table = pl.BlockSpec((rows, 128), lambda j, order: (block, 0))
    return call(
        body,
        order,
        (pairs,),
        [
            pl.BlockSpec(memory_space=pltpu.SMEM),
            natural,
            natural_both,
            column,
            column,
            pl.BlockSpec((1, 8, rows), lambda j, order: (j, 0, 0)),
            table,
            table,
        ]
        + ([] if first else [carried]),
        [
            (natural, array((rows, width))) if last else (carried, array((width, rows), jnp.float32)),
            (natural_both, array((rows, 2 * width))),
        ],
        (valid, queries, both, go, attended, lse, cosine, sine, *(() if first else (held,))),
        f"attend_back{block}",
        40 * rows * rows * width,
        transcendentals=16 * rows * rows,
    )


def middle(order, attended, mixed, tokens, cols):
    rows, width = tokens.shape
    count = len(mixed)
    last = mixed[0].shape[1] // width - 1
    chunk = math.gcd(rows, 256)

    def body(order_ref, o_ref, x_ref, cols_ref, *refs):
        weights = refs[:count]
        resid_ref, two_ref, flipped_ref, held = refs[count:]
        found = x_ref[...].astype(jnp.float32) + by_pieces(o_ref, weights)
        resid_ref[...] = found
        spread(order_ref, resid_ref, held, slice(None))
        two = layer_norm(held[...], cols_ref[2:3, :], cols_ref[3:4, :]).astype(BF)
        two_ref[...] = two
        flipped_ref[...] = two.T

    line = pl.BlockSpec((chunk, width), lambda i, order: (i, 0))
    return call(
        body,
        order,
        (rows // chunk,),
        [line, line, whole((8, width))]
        + [pl.BlockSpec((piece.shape[0], width), lambda i, order: (0, last)) for piece in mixed],
        [
            (line, array((rows, width), jnp.float32)),
            (line, array((rows, width))),
            (pl.BlockSpec((width, chunk), lambda i, order: (0, i)), array((width, rows))),
        ],
        (attended, tokens, cols, *mixed),
        "middle",
        2 * rows * width * width,
        scratch=[pltpu.VMEM((chunk, width), jnp.float32)],
    )


def feed(order, two, pair):
    rows, width = two.shape
    blocks = order.shape[0]
    hidden = (pair[0].shape[1] - width) // 2
    part = hidden // blocks
    count = len(pair)

    def body(order_ref, two_ref, *refs):
        gate_ref, up_ref, hidden_ref, flipped_ref = refs[count:]
        found = by_pieces(two_ref, refs[:count])
        gate, up = found[:, :part], found[:, part:]
        made = (gate / (1.0 + jnp.exp(-gate)) * up).astype(BF)
        gate_ref[...] = gate.astype(BF)
        up_ref[...] = up.astype(BF)
        hidden_ref[...] = made
        flipped_ref[...] = made.T

    tile = pl.BlockSpec((rows, part), lambda j, order: (0, j))
    shape = array((rows, hidden))
    return call(
        body,
        order,
        (blocks,),
        [whole((rows, width))]
        + [
            pl.BlockSpec((piece.shape[0], 2 * part), lambda j, order: (0, order[j]))
            for piece in pair
        ],
        [
            (tile, shape),
            (tile, shape),
            (tile, shape),
            (pl.BlockSpec((part, rows), lambda j, order: (j, 0)), array((hidden, rows))),
        ],
        (two, *pair),
        "feed",
        4 * rows * width * hidden,
        transcendentals=rows * hidden,
    )


def feed_back(order, upstream, gate, up, made, resid, pair, down):
    rows, width = upstream.shape
    blocks = order.shape[0]
    hidden = gate.shape[1]
    part = hidden // blocks
    count, downs = len(pair), len(down)
    each = blocks // downs

    def body(order_ref, m_ref, gate_ref, up_ref, made_ref, resid_ref, *refs):
        pairs, lows = refs[:count], refs[count : count + downs]
        out_ref, grads_ref, two_ref, total, result = refs[count + downs :]
        at = pl.program_id(0)

        @pl.when(at == 0)
        def _():
            total[...] = jnp.zeros_like(total)
            result[...] = resid_ref[...]

        def one(low):
            gate_all = gate_ref[...].astype(jnp.float32)
            up_all = up_ref[...].astype(jnp.float32)
            sigma = 1.0 / (1.0 + jnp.exp(-gate_all))
            made_grad = nt(m_ref[...], low[...])
            result[...] += jnp.dot(made_ref[...], low[...], preferred_element_type=jnp.float32)
            gate_grad = made_grad * up_all * sigma * (1.0 + gate_all * (1.0 - sigma))
            grads_ref[:, :part] = gate_grad.astype(BF)
            grads_ref[:, part:] = (made_grad * gate_all * sigma).astype(BF)

        for i in range(downs):

            @pl.when((at >= i * each) & (at < (i + 1) * each))
            def _(i=i):
                one(lows[i])

        grads = grads_ref[...]
        low = 0
        for piece in pairs:
            high = low + piece.shape[0]
            total[:, low:high] += nt(grads, piece[...])
            low = high

        @pl.when(at == blocks - 1)
        def _():
            out_ref[...] = result[...].astype(BF)
            collect(order_ref, total, two_ref)

    tile = pl.BlockSpec((rows, part), lambda j, order: (0, j))
    return call(
        body,
        order,
        (blocks,),
        [whole((rows, width)), tile, tile, tile, whole((rows, width))]
        + [
            pl.BlockSpec((piece.shape[0], 2 * part), lambda j, order: (0, order[j]))
            for piece in pair
        ]
        + [
            pl.BlockSpec(
                (part, width), lambda j, order, i=i: (jnp.clip(j - i * each, 0, each - 1), 0)
            )
            for i in range(downs)
        ],
        [
            (whole((rows, width)), array((rows, width))),
            (
                pl.BlockSpec((rows, 2 * part), lambda j, order: (0, order[j])),
                array((rows, 2 * hidden)),
            ),
            (whole((rows, width)), array((rows, width), jnp.float32)),
        ],
        (upstream, gate, up, made, resid, *pair, *down),
        "feed_back",
        8 * rows * width * hidden,
        scratch=[pltpu.VMEM((rows, width), jnp.float32), pltpu.VMEM((rows, width), jnp.float32)],
        transcendentals=rows * hidden,
    )


def norm_back(values, grads, gain):
    centre = values - jnp.mean(values, axis=-1, keepdims=True)
    scale = lax.rsqrt(jnp.mean(centre * centre, axis=-1, keepdims=True) + epsilon)
    normed = centre * scale
    scaled = grads * gain
    inner = jnp.mean(scaled * normed, axis=-1, keepdims=True)
    found = (scaled - jnp.mean(scaled, axis=-1, keepdims=True) - normed * inner) * scale
    return (
        found,
        jnp.sum(grads * normed, axis=0, keepdims=True),
        jnp.sum(grads, axis=0, keepdims=True),
    )


def middle_back(order, grads, resid, upstream, mixed, gain):
    rows, width = resid.shape
    count = len(mixed)
    last = mixed[0].shape[1] // width - 1
    chunk = math.gcd(rows, 256)

    def body(order_ref, grads_ref, resid_ref, m_ref, gain_ref, *refs):
        weights = refs[:count]
        y_ref, a_ref, go_ref, edge_ref = refs[count:]

        @pl.when(pl.program_id(0) == 0)
        def _():
            edge_ref[...] = jnp.zeros_like(edge_ref)

        found, gain_grad, shift_grad = norm_back(resid_ref[...], grads_ref[...], gain_ref[...])
        found = m_ref[...].astype(jnp.float32) + found
        edge_ref[0:1, :] += gain_grad
        edge_ref[1:2, :] += shift_grad
        y_ref[...] = found
        a_ref[...] = found.astype(BF)
        low = 0
        for weight in weights:
            high = low + weight.shape[0]
            go_ref[:, low:high] = nt(a_ref[...], weight[...]).astype(BF)
            low = high

    line = pl.BlockSpec((chunk, width), lambda i, order: (i, 0))
    return call(
        body,
        order,
        (rows // chunk,),
        [line, line, line, whole((1, width))]
        + [pl.BlockSpec((piece.shape[0], width), lambda i, order: (0, last)) for piece in mixed],
        [
            (line, array((rows, width), jnp.float32)),
            (line, array((rows, width))),
            (line, array((rows, width))),
            (whole((8, width)), array((8, width), jnp.float32)),
        ],
        (grads, resid, upstream, gain[None, :], *mixed),
        "middle_back",
        2 * rows * width * width,
    )


def pull(order, dq, both, mixed, block):
    rows, width = both.shape[0], both.shape[1] // 2
    tile = 512
    tiles = width // tile
    count = len(mixed)
    skip = 0 if block == 0 else tiles
    steps = 3 * tiles - skip
    dtype = BF if block else jnp.float32

    def body(order_ref, *refs):
        lefts = refs[: 1 if block else 2]
        weights = refs[len(lefts) : len(lefts) + count]
        out_ref, total = refs[len(lefts) + count :]
        at = pl.program_id(0)

        @pl.when(at == 0)
        def _():
            total[...] = jnp.zeros_like(total)

        def one(left):
            low = 0
            for weight in weights:
                high = low + weight.shape[0]
                total[:, low:high] += nt(left[...], weight[...])
                low = high

        if block:
            one(lefts[0])
        else:

            @pl.when(at < tiles)
            def _():
                one(lefts[0])

            @pl.when(at >= tiles)
            def _():
                one(lefts[1])

        @pl.when(at == steps - 1)
        def _():
            out_ref[...] = total[...].astype(dtype)

    lefts = [] if block else [pl.BlockSpec((rows, tile), lambda j, order: (0, jnp.minimum(j, tiles - 1)))]
    lefts.append(pl.BlockSpec((rows, tile), lambda j, order: (0, jnp.maximum(j + skip - tiles, 0))))
    return call(
        body,
        order,
        (steps,),
        lefts
        + [
            pl.BlockSpec((piece.shape[0], tile), lambda j, order: (0, j + skip)) for piece in mixed
        ],
        [(whole((rows, width)), array((rows, width), dtype))],
        ((both,) if block else (dq, both)) + tuple(mixed),
        f"pull{block}",
        rows * width,
        scratch=[pltpu.VMEM((rows, width), jnp.float32)],
    )[0]


def end_back(order, parts, tokens, grads, gain):
    rows, width = tokens.shape
    count = len(parts)
    chunk = math.gcd(rows, 256)

    def body(order_ref, x_ref, y_ref, gain_ref, *refs):
        sources = refs[:count]
        out_ref, edge_ref, held, total = refs[count:]

        @pl.when(pl.program_id(0) == 0)
        def _():
            edge_ref[...] = jnp.zeros_like(edge_ref)

        held[...] = sum(source[...].astype(jnp.float32) for source in sources)
        collect(order_ref, held, total)
        found, gain_grad, shift_grad = norm_back(
            x_ref[...].astype(jnp.float32), total[...], gain_ref[...]
        )
        edge_ref[0:1, :] += gain_grad
        edge_ref[1:2, :] += shift_grad
        out_ref[...] = (y_ref[...] + found).astype(BF)

    line = pl.BlockSpec((chunk, width), lambda i, order: (i, 0))
    return call(
        body,
        order,
        (rows // chunk,),
        [line, line, whole((1, width))] + [line] * count,
        [(line, array((rows, width))), (whole((8, width)), array((8, width), jnp.float32))],
        (tokens, grads, gain[None, :], *parts),
        "end_back",
        0,
        scratch=[pltpu.VMEM((chunk, width), jnp.float32), pltpu.VMEM((chunk, width), jnp.float32)],
    )


def join(first, second, part):
    rows, width = first.shape
    stacked = jnp.stack([first.reshape(rows, -1, part), second.reshape(rows, -1, part)], axis=2)
    return stacked.reshape(rows, 2 * width)


def part_ways(both, part):
    rows, width = both.shape
    cut = both.reshape(rows, -1, 2, part)
    return cut[:, :, 0].reshape(rows, width // 2), cut[:, :, 1].reshape(rows, width // 2)


def shards(
    plan,
    tokens,
    lengths,
    cotangent,
    query_weight,
    key_weight,
    value_weight,
    output_weight,
    gate_weight,
    up_weight,
    down_weight,
    attention_gain,
    attention_shift,
    feed_gain,
    feed_shift,
):
    slots = plan.slots()
    windows, local_len, width = tokens.shape
    rows = windows * local_len
    hidden = gate_weight.shape[1]
    place = lax.axis_index("ctx")
    exact = (width // plan.dp) % 128 == 0
    order = slots if exact else jnp.arange(8, dtype=jnp.int32)
    part = hidden // order.shape[0]

    def pieces_of(chain, shard):
        if exact:
            return chain.value
        return [assemble(slots, chain.value, shard.shape[0] * plan.ctx)]

    def in_slots(flipped):
        if exact:
            return flipped
        cut = flipped.reshape(plan.dp, -1, flipped.shape[1])
        return jnp.take(cut, slots, axis=0).reshape(flipped.shape)

    edge = jnp.stack([attention_gain, attention_shift, feed_gain, feed_shift], axis=1)
    edge = jnp.pad(edge, ((0, 0), (0, 124)))
    both = join(key_weight, value_weight, 128)
    mixed = jnp.concatenate([query_weight, both, edge], axis=1)
    mix = Chain(gather_steps(plan, mixed))

    seats = jnp.arange(local_len, dtype=jnp.int32)
    starts = jnp.asarray(plan.blocks)[place] * local_len
    valid = jnp.clip(lengths[0] - starts, 0, local_len)
    cosine, sine = rotary_tables((starts[:, None] + seats[None, :]).reshape(-1))
    real = (place * local_len + seats < lengths[0])[:, None]
    upstream = jnp.where(real, cotangent.reshape(rows, width), 0)
    own = tokens.reshape(rows, width)

    pair_own = jnp.concatenate([join(gate_weight, up_weight, part), output_weight], axis=1)
    early = (pair_own, cosine, sine, upstream)
    pair_own, cosine, sine, upstream = step(early, mix)
    pair = Chain(gather_steps(plan, pair_own, line=True))
    own = step(own, mix, pair)
    own = step(own, mix, pair)
    came = {}
    own, window = begin(own, window_steps(plan, own, came))
    own = finish(own, mix)
    mixed_w = pieces_of(mix, mixed)
    back = jnp.asarray(plan.back)[lax.axis_index("dp")] if exact else order

    flipped, both = {}, {}
    cols = None
    flipped[0], queries, both[0], cols = project(order, own, cols, mixed_w, cosine, sine, 0)
    both[0] = step(both[0], pair)
    state = attend(order, valid, 0, None, plan.ctx == 1, queries, both[0])
    down = None
    for k in range(1, plan.ctx):
        while k not in came:
            state = step(state, window)
        if k == min(3, plan.ctx - 1):
            down_own, state = tie(down_weight, state)
            down = Chain(gather_steps(plan, down_own))
        flipped[k], both[k] = project(order, came[k], cols, mixed_w, cosine, sine, k)
        if k == 1:
            both[k] = step(both[k], pair)
        state = attend(order, valid, k, state, k == plan.ctx - 1, queries, both[k])
    state = step(state, pair, down)
    state = finish(state, pair)
    pair_w = pieces_of(pair, pair_own)
    natural = cols[:4].reshape(4, order.shape[0], -1)[:, back].reshape(4, width)
    low, low_flipped, attended, lse = state
    resid, two, two_flipped = middle(order, low, pair_w, own, cols)
    two = step(two, down)
    gate, up, made, made_flipped = feed(order, two, pair_w)
    product = product_of(plan, [[(in_slots(made_flipped), upstream)]])
    first = product(plan.dp // 2, plan.dp)
    made, first = finish((made, first), down)
    made, down_sum = begin(made, sum_steps(plan, product, first))
    down_w = pieces_of(down, down_weight)
    output, pair_grads, two_grads = feed_back(
        order, upstream, gate, up, made, resid, pair_w, down_w
    )
    output = output.reshape(windows, local_len, width)

    two_grads, pair_grads = step((two_grads, pair_grads), down_sum)
    two_grads, pair_sum = begin(
        two_grads, sum_steps(plan, product_of(plan, [[(in_slots(two_flipped), pair_grads)]]))
    )
    y_grads, low_grads, go, edge_two = middle_back(
        order, two_grads, resid, upstream, pair_w, natural[2]
    )
    go = step(go, pair_sum)
    go, output_sum = begin(
        go, sum_steps(plan, product_of(plan, [[(in_slots(low_flipped), low_grads)]]))
    )
    held, back_way = None, None
    grads, parts = {}, {}
    flipped = {k: in_slots(flipped[k]) for k in flipped}
    for k in reversed(range(plan.ctx)):
        held, grads[k] = attend_back(
            order, valid, k, held, k == 0, queries, both[k], go, attended, lse, cosine, sine
        )
        if k:
            if k == plan.ctx - 1:
                held = step(held, down_sum, output_sum)
            else:
                if plan.line:
                    held = wait(held, back_way)
                held = step(held, pair_sum)
            held, grads[k] = tie(held, grads[k])
            parts[k] = pull(order, held, grads[k], mixed_w, k)
            held, parts[k] = tie(held, parts[k])
            if plan.line:
                if back_way is None:
                    held, back_way = begin(held, return_steps(plan, parts))
                else:
                    held = go_on(held, back_way)
            if k < plan.ctx - 1:
                held = step(held, down_sum, output_sum)
    finals = [down_sum, output_sum, pair_sum]
    held = wait(held, *finals)
    groups = [[(flipped[0], held)], [(flipped[k], grads[k]) for k in range(plan.ctx)]]
    held, last_sum = begin(held, sum_steps(plan, product_of(plan, groups)))
    held = go_on(held, down_sum, output_sum)
    held = step(held, last_sum)
    part_grads = pull(order, held, grads[0], mixed_w, 0)
    if plan.line:
        part_grads = finish(part_grads, back_way)
        sends = back_way.value
    else:
        sends = [lax.ppermute(parts[k], AXES, plan.across[k]) for k in range(1, plan.ctx)]
    tokens_grad, edge_one = end_back(
        order, [part_grads, *sends], own, y_grads, natural[0]
    )
    edge_one = step(edge_one, last_sum)
    edge_one = go_on(edge_one, pair_sum)
    vectors = sum_vectors(plan, (edge_one[0], edge_one[1], edge_two[0], edge_two[1]))
    finish((), last_sum)
    finish((), down_sum, output_sum, pair_sum)
    gate_grad, up_grad = part_ways(pair_sum.value, part)
    key_grad, value_grad = part_ways(last_sum.value[:, width:], 128)
    return (
        output,
        tokens_grad.reshape(windows, local_len, width),
        last_sum.value[:, :width],
        key_grad,
        value_grad,
        output_sum.value,
        gate_grad,
        up_grad,
        down_sum.value,
        *vectors,
    )


def solution(mesh):
    return jax.shard_map(
        functools.partial(shards, Plan(mesh)),
        mesh=mesh,
        in_specs=(
            P("dp", "ctx", None),
            P("dp"),
            P("dp", "ctx", None),
            P(("dp", "ctx"), None),
            P(("dp", "ctx"), None),
            P(("dp", "ctx"), None),
            P(("dp", "ctx"), None),
            P(("dp", "ctx"), None),
            P(("dp", "ctx"), None),
            P(("dp", "ctx"), None),
            P(("dp", "ctx")),
            P(("dp", "ctx")),
            P(("dp", "ctx")),
            P(("dp", "ctx")),
        ),
        out_specs=(
            P("dp", "ctx", None),
            P("dp", "ctx", None),
            P(("dp", "ctx"), None),
            P(("dp", "ctx"), None),
            P(("dp", "ctx"), None),
            P(("dp", "ctx"), None),
            P(("dp", "ctx"), None),
            P(("dp", "ctx"), None),
            P(("dp", "ctx"), None),
            P(("dp", "ctx")),
            P(("dp", "ctx")),
            P(("dp", "ctx")),
            P(("dp", "ctx")),
        ),
        check_vma=False,
    )
```

```python
import functools
import math

import numpy as np

import jax
import jax.numpy as jnp
from jax import lax
from jax.experimental import pallas as pl
from jax.experimental.pallas import tpu as pltpu
from jax.sharding import PartitionSpec as P

H = 16
HD = 64
L = 2048


epsilon = 1e-05
masked_score = -1e30


def layer_norm(values, gain, shift):
    centre = values - jnp.mean(values, axis=-1, keepdims=True)
    spread = jnp.mean(centre * centre, axis=-1, keepdims=True)
    return centre * lax.rsqrt(spread + epsilon) * gain + shift


def rotary_tables(positions):
    half = HD // 2
    turns = jnp.arange(2 * HD, dtype=jnp.int32) % half
    freqs = jnp.exp(turns.astype(jnp.float32) * (-2.0 * math.log(10000.0) / HD))
    angles = positions.astype(jnp.float32)[:, None] * freqs[None, :]
    return (jnp.cos(angles), jnp.sin(angles))


AXES = ("dp", "ctx")
BF = jnp.bfloat16


class Plan:
    def __init__(self, mesh):
        self.dp, self.ctx = mesh.shape["dp"], mesh.shape["ctx"]
        self.stages = self.dp.bit_length() - 2
        self.ctx_bits = self.ctx.bit_length() - 1
        orders = (list(range(1, self.stages + 1)), list(range(self.stages, 0, -1)))
        self.core = self.pairs(lambda d, z: (d ^ 1, z))
        self.stage = [
            self.pairs(lambda d, z, t=t: (d ^ (1 << orders[d & 1][t]), z)) for t in range(self.stages)
        ]
        self.across = [self.pairs(lambda d, z, k=k: (d, z ^ k)) for k in range(self.ctx)]
        self.line = self.ctx == 4
        self.inner = self.pairs(lambda d, z: (d, z ^ 3), (1, 2))
        self.outward = self.pairs(lambda d, z: (d, z ^ 1), (1, 2))
        self.inward = self.pairs(lambda d, z: (d, z ^ 1), (0, 3))
        self.blocks = np.arange(self.ctx)[:, None] ^ np.arange(self.ctx)[None, :]
        if self.line:
            self.blocks = np.array([[0, 1, 2, 3], [1, 0, 2, 3], [2, 3, 1, 0], [3, 2, 1, 0]])
        self.blocks = self.blocks.astype(np.int32)
        half = self.dp // 2
        table = np.zeros((self.dp, self.dp), np.int32)
        for d in range(self.dp):
            for j in range(self.dp):
                owner = d ^ 1 if j >= half else d
                block = owner
                for t in range(self.stages):
                    if (j % half) >> (self.stages - 1 - t) & 1:
                        block ^= 1 << orders[owner & 1][t]
                table[d, j] = block
        self.table = table
        self.back = np.argsort(table, axis=1).astype(np.int32)

    def pairs(self, target, places=None):
        found = []
        for d in range(self.dp):
            for z in range(self.ctx) if places is None else places:
                other, place = target(d, z)
                found.append((d * self.ctx + z, other * self.ctx + place))
        return found

    def slots(self):
        return jnp.asarray(self.table)[lax.axis_index("dp")]


def assemble(slots, pieces, rows):
    blocks = slots.shape[0]
    width = pieces[0].shape[1]
    sizes = [piece.shape[0] // rows for piece in pieces]
    starts = [sum(sizes[:i]) for i in range(len(sizes))]

    def body(order, *refs):
        slot = pl.program_id(0)
        out = refs[-1]
        for piece, start, size in zip(refs, starts, sizes):

            @pl.when((slot >= start) & (slot < start + size))
            def _(piece=piece):
                out[...] = piece[...]

    specs = [
        pl.BlockSpec(
            (rows, width),
            lambda j, order, start=start, size=size: (jnp.clip(j - start, 0, size - 1), 0),
        )
        for start, size in zip(starts, sizes)
    ]
    return pl.pallas_call(
        body,
        out_shape=jax.ShapeDtypeStruct((blocks * rows, width), pieces[0].dtype),
        grid_spec=pltpu.PrefetchScalarGridSpec(
            num_scalar_prefetch=1,
            grid=(blocks,),
            in_specs=specs,
            out_specs=pl.BlockSpec((rows, width), lambda j, order: (order[j], 0)),
        ),
        name="assemble",
    )(slots, *pieces)


def tie(values, others):
    leaves, tree = jax.tree.flatten((values, others))
    return jax.tree.unflatten(tree, lax.optimization_barrier(leaves))


class Chain:
    def __init__(self, steps):
        self.steps = steps
        self.flying, self.sent = next(steps)
        self.done = False
        self.value = None

    def land(self, came):
        if self.done:
            return
        try:
            self.flying, self.sent = self.steps.send(came)
        except StopIteration as stop:
            self.flying, self.sent, self.done, self.value = [], [], True, stop.value


def step(main, *chains):
    main, came = tie(main, [chain.flying for chain in chains])
    for chain, arrays in zip(chains, came):
        chain.land(arrays)
    return tie(main, [chain.sent for chain in chains])[0]


def wait(main, *chains):
    main, came = tie(main, [chain.flying for chain in chains])
    for chain, arrays in zip(chains, came):
        chain.came = arrays
    return main


def go_on(main, *chains):
    main, came = tie(main, [chain.came for chain in chains])
    for chain, arrays in zip(chains, came):
        chain.land(arrays)
    return tie(main, [chain.sent for chain in chains])[0]


def begin(main, steps):
    chain = Chain(steps)
    return tie(main, chain.sent)[0], chain


def finish(main, *chains):
    while not all(chain.done for chain in chains):
        main = step(main, *chains)
    return main


def gather_steps(plan, shard, line=False):
    place = lax.axis_index("ctx")
    if line and plan.line:
        near, middle = yield (
            [lax.ppermute(shard, AXES, plan.across[1]), lax.ppermute(shard, AXES, plan.inner)],
            [shard],
        )
        far, cross = yield (
            [lax.ppermute(middle, AXES, plan.outward), lax.ppermute(near, AXES, plan.inner)],
            [middle, near],
        )
        (last,) = yield [lax.ppermute(cross, AXES, plan.outward)], [cross]
        two, three = middle + far, cross + last
        upper = place >= 2
        blocks = [shard, near, jnp.where(upper, three, two), jnp.where(upper, two, three)]
        odd = place % 2 == 1
        run = jnp.where(
            upper,
            jnp.concatenate(blocks[2:] + [jnp.where(odd, near, shard), jnp.where(odd, shard, near)]),
            jnp.concatenate([jnp.where(odd, near, shard), jnp.where(odd, shard, near)] + blocks[2:]),
        )
    else:
        blocks = yield (
            [lax.ppermute(shard, AXES, plan.across[k]) for k in range(1, plan.ctx)],
            [shard],
        )
        blocks = [shard, *blocks]
        for bit in range(plan.ctx_bits):
            upper = (place >> bit) & 1 == 1
            blocks = [
                jnp.where(upper, jnp.concatenate([b, a]), jnp.concatenate([a, b]))
                for a, b in zip(blocks[::2], blocks[1::2])
            ]
        run = blocks[0]
    *early, final = reversed(plan.stage)
    for pairs in early:
        (other,) = yield [lax.ppermute(run, AXES, pairs)], [run]
        run = jnp.concatenate([run, other])
    other, far = yield [lax.ppermute(run, AXES, final), lax.ppermute(run, AXES, plan.core)], [run]
    (last,) = yield [lax.ppermute(other, AXES, plan.core)], [other]
    return [run, other, far, last]


def add(a, b):
    return (a.astype(jnp.float32) + b.astype(jnp.float32)).astype(BF)


def window_steps(plan, own, came):
    if not plan.line:
        others = yield [lax.ppermute(own, AXES, plan.across[k]) for k in range(1, plan.ctx)], [own]
        came.update(enumerate(others, 1))
        return
    near, middle = yield (
        [lax.ppermute(own, AXES, plan.across[1]), lax.ppermute(own, AXES, plan.inner)],
        [own],
    )
    came[1] = near
    far, cross = yield (
        [lax.ppermute(middle, AXES, plan.outward), lax.ppermute(near, AXES, plan.inner)],
        [middle, near],
    )
    came[2] = middle + far
    (last,) = yield [lax.ppermute(cross, AXES, plan.outward)], [cross]
    came[3] = cross + last


def return_steps(plan, parts):
    (came,) = yield [lax.ppermute(parts[3], AXES, plan.inward)], [parts[3]]
    run = add(parts[3], came)
    near, cross = yield (
        [lax.ppermute(parts[2], AXES, plan.inward), lax.ppermute(run, AXES, plan.inner)],
        [parts[2], run],
    )
    run, last = add(parts[2], near), add(parts[1], cross)
    return (
        yield (
            [
                lax.ppermute(run, AXES, plan.inner),
                lax.ppermute(last, AXES, plan.across[1]),
            ],
            [run, last],
        )
    )


def sum_steps(plan, product, send=None):
    place = lax.axis_index("ctx")
    half = plan.dp // 2

    if send is None:
        send = product(half, plan.dp)
    (other,) = yield [lax.ppermute(send, AXES, plan.core)], [send]
    rows = other.shape[0] // half
    size = half // 2
    send = product(size, half, other[size * rows :])
    flying = [lax.ppermute(send, AXES, plan.stage[0])]
    keep = product(0, size, other[: size * rows])
    (other,) = yield flying, [send, keep]
    held = add(keep, other)
    for pairs in plan.stage[1:]:
        size //= 2
        send = held[size * rows :]
        (other,) = yield [lax.ppermute(send, AXES, pairs)], [send]
        held = add(held[: size * rows], other)
    width = held.shape[1]
    for bit in range(plan.ctx_bits):
        left = 1 << (plan.ctx_bits - bit - 1)
        lower = (place >> bit) & 1
        cut = held.reshape(left, 2, -1, width)
        send = lax.dynamic_index_in_dim(cut, 1 - lower, 1, False).reshape(-1, width)
        keep = lax.dynamic_index_in_dim(cut, lower, 1, False).reshape(-1, width)
        (other,) = yield [lax.ppermute(send, AXES, plan.across[1 << bit])], [send]
        if left > 1:
            held = add(keep, other)
        else:
            held = keep.astype(jnp.float32) + other.astype(jnp.float32)
    return held


def sum_vectors(plan, vectors):
    count = plan.dp * plan.ctx
    packed = jnp.stack(vectors).reshape(len(vectors), count, -1).transpose(1, 0, 2)
    part = packed.shape[2]
    packed = packed.reshape(count, len(vectors) * part)
    came = lax.all_to_all(packed, AXES, split_axis=0, concat_axis=0, tiled=True)
    whole = jnp.sum(came, axis=0)
    return [whole[i * part : (i + 1) * part] for i in range(len(vectors))]


def nt(a, b):
    return lax.dot_general(a, b, (((1,), (1,)), ((), ())), preferred_element_type=jnp.float32)


def turn(values, cosine, sine):
    lane = lax.broadcasted_iota(jnp.int32, values.shape, 1)
    ahead = pltpu.roll(values, 128 - HD // 2, 1)
    behind = pltpu.roll(values, HD // 2, 1)
    turned = jnp.where(lane % HD < HD // 2, -ahead, behind)
    return values * cosine + turned * sine


def head_parts(values):
    lane = lax.broadcasted_iota(jnp.int32, values.shape, 1)
    zero = jnp.zeros_like(values)
    return [jnp.where(lane < HD, values, zero), jnp.where(lane < HD, zero, values)]


def product_of(plan, groups):
    def product(start, end, more=None):
        columns = []
        low = 0
        for terms in groups:
            found = 0.0
            for flipped, right in terms:
                rows = flipped.shape[0] // plan.dp
                part = flipped[start * rows : end * rows]
                found = found + jnp.dot(part, right, preferred_element_type=jnp.float32)
            high = low + found.shape[1]
            if more is not None:
                found = found + more[:, low:high].astype(jnp.float32)
            columns.append(found.astype(BF))
            low = high
        return columns[0] if len(columns) == 1 else jnp.concatenate(columns, axis=1)

    return product


def whole(shape):
    return pl.BlockSpec(shape, lambda *at: (0,) * len(shape))


def call(body, order, grid, ins, outs, operands, name, flops, scratch=(), transcendentals=0):
    size = lambda a: math.prod(a.shape) * jnp.dtype(a.dtype).itemsize
    out_shape = [shape for spec, shape in outs]
    return pl.pallas_call(
        body,
        out_shape=out_shape,
        grid_spec=pltpu.PrefetchScalarGridSpec(
            num_scalar_prefetch=1,
            grid=grid,
            in_specs=ins,
            out_specs=[spec for spec, shape in outs],
            scratch_shapes=list(scratch),
        ),
        cost_estimate=pl.CostEstimate(
            flops=flops,
            bytes_accessed=sum(size(a) for a in [*operands, *out_shape]),
            transcendentals=transcendentals,
        ),
        name=name,
    )(order, *operands)


def array(shape, dtype=BF):
    return jax.ShapeDtypeStruct(shape, dtype)


def spread(order, source, target, rows):
    blocks = order.shape[0]
    part = source.shape[1] // blocks
    for j in range(blocks):
        at = pl.multiple_of(order[j] * part, 128)
        target[rows, j * part : (j + 1) * part] = source[rows, pl.ds(at, part)].astype(target.dtype)


def collect(order, source, target):
    blocks = order.shape[0]
    part = source.shape[1] // blocks
    for j in range(blocks):
        at = pl.multiple_of(order[j] * part, 128)
        target[:, pl.ds(at, part)] = source[:, j * part : (j + 1) * part].astype(target.dtype)


def by_pieces(left, pieces):
    found, low = 0.0, 0
    for piece in pieces:
        high = low + piece.shape[0]
        found = found + jnp.dot(left[:, low:high], piece[...], preferred_element_type=jnp.float32)
        low = high
    return found


def project(order, source, cols, mixed, cosine, sine, block):
    rows, width = source.shape
    tile = 512
    tiles = width // tile
    skip = 0 if block == 0 else tiles
    count = len(mixed)
    scale = 1.0 / math.sqrt(HD)

    def body(order_ref, source_ref, cos_ref, sin_ref, *refs):
        weights, edges = refs[:count], refs[count : -1 - found_outs]
        outs, normed = refs[-1 - found_outs : -1], refs[-1]
        cols_ref = outs[-1] if block == 0 else edges[0]
        at = pl.program_id(0) + skip

        @pl.when(at == skip)
        def _():
            if block == 0:
                low = 0
                for edge in edges:
                    high = low + edge.shape[0]
                    cols_ref[:, low:high] = edge[...].astype(jnp.float32).T[:8]
                    low = high
            spread(order_ref, source_ref, normed, slice(None))
            chunk = math.gcd(rows, 128)

            def one(i, unused):
                here = pl.ds(pl.multiple_of(i * chunk, chunk), chunk)
                found = normed[here, :].astype(jnp.float32)
                normed[here, :] = layer_norm(found, cols_ref[0:1, :], cols_ref[1:2, :]).astype(BF)
                return unused

            lax.fori_loop(0, rows // chunk, one, 0)
            outs[0][...] = normed[...].T

        found = by_pieces(normed, weights)

        def turned(c):
            return turn(found[:, c : c + 128], cos_ref[...], sin_ref[...]).astype(BF)

        if block == 0:

            @pl.when(at < tiles)
            def _():
                for c in range(0, tile, 128):
                    outs[1][:, c : c + 128] = (turned(c).astype(jnp.float32) * scale).astype(BF)

        @pl.when(at >= tiles)
        def _():
            both_ref = outs[2] if block == 0 else outs[1]
            for c in range(0, tile, 256):
                both_ref[:, c : c + 128] = turned(c)
                both_ref[:, c + 128 : c + 256] = found[:, c + 128 : c + 256].astype(BF)

    table = pl.BlockSpec((rows, 128), lambda j, order: (block, 0))
    outs = [(whole((width, rows)), array((width, rows)))]
    if block == 0:
        outs.append(
            (
                pl.BlockSpec((rows, tile), lambda j, order: (0, jnp.minimum(j, tiles - 1))),
                array((rows, width)),
            )
        )
    outs.append(
        (
            pl.BlockSpec((rows, tile), lambda j, order: (0, jnp.maximum(j + skip - tiles, 0))),
            array((rows, 2 * width)),
        )
    )
    if block == 0:
        outs.append((whole((8, width)), array((8, width), jnp.float32)))
        edges = [
            pl.BlockSpec((piece.shape[0], 128), lambda j, order: (0, 3 * width // 128))
            for piece in mixed
        ]
    else:
        edges = [whole((8, width))]
    found_outs = len(outs)
    return call(
        body,
        order,
        (3 * tiles - skip,),
        [whole((rows, width)), table, table]
        + [
            pl.BlockSpec((piece.shape[0], tile), lambda j, order: (0, j + skip)) for piece in mixed
        ]
        + edges,
        outs,
        (source, cosine, sine, *mixed, *(mixed if block == 0 else [cols])),
        f"project{block}",
        32 * rows * width * width * (2 if block else 3),
        scratch=[pltpu.VMEM((rows, width), BF)],
    )


def attend(order, valid, block, state, last, queries, both):
    rows, width = queries.shape
    pairs = width // 128
    first = state is None

    def body(order_ref, valid_ref, q_ref, kv_ref, *refs):
        outs = refs if first else refs[2:]
        parts = head_parts(q_ref[...])
        keys = kv_ref[:, :128]
        flipped = kv_ref[:, 128:].T
        tops, masses, sums = [], [], []
        for head in range(2):
            scores = nt(keys, parts[head])
            seat = lax.broadcasted_iota(jnp.int32, scores.shape, 0)
            scores = jnp.where(seat < valid_ref[block], scores, masked_score)
            top = jnp.max(scores, axis=0, keepdims=True)
            if not first:
                top = jnp.maximum(top, refs[0][0, head : head + 1, :])
            expo = jnp.exp(scores - top)
            mass = jnp.sum(expo, axis=0, keepdims=True)
            held = jnp.dot(
                flipped[head * HD : (head + 1) * HD, :],
                expo.astype(BF),
                preferred_element_type=jnp.float32,
            )
            if not first:
                factor = jnp.exp(refs[0][0, head : head + 1, :] - top)
                mass = mass + refs[0][0, head + 2 : head + 3, :] * factor
                held = held + refs[1][head * HD : (head + 1) * HD, :] * factor
            tops.append(top)
            masses.append(mass)
            sums.append(held)
        blank = jnp.zeros((4, rows), jnp.float32)
        if last:
            found = jnp.concatenate([s / m for s, m in zip(sums, masses)], axis=0)
            outs[1][...] = found.astype(BF)
            found = found.T
            outs[0][...] = found.astype(BF)
            outs[2][...] = found
            lse = [t + jnp.log(m) for t, m in zip(tops, masses)]
            outs[3][...] = jnp.concatenate(lse + masses + [blank], axis=0)[None]
        else:
            outs[0][...] = jnp.concatenate(tops + masses + [blank], axis=0)[None]
            outs[1][...] = jnp.concatenate(sums, axis=0)

    column = pl.BlockSpec((rows, 128), lambda j, order: (0, j))
    stats = pl.BlockSpec((1, 8, rows), lambda j, order: (j, 0, 0))
    carried = pl.BlockSpec((128, rows), lambda j, order: (j, 0))
    stats_shape = array((pairs, 8, rows), jnp.float32)
    if last:
        outs = [
            (column, array((rows, width))),
            (carried, array((width, rows))),
            (column, array((rows, width), jnp.float32)),
            (stats, stats_shape),
        ]
    else:
        outs = [(stats, stats_shape), (carried, array((width, rows), jnp.float32))]
    return call(
        body,
        order,
        (pairs,),
        [
            pl.BlockSpec(memory_space=pltpu.SMEM),
            pl.BlockSpec((rows, 128), lambda j, order: (0, order[j])),
            pl.BlockSpec((rows, 256), lambda j, order: (0, order[j])),
        ]
        + ([] if first else [stats, carried]),
        outs,
        (valid, queries, both, *(() if first else state)),
        f"attend{block}",
        256 * rows * rows * width,
        transcendentals=16 * rows * rows,
    )


def attend_back(order, valid, block, held, last, queries, both, go, attended, lse, cosine, sine):
    rows, width = queries.shape
    pairs = width // 128
    scale = 1.0 / math.sqrt(HD)
    first = held is None

    def body(order_ref, valid_ref, q_ref, kv_ref, go_ref, o_ref, lse_ref, cos_ref, sin_ref, *refs):
        dq_ref, dkv_ref = refs[-2:]
        keys = kv_ref[:, :128]
        values = kv_ref[:, 128:]
        go_all = go_ref[...]
        q_parts = head_parts(q_ref[...])
        go_parts = head_parts(go_all)
        crossed = (go_all.astype(jnp.float32) * o_ref[...]).T
        flipped = keys.T
        dk = jnp.zeros((rows, 128), jnp.float32)
        dv = jnp.zeros((rows, 128), jnp.float32)
        dq = []
        for head in range(2):
            delta = jnp.sum(crossed[head * HD : (head + 1) * HD, :], axis=0, keepdims=True)
            scores = nt(keys, q_parts[head])
            seat = lax.broadcasted_iota(jnp.int32, scores.shape, 0)
            scores = jnp.where(seat < valid_ref[block], scores, masked_score)
            probs = jnp.exp(scores - lse_ref[0, head : head + 1, :])
            grad_probs = nt(values, go_parts[head])
            grad_scores = (probs * (grad_probs - delta)).astype(BF)
            dv = dv + jnp.dot(probs.astype(BF), go_parts[head], preferred_element_type=jnp.float32)
            dk = dk + jnp.dot(grad_scores, q_parts[head], preferred_element_type=jnp.float32)
            dq.append(
                jnp.dot(
                    flipped[head * HD : (head + 1) * HD, :],
                    grad_scores,
                    preferred_element_type=jnp.float32,
                )
            )
        dkv_ref[:, :128] = turn(dk, cos_ref[...], -sin_ref[...]).astype(BF)
        dkv_ref[:, 128:] = dv.astype(BF)
        found = jnp.concatenate(dq, axis=0)
        if not first:
            found = found + refs[0][...]
        if last:
            dq_ref[...] = turn(found.T * scale, cos_ref[...], -sin_ref[...]).astype(BF)
        else:
            dq_ref[...] = found

    column = pl.BlockSpec((rows, 128), lambda j, order: (0, j))
    natural = pl.BlockSpec((rows, 128), lambda j, order: (0, order[j]))
    natural_both = pl.BlockSpec((rows, 256), lambda j, order: (0, order[j]))
    carried = pl.BlockSpec((128, rows), lambda j, order: (j, 0))
    table = pl.BlockSpec((rows, 128), lambda j, order: (block, 0))
    return call(
        body,
        order,
        (pairs,),
        [
            pl.BlockSpec(memory_space=pltpu.SMEM),
            natural,
            natural_both,
            column,
            column,
            pl.BlockSpec((1, 8, rows), lambda j, order: (j, 0, 0)),
            table,
            table,
        ]
        + ([] if first else [carried]),
        [
            (natural, array((rows, width))) if last else (carried, array((width, rows), jnp.float32)),
            (natural_both, array((rows, 2 * width))),
        ],
        (valid, queries, both, go, attended, lse, cosine, sine, *(() if first else (held,))),
        f"attend_back{block}",
        40 * rows * rows * width,
        transcendentals=16 * rows * rows,
    )


def middle(order, attended, mixed, tokens, cols):
    rows, width = tokens.shape
    count = len(mixed)
    last = mixed[0].shape[1] // width - 1
    chunk = math.gcd(rows, 256)

    def body(order_ref, o_ref, x_ref, cols_ref, *refs):
        weights = refs[:count]
        resid_ref, two_ref, flipped_ref, held = refs[count:]
        found = x_ref[...].astype(jnp.float32) + by_pieces(o_ref, weights)
        resid_ref[...] = found
        spread(order_ref, resid_ref, held, slice(None))
        two = layer_norm(held[...], cols_ref[2:3, :], cols_ref[3:4, :]).astype(BF)
        two_ref[...] = two
        flipped_ref[...] = two.T

    line = pl.BlockSpec((chunk, width), lambda i, order: (i, 0))
    return call(
        body,
        order,
        (rows // chunk,),
        [line, line, whole((8, width))]
        + [pl.BlockSpec((piece.shape[0], width), lambda i, order: (0, last)) for piece in mixed],
        [
            (line, array((rows, width), jnp.float32)),
            (line, array((rows, width))),
            (pl.BlockSpec((width, chunk), lambda i, order: (0, i)), array((width, rows))),
        ],
        (attended, tokens, cols, *mixed),
        "middle",
        2 * rows * width * width,
        scratch=[pltpu.VMEM((chunk, width), jnp.float32)],
    )


def feed(order, two, pair):
    rows, width = two.shape
    blocks = order.shape[0]
    hidden = (pair[0].shape[1] - width) // 2
    part = hidden // blocks
    count = len(pair)

    def body(order_ref, two_ref, *refs):
        gate_ref, up_ref, hidden_ref, flipped_ref = refs[count:]
        found = by_pieces(two_ref, refs[:count])
        gate, up = found[:, :part], found[:, part:]
        made = (gate / (1.0 + jnp.exp(-gate)) * up).astype(BF)
        gate_ref[...] = gate.astype(BF)
        up_ref[...] = up.astype(BF)
        hidden_ref[...] = made
        flipped_ref[...] = made.T

    tile = pl.BlockSpec((rows, part), lambda j, order: (0, j))
    shape = array((rows, hidden))
    return call(
        body,
        order,
        (blocks,),
        [whole((rows, width))]
        + [
            pl.BlockSpec((piece.shape[0], 2 * part), lambda j, order: (0, order[j]))
            for piece in pair
        ],
        [
            (tile, shape),
            (tile, shape),
            (tile, shape),
            (pl.BlockSpec((part, rows), lambda j, order: (j, 0)), array((hidden, rows))),
        ],
        (two, *pair),
        "feed",
        4 * rows * width * hidden,
        transcendentals=rows * hidden,
    )


def feed_back(order, upstream, gate, up, made, resid, pair, down):
    rows, width = upstream.shape
    blocks = order.shape[0]
    hidden = gate.shape[1]
    part = hidden // blocks
    count, downs = len(pair), len(down)
    each = blocks // downs

    def body(order_ref, m_ref, gate_ref, up_ref, made_ref, resid_ref, *refs):
        pairs, lows = refs[:count], refs[count : count + downs]
        out_ref, grads_ref, two_ref, total, result = refs[count + downs :]
        at = pl.program_id(0)

        @pl.when(at == 0)
        def _():
            total[...] = jnp.zeros_like(total)
            result[...] = resid_ref[...]

        def one(low):
            gate_all = gate_ref[...].astype(jnp.float32)
            up_all = up_ref[...].astype(jnp.float32)
            sigma = 1.0 / (1.0 + jnp.exp(-gate_all))
            made_grad = nt(m_ref[...], low[...])
            result[...] += jnp.dot(made_ref[...], low[...], preferred_element_type=jnp.float32)
            gate_grad = made_grad * up_all * sigma * (1.0 + gate_all * (1.0 - sigma))
            grads_ref[:, :part] = gate_grad.astype(BF)
            grads_ref[:, part:] = (made_grad * gate_all * sigma).astype(BF)

        for i in range(downs):

            @pl.when((at >= i * each) & (at < (i + 1) * each))
            def _(i=i):
                one(lows[i])

        grads = grads_ref[...]
        low = 0
        for piece in pairs:
            high = low + piece.shape[0]
            total[:, low:high] += nt(grads, piece[...])
            low = high

        @pl.when(at == blocks - 1)
        def _():
            out_ref[...] = result[...].astype(BF)
            collect(order_ref, total, two_ref)

    tile = pl.BlockSpec((rows, part), lambda j, order: (0, j))
    return call(
        body,
        order,
        (blocks,),
        [whole((rows, width)), tile, tile, tile, whole((rows, width))]
        + [
            pl.BlockSpec((piece.shape[0], 2 * part), lambda j, order: (0, order[j]))
            for piece in pair
        ]
        + [
            pl.BlockSpec(
                (part, width), lambda j, order, i=i: (jnp.clip(j - i * each, 0, each - 1), 0)
            )
            for i in range(downs)
        ],
        [
            (whole((rows, width)), array((rows, width))),
            (
                pl.BlockSpec((rows, 2 * part), lambda j, order: (0, order[j])),
                array((rows, 2 * hidden)),
            ),
            (whole((rows, width)), array((rows, width), jnp.float32)),
        ],
        (upstream, gate, up, made, resid, *pair, *down),
        "feed_back",
        8 * rows * width * hidden,
        scratch=[pltpu.VMEM((rows, width), jnp.float32), pltpu.VMEM((rows, width), jnp.float32)],
        transcendentals=rows * hidden,
    )


def norm_back(values, grads, gain):
    centre = values - jnp.mean(values, axis=-1, keepdims=True)
    scale = lax.rsqrt(jnp.mean(centre * centre, axis=-1, keepdims=True) + epsilon)
    normed = centre * scale
    scaled = grads * gain
    inner = jnp.mean(scaled * normed, axis=-1, keepdims=True)
    found = (scaled - jnp.mean(scaled, axis=-1, keepdims=True) - normed * inner) * scale
    return (
        found,
        jnp.sum(grads * normed, axis=0, keepdims=True),
        jnp.sum(grads, axis=0, keepdims=True),
    )


def middle_back(order, grads, resid, upstream, mixed, gain):
    rows, width = resid.shape
    count = len(mixed)
    last = mixed[0].shape[1] // width - 1
    chunk = math.gcd(rows, 256)

    def body(order_ref, grads_ref, resid_ref, m_ref, gain_ref, *refs):
        weights = refs[:count]
        y_ref, a_ref, go_ref, edge_ref = refs[count:]

        @pl.when(pl.program_id(0) == 0)
        def _():
            edge_ref[...] = jnp.zeros_like(edge_ref)

        found, gain_grad, shift_grad = norm_back(resid_ref[...], grads_ref[...], gain_ref[...])
        found = m_ref[...].astype(jnp.float32) + found
        edge_ref[0:1, :] += gain_grad
        edge_ref[1:2, :] += shift_grad
        y_ref[...] = found
        a_ref[...] = found.astype(BF)
        low = 0
        for weight in weights:
            high = low + weight.shape[0]
            go_ref[:, low:high] = nt(a_ref[...], weight[...]).astype(BF)
            low = high

    line = pl.BlockSpec((chunk, width), lambda i, order: (i, 0))
    return call(
        body,
        order,
        (rows // chunk,),
        [line, line, line, whole((1, width))]
        + [pl.BlockSpec((piece.shape[0], width), lambda i, order: (0, last)) for piece in mixed],
        [
            (line, array((rows, width), jnp.float32)),
            (line, array((rows, width))),
            (line, array((rows, width))),
            (whole((8, width)), array((8, width), jnp.float32)),
        ],
        (grads, resid, upstream, gain[None, :], *mixed),
        "middle_back",
        2 * rows * width * width,
    )


def pull(order, dq, both, mixed, block):
    rows, width = both.shape[0], both.shape[1] // 2
    tile = 512
    tiles = width // tile
    count = len(mixed)
    skip = 0 if block == 0 else tiles
    steps = 3 * tiles - skip
    dtype = BF if block else jnp.float32

    def body(order_ref, *refs):
        lefts = refs[: 1 if block else 2]
        weights = refs[len(lefts) : len(lefts) + count]
        out_ref, total = refs[len(lefts) + count :]
        at = pl.program_id(0)

        @pl.when(at == 0)
        def _():
            total[...] = jnp.zeros_like(total)

        def one(left):
            low = 0
            for weight in weights:
                high = low + weight.shape[0]
                total[:, low:high] += nt(left[...], weight[...])
                low = high

        if block:
            one(lefts[0])
        else:

            @pl.when(at < tiles)
            def _():
                one(lefts[0])

            @pl.when(at >= tiles)
            def _():
                one(lefts[1])

        @pl.when(at == steps - 1)
        def _():
            out_ref[...] = total[...].astype(dtype)

    lefts = [] if block else [pl.BlockSpec((rows, tile), lambda j, order: (0, jnp.minimum(j, tiles - 1)))]
    lefts.append(pl.BlockSpec((rows, tile), lambda j, order: (0, jnp.maximum(j + skip - tiles, 0))))
    return call(
        body,
        order,
        (steps,),
        lefts
        + [
            pl.BlockSpec((piece.shape[0], tile), lambda j, order: (0, j + skip)) for piece in mixed
        ],
        [(whole((rows, width)), array((rows, width), dtype))],
        ((both,) if block else (dq, both)) + tuple(mixed),
        f"pull{block}",
        rows * width * (1 if block else 96 * width),
        scratch=[pltpu.VMEM((rows, width), jnp.float32)],
    )[0]


def end_back(order, parts, tokens, grads, gain):
    rows, width = tokens.shape
    count = len(parts)
    chunk = math.gcd(rows, 256)

    def body(order_ref, x_ref, y_ref, gain_ref, *refs):
        sources = refs[:count]
        out_ref, edge_ref, held, total = refs[count:]

        @pl.when(pl.program_id(0) == 0)
        def _():
            edge_ref[...] = jnp.zeros_like(edge_ref)

        held[...] = sum(source[...].astype(jnp.float32) for source in sources)
        collect(order_ref, held, total)
        found, gain_grad, shift_grad = norm_back(
            x_ref[...].astype(jnp.float32), total[...], gain_ref[...]
        )
        edge_ref[0:1, :] += gain_grad
        edge_ref[1:2, :] += shift_grad
        out_ref[...] = (y_ref[...] + found).astype(BF)

    line = pl.BlockSpec((chunk, width), lambda i, order: (i, 0))
    return call(
        body,
        order,
        (rows // chunk,),
        [line, line, whole((1, width))] + [line] * count,
        [(line, array((rows, width))), (whole((8, width)), array((8, width), jnp.float32))],
        (tokens, grads, gain[None, :], *parts),
        "end_back",
        0,
        scratch=[pltpu.VMEM((chunk, width), jnp.float32), pltpu.VMEM((chunk, width), jnp.float32)],
    )


def join(first, second, part):
    rows, width = first.shape
    stacked = jnp.stack([first.reshape(rows, -1, part), second.reshape(rows, -1, part)], axis=2)
    return stacked.reshape(rows, 2 * width)


def part_ways(both, part):
    rows, width = both.shape
    cut = both.reshape(rows, -1, 2, part)
    return cut[:, :, 0].reshape(rows, width // 2), cut[:, :, 1].reshape(rows, width // 2)


def shards(
    plan,
    tokens,
    lengths,
    cotangent,
    query_weight,
    key_weight,
    value_weight,
    output_weight,
    gate_weight,
    up_weight,
    down_weight,
    attention_gain,
    attention_shift,
    feed_gain,
    feed_shift,
):
    slots = plan.slots()
    windows, local_len, width = tokens.shape
    rows = windows * local_len
    hidden = gate_weight.shape[1]
    place = lax.axis_index("ctx")
    exact = (width // plan.dp) % 128 == 0
    order = slots if exact else jnp.arange(8, dtype=jnp.int32)
    part = hidden // order.shape[0]

    def pieces_of(chain, shard):
        if exact:
            return chain.value
        return [assemble(slots, chain.value, shard.shape[0] * plan.ctx)]

    def in_slots(flipped):
        if exact:
            return flipped
        cut = flipped.reshape(plan.dp, -1, flipped.shape[1])
        return jnp.take(cut, slots, axis=0).reshape(flipped.shape)

    edge = jnp.stack([attention_gain, attention_shift, feed_gain, feed_shift], axis=1)
    edge = jnp.pad(edge, ((0, 0), (0, 124)))
    both = join(key_weight, value_weight, 128)
    mixed = jnp.concatenate([query_weight, both, edge], axis=1)
    mix = Chain(gather_steps(plan, mixed))

    seats = jnp.arange(local_len, dtype=jnp.int32)
    starts = jnp.asarray(plan.blocks)[place] * local_len
    valid = jnp.clip(lengths[0] - starts, 0, local_len)
    cosine, sine = rotary_tables((starts[:, None] + seats[None, :]).reshape(-1))
    real = (place * local_len + seats < lengths[0])[:, None]
    upstream = jnp.where(real, cotangent.reshape(rows, width), 0)
    own = tokens.reshape(rows, width)

    pair_own = jnp.concatenate([join(gate_weight, up_weight, part), output_weight], axis=1)
    early = (pair_own, cosine, sine, upstream)
    pair_own, cosine, sine, upstream = step(early, mix)
    pair = Chain(gather_steps(plan, pair_own, line=True))
    own = step(own, mix, pair)
    own = step(own, mix, pair)
    came = {}
    own, window = begin(own, window_steps(plan, own, came))
    own = finish(own, mix)
    mixed_w = pieces_of(mix, mixed)
    back = jnp.asarray(plan.back)[lax.axis_index("dp")] if exact else order

    flipped, both = {}, {}
    cols = None
    flipped[0], queries, both[0], cols = project(order, own, cols, mixed_w, cosine, sine, 0)
    both[0] = step(both[0], pair)
    state = attend(order, valid, 0, None, plan.ctx == 1, queries, both[0])
    down = None
    for k in range(1, plan.ctx):
        while k not in came:
            state = step(state, window)
        if k == min(3, plan.ctx - 1):
            down_own, state = tie(down_weight, state)
            down = Chain(gather_steps(plan, down_own))
        flipped[k], both[k] = project(order, came[k], cols, mixed_w, cosine, sine, k)
        if k in (1, plan.ctx - 1):
            both[k] = step(both[k], pair)
        state = attend(order, valid, k, state, k == plan.ctx - 1, queries, both[k])
    state = step(state, pair, down)
    state = finish(state, pair)
    pair_w = pieces_of(pair, pair_own)
    natural = cols[:4].reshape(4, order.shape[0], -1)[:, back].reshape(4, width)
    low, low_flipped, attended, lse = state
    resid, two, two_flipped = middle(order, low, pair_w, own, cols)
    two = step(two, down)
    gate, up, made, made_flipped = feed(order, two, pair_w)
    product = product_of(plan, [[(in_slots(made_flipped), upstream)]])
    first = product(plan.dp // 2, plan.dp)
    made, first = finish((made, first), down)
    made, down_sum = begin(made, sum_steps(plan, product, first))
    down_w = pieces_of(down, down_weight)
    output, pair_grads, two_grads = feed_back(
        order, upstream, gate, up, made, resid, pair_w, down_w
    )
    output = output.reshape(windows, local_len, width)

    two_grads, pair_grads = step((two_grads, pair_grads), down_sum)
    two_grads, pair_sum = begin(
        two_grads, sum_steps(plan, product_of(plan, [[(in_slots(two_flipped), pair_grads)]]))
    )
    y_grads, low_grads, go, edge_two = middle_back(
        order, two_grads, resid, upstream, pair_w, natural[2]
    )
    go = step(go, pair_sum)
    go, output_sum = begin(
        go, sum_steps(plan, product_of(plan, [[(in_slots(low_flipped), low_grads)]]))
    )
    held, back_way = None, None
    grads, parts = {}, {}
    flipped = {k: in_slots(flipped[k]) for k in flipped}
    for k in reversed(range(plan.ctx)):
        held, grads[k] = attend_back(
            order, valid, k, held, k == 0, queries, both[k], go, attended, lse, cosine, sine
        )
        if k:
            if k == plan.ctx - 1:
                held = step(held, down_sum, output_sum)
            else:
                held = step(held, pair_sum)
                if plan.line:
                    held = wait(held, back_way)
            held, grads[k] = tie(held, grads[k])
            parts[k] = pull(order, held, grads[k], mixed_w, k)
            held, parts[k] = tie(held, parts[k])
            if plan.line:
                if back_way is None:
                    held, back_way = begin(held, return_steps(plan, parts))
                else:
                    held = go_on(held, back_way)
            if k < plan.ctx - 1:
                held = step(held, down_sum, output_sum)
    finals = [down_sum, output_sum, pair_sum]
    held = wait(held, *finals)
    groups = [[(flipped[0], held)], [(flipped[k], grads[k]) for k in range(plan.ctx)]]
    held, last_sum = begin(held, sum_steps(plan, product_of(plan, groups)))
    held = go_on(held, down_sum, output_sum)
    held = step(held, last_sum)
    held = go_on(held, pair_sum)
    part_grads = pull(order, held, grads[0], mixed_w, 0)
    if plan.line:
        part_grads = finish(part_grads, back_way)
    part_grads = step(part_grads, last_sum)
    if plan.line:
        sends = back_way.value
    else:
        sends = [lax.ppermute(parts[k], AXES, plan.across[k]) for k in range(1, plan.ctx)]
    tokens_grad, edge_one = end_back(
        order, [part_grads, *sends], own, y_grads, natural[0]
    )
    edge_one = step(edge_one, pair_sum)
    edge_one = step(edge_one, last_sum)
    vectors = sum_vectors(plan, (edge_one[0], edge_one[1], edge_two[0], edge_two[1]))
    finish((), last_sum)
    finish((), down_sum, output_sum, pair_sum)
    gate_grad, up_grad = part_ways(pair_sum.value, part)
    key_grad, value_grad = part_ways(last_sum.value[:, width:], 128)
    return (
        output,
        tokens_grad.reshape(windows, local_len, width),
        last_sum.value[:, :width],
        key_grad,
        value_grad,
        output_sum.value,
        gate_grad,
        up_grad,
        down_sum.value,
        *vectors,
    )


def solution(mesh):
    return jax.shard_map(
        functools.partial(shards, Plan(mesh)),
        mesh=mesh,
        in_specs=(
            P("dp", "ctx", None),
            P("dp"),
            P("dp", "ctx", None),
            P(("dp", "ctx"), None),
            P(("dp", "ctx"), None),
            P(("dp", "ctx"), None),
            P(("dp", "ctx"), None),
            P(("dp", "ctx"), None),
            P(("dp", "ctx"), None),
            P(("dp", "ctx"), None),
            P(("dp", "ctx")),
            P(("dp", "ctx")),
            P(("dp", "ctx")),
            P(("dp", "ctx")),
        ),
        out_specs=(
            P("dp", "ctx", None),
            P("dp", "ctx", None),
            P(("dp", "ctx"), None),
            P(("dp", "ctx"), None),
            P(("dp", "ctx"), None),
            P(("dp", "ctx"), None),
            P(("dp", "ctx"), None),
            P(("dp", "ctx"), None),
            P(("dp", "ctx"), None),
            P(("dp", "ctx")),
            P(("dp", "ctx")),
            P(("dp", "ctx")),
            P(("dp", "ctx")),
        ),
        check_vma=False,
    )
```

```python
import functools
import math

import numpy as np

import jax
import jax.numpy as jnp
from jax import lax
from jax.experimental import pallas as pl
from jax.experimental.pallas import tpu as pltpu
from jax.sharding import PartitionSpec as P

H = 16
HD = 64
L = 2048


epsilon = 1e-05
masked_score = -1e30


def layer_norm(values, gain, shift):
    centre = values - jnp.mean(values, axis=-1, keepdims=True)
    spread = jnp.mean(centre * centre, axis=-1, keepdims=True)
    return centre * lax.rsqrt(spread + epsilon) * gain + shift


def rotary_tables(positions):
    half = HD // 2
    turns = jnp.arange(2 * HD, dtype=jnp.int32) % half
    freqs = jnp.exp(turns.astype(jnp.float32) * (-2.0 * math.log(10000.0) / HD))
    angles = positions.astype(jnp.float32)[:, None] * freqs[None, :]
    return (jnp.cos(angles), jnp.sin(angles))


AXES = ("dp", "ctx")
BF = jnp.bfloat16


class Plan:
    def __init__(self, mesh):
        self.dp, self.ctx = mesh.shape["dp"], mesh.shape["ctx"]
        self.stages = self.dp.bit_length() - 2
        self.ctx_bits = self.ctx.bit_length() - 1
        orders = (list(range(1, self.stages + 1)), list(range(self.stages, 0, -1)))
        self.core = self.pairs(lambda d, z: (d ^ 1, z))
        self.stage = [
            self.pairs(lambda d, z, t=t: (d ^ (1 << orders[d & 1][t]), z)) for t in range(self.stages)
        ]
        self.across = [self.pairs(lambda d, z, k=k: (d, z ^ k)) for k in range(self.ctx)]
        self.line = self.ctx == 4
        self.inner = self.pairs(lambda d, z: (d, z ^ 3), (1, 2))
        self.outward = self.pairs(lambda d, z: (d, z ^ 1), (1, 2))
        self.inward = self.pairs(lambda d, z: (d, z ^ 1), (0, 3))
        self.blocks = np.arange(self.ctx)[:, None] ^ np.arange(self.ctx)[None, :]
        if self.line:
            self.blocks = np.array([[0, 1, 2, 3], [1, 0, 2, 3], [2, 3, 1, 0], [3, 2, 1, 0]])
        self.blocks = self.blocks.astype(np.int32)
        half = self.dp // 2
        table = np.zeros((self.dp, self.dp), np.int32)
        for d in range(self.dp):
            for j in range(self.dp):
                owner = d ^ 1 if j >= half else d
                block = owner
                for t in range(self.stages):
                    if (j % half) >> (self.stages - 1 - t) & 1:
                        block ^= 1 << orders[owner & 1][t]
                table[d, j] = block
        self.table = table
        self.back = np.argsort(table, axis=1).astype(np.int32)

    def pairs(self, target, places=None):
        found = []
        for d in range(self.dp):
            for z in range(self.ctx) if places is None else places:
                other, place = target(d, z)
                found.append((d * self.ctx + z, other * self.ctx + place))
        return found

    def slots(self):
        return jnp.asarray(self.table)[lax.axis_index("dp")]


def assemble(slots, pieces, rows):
    blocks = slots.shape[0]
    width = pieces[0].shape[1]
    sizes = [piece.shape[0] // rows for piece in pieces]
    starts = [sum(sizes[:i]) for i in range(len(sizes))]

    def body(order, *refs):
        slot = pl.program_id(0)
        out = refs[-1]
        for piece, start, size in zip(refs, starts, sizes):

            @pl.when((slot >= start) & (slot < start + size))
            def _(piece=piece):
                out[...] = piece[...]

    specs = [
        pl.BlockSpec(
            (rows, width),
            lambda j, order, start=start, size=size: (jnp.clip(j - start, 0, size - 1), 0),
        )
        for start, size in zip(starts, sizes)
    ]
    return pl.pallas_call(
        body,
        out_shape=jax.ShapeDtypeStruct((blocks * rows, width), pieces[0].dtype),
        grid_spec=pltpu.PrefetchScalarGridSpec(
            num_scalar_prefetch=1,
            grid=(blocks,),
            in_specs=specs,
            out_specs=pl.BlockSpec((rows, width), lambda j, order: (order[j], 0)),
        ),
        name="assemble",
    )(slots, *pieces)


def tie(values, others):
    leaves, tree = jax.tree.flatten((values, others))
    return jax.tree.unflatten(tree, lax.optimization_barrier(leaves))


class Chain:
    def __init__(self, steps):
        self.steps = steps
        self.flying, self.sent = next(steps)
        self.done = False
        self.value = None

    def land(self, came):
        if self.done:
            return
        try:
            self.flying, self.sent = self.steps.send(came)
        except StopIteration as stop:
            self.flying, self.sent, self.done, self.value = [], [], True, stop.value


def step(main, *chains):
    main, came = tie(main, [chain.flying for chain in chains])
    for chain, arrays in zip(chains, came):
        chain.land(arrays)
    return tie(main, [chain.sent for chain in chains])[0]


def wait(main, *chains):
    main, came = tie(main, [chain.flying for chain in chains])
    for chain, arrays in zip(chains, came):
        chain.came = arrays
    return main


def go_on(main, *chains):
    main, came = tie(main, [chain.came for chain in chains])
    for chain, arrays in zip(chains, came):
        chain.land(arrays)
    return tie(main, [chain.sent for chain in chains])[0]


def begin(main, steps):
    chain = Chain(steps)
    return tie(main, chain.sent)[0], chain


def finish(main, *chains):
    while not all(chain.done for chain in chains):
        main = step(main, *chains)
    return main


def gather_steps(plan, shard, line=False):
    place = lax.axis_index("ctx")
    if line and plan.line:
        near, middle = yield (
            [lax.ppermute(shard, AXES, plan.across[1]), lax.ppermute(shard, AXES, plan.inner)],
            [shard],
        )
        far, cross = yield (
            [lax.ppermute(middle, AXES, plan.outward), lax.ppermute(near, AXES, plan.inner)],
            [middle, near],
        )
        (last,) = yield [lax.ppermute(cross, AXES, plan.outward)], [cross]
        two, three = middle + far, cross + last
        upper = place >= 2
        blocks = [shard, near, jnp.where(upper, three, two), jnp.where(upper, two, three)]
        odd = place % 2 == 1
        run = jnp.where(
            upper,
            jnp.concatenate(blocks[2:] + [jnp.where(odd, near, shard), jnp.where(odd, shard, near)]),
            jnp.concatenate([jnp.where(odd, near, shard), jnp.where(odd, shard, near)] + blocks[2:]),
        )
    else:
        blocks = yield (
            [lax.ppermute(shard, AXES, plan.across[k]) for k in range(1, plan.ctx)],
            [shard],
        )
        blocks = [shard, *blocks]
        for bit in range(plan.ctx_bits):
            upper = (place >> bit) & 1 == 1
            blocks = [
                jnp.where(upper, jnp.concatenate([b, a]), jnp.concatenate([a, b]))
                for a, b in zip(blocks[::2], blocks[1::2])
            ]
        run = blocks[0]
    *early, final = reversed(plan.stage)
    for pairs in early:
        (other,) = yield [lax.ppermute(run, AXES, pairs)], [run]
        run = jnp.concatenate([run, other])
    other, far = yield [lax.ppermute(run, AXES, final), lax.ppermute(run, AXES, plan.core)], [run]
    (last,) = yield [lax.ppermute(other, AXES, plan.core)], [other]
    return [run, other, far, last]


def add(a, b):
    return (a.astype(jnp.float32) + b.astype(jnp.float32)).astype(BF)


def window_steps(plan, own, came):
    if not plan.line:
        others = yield [lax.ppermute(own, AXES, plan.across[k]) for k in range(1, plan.ctx)], [own]
        came.update(enumerate(others, 1))
        return
    near, middle = yield (
        [lax.ppermute(own, AXES, plan.across[1]), lax.ppermute(own, AXES, plan.inner)],
        [own],
    )
    came[1] = near
    far, cross = yield (
        [lax.ppermute(middle, AXES, plan.outward), lax.ppermute(near, AXES, plan.inner)],
        [middle, near],
    )
    came[2] = middle + far
    (last,) = yield [lax.ppermute(cross, AXES, plan.outward)], [cross]
    came[3] = cross + last


def return_steps(plan, parts):
    (came,) = yield [lax.ppermute(parts[3], AXES, plan.inward)], [parts[3]]
    run = add(parts[3], came)
    near, cross = yield (
        [lax.ppermute(parts[2], AXES, plan.inward), lax.ppermute(run, AXES, plan.inner)],
        [parts[2], run],
    )
    run, last = add(parts[2], near), add(parts[1], cross)
    return (
        yield (
            [
                lax.ppermute(run, AXES, plan.inner),
                lax.ppermute(last, AXES, plan.across[1]),
            ],
            [run, last],
        )
    )


def sum_steps(plan, product, send=None):
    place = lax.axis_index("ctx")
    half = plan.dp // 2

    if send is None:
        send = product(half, plan.dp)
    (other,) = yield [lax.ppermute(send, AXES, plan.core)], [send]
    rows = other.shape[0] // half
    size = half // 2
    send = product(size, half, other[size * rows :])
    flying = [lax.ppermute(send, AXES, plan.stage[0])]
    keep = product(0, size, other[: size * rows])
    (other,) = yield flying, [send, keep]
    held = add(keep, other)
    for pairs in plan.stage[1:]:
        size //= 2
        send = held[size * rows :]
        (other,) = yield [lax.ppermute(send, AXES, pairs)], [send]
        held = add(held[: size * rows], other)
    width = held.shape[1]
    for bit in range(plan.ctx_bits):
        left = 1 << (plan.ctx_bits - bit - 1)
        lower = (place >> bit) & 1
        cut = held.reshape(left, 2, -1, width)
        send = lax.dynamic_index_in_dim(cut, 1 - lower, 1, False).reshape(-1, width)
        keep = lax.dynamic_index_in_dim(cut, lower, 1, False).reshape(-1, width)
        (other,) = yield [lax.ppermute(send, AXES, plan.across[1 << bit])], [send]
        if left > 1:
            held = add(keep, other)
        else:
            held = keep.astype(jnp.float32) + other.astype(jnp.float32)
    return held


def sum_vectors(plan, vectors):
    count = plan.dp * plan.ctx
    packed = jnp.stack(vectors).reshape(len(vectors), count, -1).transpose(1, 0, 2)
    part = packed.shape[2]
    packed = packed.reshape(count, len(vectors) * part)
    came = lax.all_to_all(packed, AXES, split_axis=0, concat_axis=0, tiled=True)
    whole = jnp.sum(came, axis=0)
    return [whole[i * part : (i + 1) * part] for i in range(len(vectors))]


def nt(a, b):
    return lax.dot_general(a, b, (((1,), (1,)), ((), ())), preferred_element_type=jnp.float32)


def turn(values, cosine, sine):
    lane = lax.broadcasted_iota(jnp.int32, values.shape, 1)
    ahead = pltpu.roll(values, 128 - HD // 2, 1)
    behind = pltpu.roll(values, HD // 2, 1)
    turned = jnp.where(lane % HD < HD // 2, -ahead, behind)
    return values * cosine + turned * sine


def head_parts(values):
    lane = lax.broadcasted_iota(jnp.int32, values.shape, 1)
    zero = jnp.zeros_like(values)
    return [jnp.where(lane < HD, values, zero), jnp.where(lane < HD, zero, values)]


def product_of(plan, groups):
    def product(start, end, more=None):
        columns = []
        low = 0
        for terms in groups:
            found = 0.0
            for flipped, right in terms:
                rows = flipped.shape[0] // plan.dp
                part = flipped[start * rows : end * rows]
                found = found + jnp.dot(part, right, preferred_element_type=jnp.float32)
            high = low + found.shape[1]
            if more is not None:
                found = found + more[:, low:high].astype(jnp.float32)
            columns.append(found.astype(BF))
            low = high
        return columns[0] if len(columns) == 1 else jnp.concatenate(columns, axis=1)

    return product


def whole(shape):
    return pl.BlockSpec(shape, lambda *at: (0,) * len(shape))


def call(body, order, grid, ins, outs, operands, name, flops, scratch=(), transcendentals=0):
    size = lambda a: math.prod(a.shape) * jnp.dtype(a.dtype).itemsize
    out_shape = [shape for spec, shape in outs]
    return pl.pallas_call(
        body,
        out_shape=out_shape,
        grid_spec=pltpu.PrefetchScalarGridSpec(
            num_scalar_prefetch=1,
            grid=grid,
            in_specs=ins,
            out_specs=[spec for spec, shape in outs],
            scratch_shapes=list(scratch),
        ),
        cost_estimate=pl.CostEstimate(
            flops=flops,
            bytes_accessed=sum(size(a) for a in [*operands, *out_shape]),
            transcendentals=transcendentals,
        ),
        name=name,
    )(order, *operands)


def array(shape, dtype=BF):
    return jax.ShapeDtypeStruct(shape, dtype)


def spread(order, source, target, rows):
    blocks = order.shape[0]
    part = source.shape[1] // blocks
    for j in range(blocks):
        at = pl.multiple_of(order[j] * part, 128)
        target[rows, j * part : (j + 1) * part] = source[rows, pl.ds(at, part)].astype(target.dtype)


def collect(order, source, target):
    blocks = order.shape[0]
    part = source.shape[1] // blocks
    for j in range(blocks):
        at = pl.multiple_of(order[j] * part, 128)
        target[:, pl.ds(at, part)] = source[:, j * part : (j + 1) * part].astype(target.dtype)


def by_pieces(left, pieces):
    found, low = 0.0, 0
    for piece in pieces:
        high = low + piece.shape[0]
        found = found + jnp.dot(left[:, low:high], piece[...], preferred_element_type=jnp.float32)
        low = high
    return found


def project(order, source, cols, mixed, cosine, sine, block):
    rows, width = source.shape
    tile = 512
    tiles = width // tile
    skip = 0 if block == 0 else tiles
    count = len(mixed)
    scale = 1.0 / math.sqrt(HD)

    def body(order_ref, source_ref, cos_ref, sin_ref, *refs):
        weights, edges = refs[:count], refs[count : -1 - found_outs]
        outs, normed = refs[-1 - found_outs : -1], refs[-1]
        cols_ref = outs[-1] if block == 0 else edges[0]
        at = pl.program_id(0) + skip

        @pl.when(at == skip)
        def _():
            if block == 0:
                low = 0
                for edge in edges:
                    high = low + edge.shape[0]
                    cols_ref[:, low:high] = edge[...].astype(jnp.float32).T[:8]
                    low = high
            spread(order_ref, source_ref, normed, slice(None))
            chunk = math.gcd(rows, 128)

            def one(i, unused):
                here = pl.ds(pl.multiple_of(i * chunk, chunk), chunk)
                found = normed[here, :].astype(jnp.float32)
                normed[here, :] = layer_norm(found, cols_ref[0:1, :], cols_ref[1:2, :]).astype(BF)
                return unused

            lax.fori_loop(0, rows // chunk, one, 0)
            outs[0][...] = normed[...].T

        found = by_pieces(normed, weights)

        def turned(c):
            return turn(found[:, c : c + 128], cos_ref[...], sin_ref[...]).astype(BF)

        if block == 0:

            @pl.when(at < tiles)
            def _():
                for c in range(0, tile, 128):
                    outs[1][:, c : c + 128] = (turned(c).astype(jnp.float32) * scale).astype(BF)

        @pl.when(at >= tiles)
        def _():
            both_ref = outs[2] if block == 0 else outs[1]
            for c in range(0, tile, 256):
                both_ref[:, c : c + 128] = turned(c)
                both_ref[:, c + 128 : c + 256] = found[:, c + 128 : c + 256].astype(BF)

    table = pl.BlockSpec((rows, 128), lambda j, order: (block, 0))
    outs = [(whole((width, rows)), array((width, rows)))]
    if block == 0:
        outs.append(
            (
                pl.BlockSpec((rows, tile), lambda j, order: (0, jnp.minimum(j, tiles - 1))),
                array((rows, width)),
            )
        )
    outs.append(
        (
            pl.BlockSpec((rows, tile), lambda j, order: (0, jnp.maximum(j + skip - tiles, 0))),
            array((rows, 2 * width)),
        )
    )
    if block == 0:
        outs.append((whole((8, width)), array((8, width), jnp.float32)))
        edges = [
            pl.BlockSpec((piece.shape[0], 128), lambda j, order: (0, 3 * width // 128))
            for piece in mixed
        ]
    else:
        edges = [whole((8, width))]
    found_outs = len(outs)
    return call(
        body,
        order,
        (3 * tiles - skip,),
        [whole((rows, width)), table, table]
        + [
            pl.BlockSpec((piece.shape[0], tile), lambda j, order: (0, j + skip)) for piece in mixed
        ]
        + edges,
        outs,
        (source, cosine, sine, *mixed, *(mixed if block == 0 else [cols])),
        f"project{block}",
        32 * rows * width * width * (2 if block else 3),
        scratch=[pltpu.VMEM((rows, width), BF)],
    )


def attend(order, valid, block, state, last, queries, both):
    rows, width = queries.shape
    pairs = width // 128
    first = state is None

    def body(order_ref, valid_ref, q_ref, kv_ref, *refs):
        outs = refs if first else refs[2:]
        parts = head_parts(q_ref[...])
        keys = kv_ref[:, :128]
        flipped = kv_ref[:, 128:].T
        tops, masses, sums = [], [], []
        for head in range(2):
            scores = nt(keys, parts[head])
            seat = lax.broadcasted_iota(jnp.int32, scores.shape, 0)
            scores = jnp.where(seat < valid_ref[block], scores, masked_score)
            top = jnp.max(scores, axis=0, keepdims=True)
            if not first:
                top = jnp.maximum(top, refs[0][0, head : head + 1, :])
            expo = jnp.exp(scores - top)
            mass = jnp.sum(expo, axis=0, keepdims=True)
            held = jnp.dot(
                flipped[head * HD : (head + 1) * HD, :],
                expo.astype(BF),
                preferred_element_type=jnp.float32,
            )
            if not first:
                factor = jnp.exp(refs[0][0, head : head + 1, :] - top)
                mass = mass + refs[0][0, head + 2 : head + 3, :] * factor
                held = held + refs[1][head * HD : (head + 1) * HD, :] * factor
            tops.append(top)
            masses.append(mass)
            sums.append(held)
        blank = jnp.zeros((4, rows), jnp.float32)
        if last:
            found = jnp.concatenate([s / m for s, m in zip(sums, masses)], axis=0)
            outs[1][...] = found.astype(BF)
            found = found.T
            outs[0][...] = found.astype(BF)
            outs[2][...] = found
            lse = [t + jnp.log(m) for t, m in zip(tops, masses)]
            outs[3][...] = jnp.concatenate(lse + masses + [blank], axis=0)[None]
        else:
            outs[0][...] = jnp.concatenate(tops + masses + [blank], axis=0)[None]
            outs[1][...] = jnp.concatenate(sums, axis=0)

    column = pl.BlockSpec((rows, 128), lambda j, order: (0, j))
    stats = pl.BlockSpec((1, 8, rows), lambda j, order: (j, 0, 0))
    carried = pl.BlockSpec((128, rows), lambda j, order: (j, 0))
    stats_shape = array((pairs, 8, rows), jnp.float32)
    if last:
        outs = [
            (column, array((rows, width))),
            (carried, array((width, rows))),
            (column, array((rows, width), jnp.float32)),
            (stats, stats_shape),
        ]
    else:
        outs = [(stats, stats_shape), (carried, array((width, rows), jnp.float32))]
    return call(
        body,
        order,
        (pairs,),
        [
            pl.BlockSpec(memory_space=pltpu.SMEM),
            pl.BlockSpec((rows, 128), lambda j, order: (0, order[j])),
            pl.BlockSpec((rows, 256), lambda j, order: (0, order[j])),
        ]
        + ([] if first else [stats, carried]),
        outs,
        (valid, queries, both, *(() if first else state)),
        f"attend{block}",
        256 * rows * rows * width,
        transcendentals=16 * rows * rows,
    )


def attend_back(order, valid, block, held, last, queries, both, go, attended, lse, cosine, sine):
    rows, width = queries.shape
    pairs = width // 128
    scale = 1.0 / math.sqrt(HD)
    first = held is None

    def body(order_ref, valid_ref, q_ref, kv_ref, go_ref, o_ref, lse_ref, cos_ref, sin_ref, *refs):
        dq_ref, dkv_ref = refs[-2:]
        keys = kv_ref[:, :128]
        values = kv_ref[:, 128:]
        go_all = go_ref[...]
        q_parts = head_parts(q_ref[...])
        go_parts = head_parts(go_all)
        crossed = (go_all.astype(jnp.float32) * o_ref[...]).T
        flipped = keys.T
        dk = jnp.zeros((rows, 128), jnp.float32)
        dv = jnp.zeros((rows, 128), jnp.float32)
        dq = []
        for head in range(2):
            delta = jnp.sum(crossed[head * HD : (head + 1) * HD, :], axis=0, keepdims=True)
            scores = nt(keys, q_parts[head])
            seat = lax.broadcasted_iota(jnp.int32, scores.shape, 0)
            scores = jnp.where(seat < valid_ref[block], scores, masked_score)
            probs = jnp.exp(scores - lse_ref[0, head : head + 1, :])
            grad_probs = nt(values, go_parts[head])
            grad_scores = (probs * (grad_probs - delta)).astype(BF)
            dv = dv + jnp.dot(probs.astype(BF), go_parts[head], preferred_element_type=jnp.float32)
            dk = dk + jnp.dot(grad_scores, q_parts[head], preferred_element_type=jnp.float32)
            dq.append(
                jnp.dot(
                    flipped[head * HD : (head + 1) * HD, :],
                    grad_scores,
                    preferred_element_type=jnp.float32,
                )
            )
        dkv_ref[:, :128] = turn(dk, cos_ref[...], -sin_ref[...]).astype(BF)
        dkv_ref[:, 128:] = dv.astype(BF)
        found = jnp.concatenate(dq, axis=0)
        if not first:
            found = found + refs[0][...]
        if last:
            dq_ref[...] = turn(found.T * scale, cos_ref[...], -sin_ref[...]).astype(BF)
        else:
            dq_ref[...] = found

    column = pl.BlockSpec((rows, 128), lambda j, order: (0, j))
    natural = pl.BlockSpec((rows, 128), lambda j, order: (0, order[j]))
    natural_both = pl.BlockSpec((rows, 256), lambda j, order: (0, order[j]))
    carried = pl.BlockSpec((128, rows), lambda j, order: (j, 0))
    table = pl.BlockSpec((rows, 128), lambda j, order: (block, 0))
    return call(
        body,
        order,
        (pairs,),
        [
            pl.BlockSpec(memory_space=pltpu.SMEM),
            natural,
            natural_both,
            column,
            column,
            pl.BlockSpec((1, 8, rows), lambda j, order: (j, 0, 0)),
            table,
            table,
        ]
        + ([] if first else [carried]),
        [
            (natural, array((rows, width))) if last else (carried, array((width, rows), jnp.float32)),
            (natural_both, array((rows, 2 * width))),
        ],
        (valid, queries, both, go, attended, lse, cosine, sine, *(() if first else (held,))),
        f"attend_back{block}",
        40 * rows * rows * width,
        transcendentals=16 * rows * rows,
    )


def middle(order, attended, mixed, tokens, cols):
    rows, width = tokens.shape
    count = len(mixed)
    last = mixed[0].shape[1] // width - 1
    chunk = math.gcd(rows, 256)

    def body(order_ref, o_ref, x_ref, cols_ref, *refs):
        weights = refs[:count]
        resid_ref, two_ref, flipped_ref, held = refs[count:]
        found = x_ref[...].astype(jnp.float32) + by_pieces(o_ref, weights)
        resid_ref[...] = found
        spread(order_ref, resid_ref, held, slice(None))
        two = layer_norm(held[...], cols_ref[2:3, :], cols_ref[3:4, :]).astype(BF)
        two_ref[...] = two
        flipped_ref[...] = two.T

    line = pl.BlockSpec((chunk, width), lambda i, order: (i, 0))
    return call(
        body,
        order,
        (rows // chunk,),
        [line, line, whole((8, width))]
        + [pl.BlockSpec((piece.shape[0], width), lambda i, order: (0, last)) for piece in mixed],
        [
            (line, array((rows, width), jnp.float32)),
            (line, array((rows, width))),
            (pl.BlockSpec((width, chunk), lambda i, order: (0, i)), array((width, rows))),
        ],
        (attended, tokens, cols, *mixed),
        "middle",
        2 * rows * width * width,
        scratch=[pltpu.VMEM((chunk, width), jnp.float32)],
    )


def feed(order, two, pair):
    rows, width = two.shape
    blocks = order.shape[0]
    hidden = (pair[0].shape[1] - width) // 2
    part = hidden // blocks
    count = len(pair)

    def body(order_ref, two_ref, *refs):
        gate_ref, up_ref, hidden_ref, flipped_ref = refs[count:]
        found = by_pieces(two_ref, refs[:count])
        gate, up = found[:, :part], found[:, part:]
        made = (gate / (1.0 + jnp.exp(-gate)) * up).astype(BF)
        gate_ref[...] = gate.astype(BF)
        up_ref[...] = up.astype(BF)
        hidden_ref[...] = made
        flipped_ref[...] = made.T

    tile = pl.BlockSpec((rows, part), lambda j, order: (0, j))
    shape = array((rows, hidden))
    return call(
        body,
        order,
        (blocks,),
        [whole((rows, width))]
        + [
            pl.BlockSpec((piece.shape[0], 2 * part), lambda j, order: (0, order[j]))
            for piece in pair
        ],
        [
            (tile, shape),
            (tile, shape),
            (tile, shape),
            (pl.BlockSpec((part, rows), lambda j, order: (j, 0)), array((hidden, rows))),
        ],
        (two, *pair),
        "feed",
        4 * rows * width * hidden,
        transcendentals=rows * hidden,
    )


def feed_back(order, upstream, gate, up, made, resid, pair, down):
    rows, width = upstream.shape
    blocks = order.shape[0]
    hidden = gate.shape[1]
    part = hidden // blocks
    count, downs = len(pair), len(down)
    each = blocks // downs

    def body(order_ref, m_ref, gate_ref, up_ref, made_ref, resid_ref, *refs):
        pairs, lows = refs[:count], refs[count : count + downs]
        out_ref, grads_ref, two_ref, total, result = refs[count + downs :]
        at = pl.program_id(0)

        @pl.when(at == 0)
        def _():
            total[...] = jnp.zeros_like(total)
            result[...] = resid_ref[...]

        def one(low):
            gate_all = gate_ref[...].astype(jnp.float32)
            up_all = up_ref[...].astype(jnp.float32)
            sigma = 1.0 / (1.0 + jnp.exp(-gate_all))
            made_grad = nt(m_ref[...], low[...])
            result[...] += jnp.dot(made_ref[...], low[...], preferred_element_type=jnp.float32)
            gate_grad = made_grad * up_all * sigma * (1.0 + gate_all * (1.0 - sigma))
            grads_ref[:, :part] = gate_grad.astype(BF)
            grads_ref[:, part:] = (made_grad * gate_all * sigma).astype(BF)

        for i in range(downs):

            @pl.when((at >= i * each) & (at < (i + 1) * each))
            def _(i=i):
                one(lows[i])

        grads = grads_ref[...]
        low = 0
        for piece in pairs:
            high = low + piece.shape[0]
            total[:, low:high] += nt(grads, piece[...])
            low = high

        @pl.when(at == blocks - 1)
        def _():
            out_ref[...] = result[...].astype(BF)
            collect(order_ref, total, two_ref)

    tile = pl.BlockSpec((rows, part), lambda j, order: (0, j))
    return call(
        body,
        order,
        (blocks,),
        [whole((rows, width)), tile, tile, tile, whole((rows, width))]
        + [
            pl.BlockSpec((piece.shape[0], 2 * part), lambda j, order: (0, order[j]))
            for piece in pair
        ]
        + [
            pl.BlockSpec(
                (part, width), lambda j, order, i=i: (jnp.clip(j - i * each, 0, each - 1), 0)
            )
            for i in range(downs)
        ],
        [
            (whole((rows, width)), array((rows, width))),
            (
                pl.BlockSpec((rows, 2 * part), lambda j, order: (0, order[j])),
                array((rows, 2 * hidden)),
            ),
            (whole((rows, width)), array((rows, width), jnp.float32)),
        ],
        (upstream, gate, up, made, resid, *pair, *down),
        "feed_back",
        8 * rows * width * hidden,
        scratch=[pltpu.VMEM((rows, width), jnp.float32), pltpu.VMEM((rows, width), jnp.float32)],
        transcendentals=rows * hidden,
    )


def norm_back(values, grads, gain):
    centre = values - jnp.mean(values, axis=-1, keepdims=True)
    scale = lax.rsqrt(jnp.mean(centre * centre, axis=-1, keepdims=True) + epsilon)
    normed = centre * scale
    scaled = grads * gain
    inner = jnp.mean(scaled * normed, axis=-1, keepdims=True)
    found = (scaled - jnp.mean(scaled, axis=-1, keepdims=True) - normed * inner) * scale
    return (
        found,
        jnp.sum(grads * normed, axis=0, keepdims=True),
        jnp.sum(grads, axis=0, keepdims=True),
    )


def middle_back(order, grads, resid, upstream, mixed, gain):
    rows, width = resid.shape
    count = len(mixed)
    last = mixed[0].shape[1] // width - 1
    chunk = math.gcd(rows, 256)

    def body(order_ref, grads_ref, resid_ref, m_ref, gain_ref, *refs):
        weights = refs[:count]
        y_ref, a_ref, go_ref, edge_ref = refs[count:]

        @pl.when(pl.program_id(0) == 0)
        def _():
            edge_ref[...] = jnp.zeros_like(edge_ref)

        found, gain_grad, shift_grad = norm_back(resid_ref[...], grads_ref[...], gain_ref[...])
        found = m_ref[...].astype(jnp.float32) + found
        edge_ref[0:1, :] += gain_grad
        edge_ref[1:2, :] += shift_grad
        y_ref[...] = found
        a_ref[...] = found.astype(BF)
        low = 0
        for weight in weights:
            high = low + weight.shape[0]
            go_ref[:, low:high] = nt(a_ref[...], weight[...]).astype(BF)
            low = high

    line = pl.BlockSpec((chunk, width), lambda i, order: (i, 0))
    return call(
        body,
        order,
        (rows // chunk,),
        [line, line, line, whole((1, width))]
        + [pl.BlockSpec((piece.shape[0], width), lambda i, order: (0, last)) for piece in mixed],
        [
            (line, array((rows, width), jnp.float32)),
            (line, array((rows, width))),
            (line, array((rows, width))),
            (whole((8, width)), array((8, width), jnp.float32)),
        ],
        (grads, resid, upstream, gain[None, :], *mixed),
        "middle_back",
        2 * rows * width * width,
    )


def pull(order, dq, both, mixed, block):
    rows, width = both.shape[0], both.shape[1] // 2
    tile = 512
    tiles = width // tile
    count = len(mixed)
    skip = 0 if block == 0 else tiles
    steps = 3 * tiles - skip
    dtype = BF if block else jnp.float32

    def body(order_ref, *refs):
        lefts = refs[: 1 if block else 2]
        weights = refs[len(lefts) : len(lefts) + count]
        out_ref, total = refs[len(lefts) + count :]
        at = pl.program_id(0)

        @pl.when(at == 0)
        def _():
            total[...] = jnp.zeros_like(total)

        def one(left):
            low = 0
            for weight in weights:
                high = low + weight.shape[0]
                total[:, low:high] += nt(left[...], weight[...])
                low = high

        if block:
            one(lefts[0])
        else:

            @pl.when(at < tiles)
            def _():
                one(lefts[0])

            @pl.when(at >= tiles)
            def _():
                one(lefts[1])

        @pl.when(at == steps - 1)
        def _():
            out_ref[...] = total[...].astype(dtype)

    lefts = [] if block else [pl.BlockSpec((rows, tile), lambda j, order: (0, jnp.minimum(j, tiles - 1)))]
    lefts.append(pl.BlockSpec((rows, tile), lambda j, order: (0, jnp.maximum(j + skip - tiles, 0))))
    return call(
        body,
        order,
        (steps,),
        lefts
        + [
            pl.BlockSpec((piece.shape[0], tile), lambda j, order: (0, j + skip)) for piece in mixed
        ],
        [(whole((rows, width)), array((rows, width), dtype))],
        ((both,) if block else (dq, both)) + tuple(mixed),
        f"pull{block}",
        rows * width * (1 if block else 96 * width),
        scratch=[pltpu.VMEM((rows, width), jnp.float32)],
    )[0]


def end_back(order, parts, tokens, grads, gain):
    rows, width = tokens.shape
    count = len(parts)
    chunk = math.gcd(rows, 256)

    def body(order_ref, x_ref, y_ref, gain_ref, *refs):
        sources = refs[:count]
        out_ref, edge_ref, held, total = refs[count:]

        @pl.when(pl.program_id(0) == 0)
        def _():
            edge_ref[...] = jnp.zeros_like(edge_ref)

        held[...] = sum(source[...].astype(jnp.float32) for source in sources)
        collect(order_ref, held, total)
        found, gain_grad, shift_grad = norm_back(
            x_ref[...].astype(jnp.float32), total[...], gain_ref[...]
        )
        edge_ref[0:1, :] += gain_grad
        edge_ref[1:2, :] += shift_grad
        out_ref[...] = (y_ref[...] + found).astype(BF)

    line = pl.BlockSpec((chunk, width), lambda i, order: (i, 0))
    return call(
        body,
        order,
        (rows // chunk,),
        [line, line, whole((1, width))] + [line] * count,
        [(line, array((rows, width))), (whole((8, width)), array((8, width), jnp.float32))],
        (tokens, grads, gain[None, :], *parts),
        "end_back",
        0,
        scratch=[pltpu.VMEM((chunk, width), jnp.float32), pltpu.VMEM((chunk, width), jnp.float32)],
    )


def join(first, second, part):
    rows, width = first.shape
    stacked = jnp.stack([first.reshape(rows, -1, part), second.reshape(rows, -1, part)], axis=2)
    return stacked.reshape(rows, 2 * width)


def part_ways(both, part):
    rows, width = both.shape
    cut = both.reshape(rows, -1, 2, part)
    return cut[:, :, 0].reshape(rows, width // 2), cut[:, :, 1].reshape(rows, width // 2)


def shards(
    plan,
    tokens,
    lengths,
    cotangent,
    query_weight,
    key_weight,
    value_weight,
    output_weight,
    gate_weight,
    up_weight,
    down_weight,
    attention_gain,
    attention_shift,
    feed_gain,
    feed_shift,
):
    slots = plan.slots()
    windows, local_len, width = tokens.shape
    rows = windows * local_len
    hidden = gate_weight.shape[1]
    place = lax.axis_index("ctx")
    exact = (width // plan.dp) % 128 == 0
    order = slots if exact else jnp.arange(8, dtype=jnp.int32)
    part = hidden // order.shape[0]

    def pieces_of(chain, shard):
        if exact:
            return chain.value
        return [assemble(slots, chain.value, shard.shape[0] * plan.ctx)]

    def in_slots(flipped):
        if exact:
            return flipped
        cut = flipped.reshape(plan.dp, -1, flipped.shape[1])
        return jnp.take(cut, slots, axis=0).reshape(flipped.shape)

    edge = jnp.stack([attention_gain, attention_shift, feed_gain, feed_shift], axis=1)
    edge = jnp.pad(edge, ((0, 0), (0, 124)))
    both = join(key_weight, value_weight, 128)
    mixed = jnp.concatenate([query_weight, both, edge], axis=1)
    mix = Chain(gather_steps(plan, mixed))

    seats = jnp.arange(local_len, dtype=jnp.int32)
    starts = jnp.asarray(plan.blocks)[place] * local_len
    valid = jnp.clip(lengths[0] - starts, 0, local_len)
    cosine, sine = rotary_tables((starts[:, None] + seats[None, :]).reshape(-1))
    real = (place * local_len + seats < lengths[0])[:, None]
    upstream = jnp.where(real, cotangent.reshape(rows, width), 0)
    own = tokens.reshape(rows, width)

    pair_own = jnp.concatenate([join(gate_weight, up_weight, part), output_weight], axis=1)
    early = (pair_own, cosine, sine, upstream)
    pair_own, cosine, sine, upstream = step(early, mix)
    pair = Chain(gather_steps(plan, pair_own, line=True))
    own = step(own, mix, pair)
    own = step(own, mix, pair)
    came = {}
    own, window = begin(own, window_steps(plan, own, came))
    own = finish(own, mix)
    mixed_w = pieces_of(mix, mixed)
    back = jnp.asarray(plan.back)[lax.axis_index("dp")] if exact else order

    flipped, both = {}, {}
    cols = None
    flipped[0], queries, both[0], cols = project(order, own, cols, mixed_w, cosine, sine, 0)
    both[0] = step(both[0], pair)
    state = attend(order, valid, 0, None, plan.ctx == 1, queries, both[0])
    down = None
    for k in range(1, plan.ctx):
        while k not in came:
            state = step(state, window)
        if k == min(3, plan.ctx - 1):
            down_own, state = tie(down_weight, state)
            down = Chain(gather_steps(plan, down_own))
        flipped[k], both[k] = project(order, came[k], cols, mixed_w, cosine, sine, k)
        if k in (1, plan.ctx - 1):
            both[k] = step(both[k], pair)
        state = attend(order, valid, k, state, k == plan.ctx - 1, queries, both[k])
    state = step(state, pair, down)
    state = finish(state, pair)
    pair_w = pieces_of(pair, pair_own)
    natural = cols[:4].reshape(4, order.shape[0], -1)[:, back].reshape(4, width)
    low, low_flipped, attended, lse = state
    resid, two, two_flipped = middle(order, low, pair_w, own, cols)
    two = step(two, down)
    gate, up, made, made_flipped = feed(order, two, pair_w)
    product = product_of(plan, [[(in_slots(made_flipped), upstream)]])
    first = product(plan.dp // 2, plan.dp)
    made, first = finish((made, first), down)
    made, down_sum = begin(made, sum_steps(plan, product, first))
    down_w = pieces_of(down, down_weight)
    output, pair_grads, two_grads = feed_back(
        order, upstream, gate, up, made, resid, pair_w, down_w
    )
    output = output.reshape(windows, local_len, width)

    two_grads, pair_grads = step((two_grads, pair_grads), down_sum)
    two_grads, pair_sum = begin(
        two_grads, sum_steps(plan, product_of(plan, [[(in_slots(two_flipped), pair_grads)]]))
    )
    y_grads, low_grads, go, edge_two = middle_back(
        order, two_grads, resid, upstream, pair_w, natural[2]
    )
    go = step(go, pair_sum)
    go, output_sum = begin(
        go, sum_steps(plan, product_of(plan, [[(in_slots(low_flipped), low_grads)]]))
    )
    held, back_way = None, None
    grads, parts = {}, {}
    flipped = {k: in_slots(flipped[k]) for k in flipped}
    for k in reversed(range(plan.ctx)):
        held, grads[k] = attend_back(
            order, valid, k, held, k == 0, queries, both[k], go, attended, lse, cosine, sine
        )
        if k:
            if k == plan.ctx - 1:
                held = step(held, down_sum, output_sum)
            else:
                held = step(held, pair_sum)
                if plan.line:
                    held = wait(held, back_way)
            held, grads[k] = tie(held, grads[k])
            parts[k] = pull(order, held, grads[k], mixed_w, k)
            held, parts[k] = tie(held, parts[k])
            if plan.line:
                if back_way is None:
                    held, back_way = begin(held, return_steps(plan, parts))
                else:
                    held = go_on(held, back_way)
            if k < plan.ctx - 1:
                held = step(held, down_sum, output_sum)
    finals = [down_sum, output_sum, pair_sum]
    held = wait(held, *finals)
    groups = [[(flipped[0], held)], [(flipped[k], grads[k]) for k in range(plan.ctx)]]
    held, last_sum = begin(held, sum_steps(plan, product_of(plan, groups)))
    held = go_on(held, down_sum, output_sum)
    held = step(held, last_sum)
    held = go_on(held, pair_sum)
    part_grads = pull(order, held, grads[0], mixed_w, 0)
    part_grads = finish(part_grads, down_sum, output_sum, *([back_way] if plan.line else []))
    part_grads = step(part_grads, last_sum)
    if plan.line:
        sends = back_way.value
    else:
        sends = [lax.ppermute(parts[k], AXES, plan.across[k]) for k in range(1, plan.ctx)]
    tokens_grad, edge_one = end_back(
        order, [part_grads, *sends], own, y_grads, natural[0]
    )
    edge_one = step(edge_one, pair_sum)
    edge_one = step(edge_one, last_sum)
    vectors = sum_vectors(plan, (edge_one[0], edge_one[1], edge_two[0], edge_two[1]))
    finish((), pair_sum)
    pair_grads = pair_sum.value
    for _ in range(plan.ctx_bits - 1):
        pair_grads = step(pair_grads, last_sum)
    finish((), last_sum)
    gate_grad, up_grad = part_ways(pair_grads, part)
    key_grad, value_grad = part_ways(last_sum.value[:, width:], 128)
    return (
        output,
        tokens_grad.reshape(windows, local_len, width),
        last_sum.value[:, :width],
        key_grad,
        value_grad,
        output_sum.value,
        gate_grad,
        up_grad,
        down_sum.value,
        *vectors,
    )


def solution(mesh):
    return jax.shard_map(
        functools.partial(shards, Plan(mesh)),
        mesh=mesh,
        in_specs=(
            P("dp", "ctx", None),
            P("dp"),
            P("dp", "ctx", None),
            P(("dp", "ctx"), None),
            P(("dp", "ctx"), None),
            P(("dp", "ctx"), None),
            P(("dp", "ctx"), None),
            P(("dp", "ctx"), None),
            P(("dp", "ctx"), None),
            P(("dp", "ctx"), None),
            P(("dp", "ctx")),
            P(("dp", "ctx")),
            P(("dp", "ctx")),
            P(("dp", "ctx")),
        ),
        out_specs=(
            P("dp", "ctx", None),
            P("dp", "ctx", None),
            P(("dp", "ctx"), None),
            P(("dp", "ctx"), None),
            P(("dp", "ctx"), None),
            P(("dp", "ctx"), None),
            P(("dp", "ctx"), None),
            P(("dp", "ctx"), None),
            P(("dp", "ctx"), None),
            P(("dp", "ctx")),
            P(("dp", "ctx")),
            P(("dp", "ctx")),
            P(("dp", "ctx")),
        ),
        check_vma=False,
    )
```

```python
import functools
import math

import numpy as np

import jax
import jax.numpy as jnp
from jax import lax
from jax.experimental import pallas as pl
from jax.experimental.pallas import tpu as pltpu
from jax.sharding import PartitionSpec as P

H = 16
HD = 64
L = 2048


epsilon = 1e-05
masked_score = -1e30


def layer_norm(values, gain, shift):
    centre = values - jnp.mean(values, axis=-1, keepdims=True)
    spread = jnp.mean(centre * centre, axis=-1, keepdims=True)
    return centre * lax.rsqrt(spread + epsilon) * gain + shift


def rotary_tables(positions):
    half = HD // 2
    turns = jnp.arange(2 * HD, dtype=jnp.int32) % half
    freqs = jnp.exp(turns.astype(jnp.float32) * (-2.0 * math.log(10000.0) / HD))
    angles = positions.astype(jnp.float32)[:, None] * freqs[None, :]
    return (jnp.cos(angles), jnp.sin(angles))


AXES = ("dp", "ctx")
BF = jnp.bfloat16


class Plan:
    def __init__(self, mesh):
        self.dp, self.ctx = mesh.shape["dp"], mesh.shape["ctx"]
        self.stages = self.dp.bit_length() - 2
        self.ctx_bits = self.ctx.bit_length() - 1
        orders = (list(range(1, self.stages + 1)), list(range(self.stages, 0, -1)))
        self.core = self.pairs(lambda d, z: (d ^ 1, z))
        self.stage = [
            self.pairs(lambda d, z, t=t: (d ^ (1 << orders[d & 1][t]), z)) for t in range(self.stages)
        ]
        self.across = [self.pairs(lambda d, z, k=k: (d, z ^ k)) for k in range(self.ctx)]
        self.line = self.ctx == 4
        self.inner = self.pairs(lambda d, z: (d, z ^ 3), (1, 2))
        self.outward = self.pairs(lambda d, z: (d, z ^ 1), (1, 2))
        self.inward = self.pairs(lambda d, z: (d, z ^ 1), (0, 3))
        self.blocks = np.arange(self.ctx)[:, None] ^ np.arange(self.ctx)[None, :]
        if self.line:
            self.blocks = np.array([[0, 1, 2, 3], [1, 0, 2, 3], [2, 3, 1, 0], [3, 2, 1, 0]])
        self.blocks = self.blocks.astype(np.int32)
        half = self.dp // 2
        table = np.zeros((self.dp, self.dp), np.int32)
        for d in range(self.dp):
            for j in range(self.dp):
                owner = d ^ 1 if j >= half else d
                block = owner
                for t in range(self.stages):
                    if (j % half) >> (self.stages - 1 - t) & 1:
                        block ^= 1 << orders[owner & 1][t]
                table[d, j] = block
        self.table = table
        self.back = np.argsort(table, axis=1).astype(np.int32)

    def pairs(self, target, places=None):
        found = []
        for d in range(self.dp):
            for z in range(self.ctx) if places is None else places:
                other, place = target(d, z)
                found.append((d * self.ctx + z, other * self.ctx + place))
        return found

    def slots(self):
        return jnp.asarray(self.table)[lax.axis_index("dp")]


def assemble(slots, pieces, rows):
    blocks = slots.shape[0]
    width = pieces[0].shape[1]
    sizes = [piece.shape[0] // rows for piece in pieces]
    starts = [sum(sizes[:i]) for i in range(len(sizes))]

    def body(order, *refs):
        slot = pl.program_id(0)
        out = refs[-1]
        for piece, start, size in zip(refs, starts, sizes):

            @pl.when((slot >= start) & (slot < start + size))
            def _(piece=piece):
                out[...] = piece[...]

    specs = [
        pl.BlockSpec(
            (rows, width),
            lambda j, order, start=start, size=size: (jnp.clip(j - start, 0, size - 1), 0),
        )
        for start, size in zip(starts, sizes)
    ]
    return pl.pallas_call(
        body,
        out_shape=jax.ShapeDtypeStruct((blocks * rows, width), pieces[0].dtype),
        grid_spec=pltpu.PrefetchScalarGridSpec(
            num_scalar_prefetch=1,
            grid=(blocks,),
            in_specs=specs,
            out_specs=pl.BlockSpec((rows, width), lambda j, order: (order[j], 0)),
        ),
        name="assemble",
    )(slots, *pieces)


def tie(values, others):
    leaves, tree = jax.tree.flatten((values, others))
    return jax.tree.unflatten(tree, lax.optimization_barrier(leaves))


class Chain:
    def __init__(self, steps):
        self.steps = steps
        self.flying, self.sent = next(steps)
        self.done = False
        self.value = None

    def land(self, came):
        if self.done:
            return
        try:
            self.flying, self.sent = self.steps.send(came)
        except StopIteration as stop:
            self.flying, self.sent, self.done, self.value = [], [], True, stop.value


def step(main, *chains):
    main, came = tie(main, [chain.flying for chain in chains])
    for chain, arrays in zip(chains, came):
        chain.land(arrays)
    return tie(main, [chain.sent for chain in chains])[0]


def wait(main, *chains):
    main, came = tie(main, [chain.flying for chain in chains])
    for chain, arrays in zip(chains, came):
        chain.came = arrays
    return main


def go_on(main, *chains):
    main, came = tie(main, [chain.came for chain in chains])
    for chain, arrays in zip(chains, came):
        chain.land(arrays)
    return tie(main, [chain.sent for chain in chains])[0]


def begin(main, steps):
    chain = Chain(steps)
    return tie(main, chain.sent)[0], chain


def finish(main, *chains):
    while not all(chain.done for chain in chains):
        main = step(main, *chains)
    return main


def gather_steps(plan, shard, line=False):
    place = lax.axis_index("ctx")
    if line and plan.line:
        near, middle = yield (
            [lax.ppermute(shard, AXES, plan.across[1]), lax.ppermute(shard, AXES, plan.inner)],
            [shard],
        )
        far, cross = yield (
            [lax.ppermute(middle, AXES, plan.outward), lax.ppermute(near, AXES, plan.inner)],
            [middle, near],
        )
        (last,) = yield [lax.ppermute(cross, AXES, plan.outward)], [cross]
        two, three = middle + far, cross + last
        upper = place >= 2
        blocks = [shard, near, jnp.where(upper, three, two), jnp.where(upper, two, three)]
        odd = place % 2 == 1
        run = jnp.where(
            upper,
            jnp.concatenate(blocks[2:] + [jnp.where(odd, near, shard), jnp.where(odd, shard, near)]),
            jnp.concatenate([jnp.where(odd, near, shard), jnp.where(odd, shard, near)] + blocks[2:]),
        )
    else:
        blocks = yield (
            [lax.ppermute(shard, AXES, plan.across[k]) for k in range(1, plan.ctx)],
            [shard],
        )
        blocks = [shard, *blocks]
        for bit in range(plan.ctx_bits):
            upper = (place >> bit) & 1 == 1
            blocks = [
                jnp.where(upper, jnp.concatenate([b, a]), jnp.concatenate([a, b]))
                for a, b in zip(blocks[::2], blocks[1::2])
            ]
        run = blocks[0]
    *early, final = reversed(plan.stage)
    for pairs in early:
        (other,) = yield [lax.ppermute(run, AXES, pairs)], [run]
        run = jnp.concatenate([run, other])
    other, far = yield [lax.ppermute(run, AXES, final), lax.ppermute(run, AXES, plan.core)], [run]
    (last,) = yield [lax.ppermute(other, AXES, plan.core)], [other]
    return [run, other, far, last]


def add(a, b):
    return (a.astype(jnp.float32) + b.astype(jnp.float32)).astype(BF)


def window_steps(plan, own, came):
    if not plan.line:
        others = yield [lax.ppermute(own, AXES, plan.across[k]) for k in range(1, plan.ctx)], [own]
        came.update(enumerate(others, 1))
        return
    near, middle = yield (
        [lax.ppermute(own, AXES, plan.across[1]), lax.ppermute(own, AXES, plan.inner)],
        [own],
    )
    came[1] = near
    far, cross = yield (
        [lax.ppermute(middle, AXES, plan.outward), lax.ppermute(near, AXES, plan.inner)],
        [middle, near],
    )
    came[2] = middle + far
    (last,) = yield [lax.ppermute(cross, AXES, plan.outward)], [cross]
    came[3] = cross + last


def return_steps(plan, parts):
    (came,) = yield [lax.ppermute(parts[3], AXES, plan.inward)], [parts[3]]
    run = add(parts[3], came)
    near, cross = yield (
        [lax.ppermute(parts[2], AXES, plan.inward), lax.ppermute(run, AXES, plan.inner)],
        [parts[2], run],
    )
    run, last = add(parts[2], near), add(parts[1], cross)
    return (
        yield (
            [
                lax.ppermute(run, AXES, plan.inner),
                lax.ppermute(last, AXES, plan.across[1]),
            ],
            [run, last],
        )
    )


def sum_steps(plan, product, send=None):
    place = lax.axis_index("ctx")
    half = plan.dp // 2

    if send is None:
        send = product(half, plan.dp)
    (other,) = yield [lax.ppermute(send, AXES, plan.core)], [send]
    rows = other.shape[0] // half
    size = half // 2
    send = product(size, half, other[size * rows :])
    flying = [lax.ppermute(send, AXES, plan.stage[0])]
    keep = product(0, size, other[: size * rows])
    (other,) = yield flying, [send, keep]
    held = add(keep, other)
    for pairs in plan.stage[1:]:
        size //= 2
        send = held[size * rows :]
        (other,) = yield [lax.ppermute(send, AXES, pairs)], [send]
        held = add(held[: size * rows], other)
    width = held.shape[1]
    for bit in range(plan.ctx_bits):
        left = 1 << (plan.ctx_bits - bit - 1)
        lower = (place >> bit) & 1
        cut = held.reshape(left, 2, -1, width)
        send = lax.dynamic_index_in_dim(cut, 1 - lower, 1, False).reshape(-1, width)
        keep = lax.dynamic_index_in_dim(cut, lower, 1, False).reshape(-1, width)
        (other,) = yield [lax.ppermute(send, AXES, plan.across[1 << bit])], [send]
        if left > 1:
            held = add(keep, other)
        else:
            held = keep.astype(jnp.float32) + other.astype(jnp.float32)
    return held


def sum_vectors(plan, vectors):
    count = plan.dp * plan.ctx
    packed = jnp.stack(vectors).reshape(len(vectors), count, -1).transpose(1, 0, 2)
    part = packed.shape[2]
    packed = packed.reshape(count, len(vectors) * part)
    came = lax.all_to_all(packed, AXES, split_axis=0, concat_axis=0, tiled=True)
    whole = jnp.sum(came, axis=0)
    return [whole[i * part : (i + 1) * part] for i in range(len(vectors))]


def nt(a, b):
    return lax.dot_general(a, b, (((1,), (1,)), ((), ())), preferred_element_type=jnp.float32)


def turn(values, cosine, sine):
    lane = lax.broadcasted_iota(jnp.int32, values.shape, 1)
    ahead = pltpu.roll(values, 128 - HD // 2, 1)
    behind = pltpu.roll(values, HD // 2, 1)
    turned = jnp.where(lane % HD < HD // 2, -ahead, behind)
    return values * cosine + turned * sine


def head_parts(values):
    lane = lax.broadcasted_iota(jnp.int32, values.shape, 1)
    zero = jnp.zeros_like(values)
    return [jnp.where(lane < HD, values, zero), jnp.where(lane < HD, zero, values)]


def product_of(plan, groups):
    def product(start, end, more=None):
        columns = []
        low = 0
        for terms in groups:
            found = 0.0
            for flipped, right in terms:
                rows = flipped.shape[0] // plan.dp
                part = flipped[start * rows : end * rows]
                found = found + jnp.dot(part, right, preferred_element_type=jnp.float32)
            high = low + found.shape[1]
            if more is not None:
                found = found + more[:, low:high].astype(jnp.float32)
            columns.append(found.astype(BF))
            low = high
        return columns[0] if len(columns) == 1 else jnp.concatenate(columns, axis=1)

    return product


def whole(shape):
    return pl.BlockSpec(shape, lambda *at: (0,) * len(shape))


def call(body, order, grid, ins, outs, operands, name, flops, scratch=(), transcendentals=0):
    size = lambda a: math.prod(a.shape) * jnp.dtype(a.dtype).itemsize
    out_shape = [shape for spec, shape in outs]
    return pl.pallas_call(
        body,
        out_shape=out_shape,
        grid_spec=pltpu.PrefetchScalarGridSpec(
            num_scalar_prefetch=1,
            grid=grid,
            in_specs=ins,
            out_specs=[spec for spec, shape in outs],
            scratch_shapes=list(scratch),
        ),
        cost_estimate=pl.CostEstimate(
            flops=flops,
            bytes_accessed=sum(size(a) for a in [*operands, *out_shape]),
            transcendentals=transcendentals,
        ),
        name=name,
    )(order, *operands)


def array(shape, dtype=BF):
    return jax.ShapeDtypeStruct(shape, dtype)


def spread(order, source, target, rows):
    blocks = order.shape[0]
    part = source.shape[1] // blocks
    for j in range(blocks):
        at = pl.multiple_of(order[j] * part, 128)
        target[rows, j * part : (j + 1) * part] = source[rows, pl.ds(at, part)].astype(target.dtype)


def collect(order, source, target):
    blocks = order.shape[0]
    part = source.shape[1] // blocks
    for j in range(blocks):
        at = pl.multiple_of(order[j] * part, 128)
        target[:, pl.ds(at, part)] = source[:, j * part : (j + 1) * part].astype(target.dtype)


def by_pieces(left, pieces):
    found, low = 0.0, 0
    for piece in pieces:
        high = low + piece.shape[0]
        found = found + jnp.dot(left[:, low:high], piece[...], preferred_element_type=jnp.float32)
        low = high
    return found


def project(order, source, cols, mixed, cosine, sine, block):
    rows, width = source.shape
    tile = 512
    tiles = width // tile
    skip = 0 if block == 0 else tiles
    count = len(mixed)
    scale = 1.0 / math.sqrt(HD)

    def body(order_ref, source_ref, cos_ref, sin_ref, *refs):
        weights, edges = refs[:count], refs[count : -1 - found_outs]
        outs, normed = refs[-1 - found_outs : -1], refs[-1]
        cols_ref = outs[-1] if block == 0 else edges[0]
        at = pl.program_id(0) + skip

        @pl.when(at == skip)
        def _():
            if block == 0:
                low = 0
                for edge in edges:
                    high = low + edge.shape[0]
                    cols_ref[:, low:high] = edge[...].astype(jnp.float32).T[:8]
                    low = high
            spread(order_ref, source_ref, normed, slice(None))
            chunk = math.gcd(rows, 128)

            def one(i, unused):
                here = pl.ds(pl.multiple_of(i * chunk, chunk), chunk)
                found = normed[here, :].astype(jnp.float32)
                normed[here, :] = layer_norm(found, cols_ref[0:1, :], cols_ref[1:2, :]).astype(BF)
                return unused

            lax.fori_loop(0, rows // chunk, one, 0)
            outs[0][...] = normed[...].T

        found = by_pieces(normed, weights)

        def turned(c):
            return turn(found[:, c : c + 128], cos_ref[...], sin_ref[...]).astype(BF)

        if block == 0:

            @pl.when(at < tiles)
            def _():
                for c in range(0, tile, 128):
                    outs[1][:, c : c + 128] = (turned(c).astype(jnp.float32) * scale).astype(BF)

        @pl.when(at >= tiles)
        def _():
            both_ref = outs[2] if block == 0 else outs[1]
            for c in range(0, tile, 256):
                both_ref[:, c : c + 128] = turned(c)
                both_ref[:, c + 128 : c + 256] = found[:, c + 128 : c + 256].astype(BF)

    table = pl.BlockSpec((rows, 128), lambda j, order: (block, 0))
    outs = [(whole((width, rows)), array((width, rows)))]
    if block == 0:
        outs.append(
            (
                pl.BlockSpec((rows, tile), lambda j, order: (0, jnp.minimum(j, tiles - 1))),
                array((rows, width)),
            )
        )
    outs.append(
        (
            pl.BlockSpec((rows, tile), lambda j, order: (0, jnp.maximum(j + skip - tiles, 0))),
            array((rows, 2 * width)),
        )
    )
    if block == 0:
        outs.append((whole((8, width)), array((8, width), jnp.float32)))
        edges = [
            pl.BlockSpec((piece.shape[0], 128), lambda j, order: (0, 3 * width // 128))
            for piece in mixed
        ]
    else:
        edges = [whole((8, width))]
    found_outs = len(outs)
    return call(
        body,
        order,
        (3 * tiles - skip,),
        [whole((rows, width)), table, table]
        + [
            pl.BlockSpec((piece.shape[0], tile), lambda j, order: (0, j + skip)) for piece in mixed
        ]
        + edges,
        outs,
        (source, cosine, sine, *mixed, *(mixed if block == 0 else [cols])),
        f"project{block}",
        32 * rows * width * width * (2 if block else 3),
        scratch=[pltpu.VMEM((rows, width), BF)],
    )


def attend(order, valid, block, state, last, queries, both):
    rows, width = queries.shape
    pairs = width // 128
    first = state is None

    def body(order_ref, valid_ref, q_ref, kv_ref, *refs):
        outs = refs if first else refs[2:]
        parts = head_parts(q_ref[...])
        keys = kv_ref[:, :128]
        flipped = kv_ref[:, 128:].T
        tops, masses, sums = [], [], []
        for head in range(2):
            scores = nt(keys, parts[head])
            seat = lax.broadcasted_iota(jnp.int32, scores.shape, 0)
            scores = jnp.where(seat < valid_ref[block], scores, masked_score)
            top = jnp.max(scores, axis=0, keepdims=True)
            if not first:
                top = jnp.maximum(top, refs[0][0, head : head + 1, :])
            expo = jnp.exp(scores - top)
            mass = jnp.sum(expo, axis=0, keepdims=True)
            held = jnp.dot(
                flipped[head * HD : (head + 1) * HD, :],
                expo.astype(BF),
                preferred_element_type=jnp.float32,
            )
            if not first:
                factor = jnp.exp(refs[0][0, head : head + 1, :] - top)
                mass = mass + refs[0][0, head + 2 : head + 3, :] * factor
                held = held + refs[1][head * HD : (head + 1) * HD, :] * factor
            tops.append(top)
            masses.append(mass)
            sums.append(held)
        blank = jnp.zeros((4, rows), jnp.float32)
        if last:
            found = jnp.concatenate([s / m for s, m in zip(sums, masses)], axis=0)
            outs[1][...] = found.astype(BF)
            found = found.T
            outs[0][...] = found.astype(BF)
            outs[2][...] = found
            lse = [t + jnp.log(m) for t, m in zip(tops, masses)]
            outs[3][...] = jnp.concatenate(lse + masses + [blank], axis=0)[None]
        else:
            outs[0][...] = jnp.concatenate(tops + masses + [blank], axis=0)[None]
            outs[1][...] = jnp.concatenate(sums, axis=0)

    column = pl.BlockSpec((rows, 128), lambda j, order: (0, j))
    stats = pl.BlockSpec((1, 8, rows), lambda j, order: (j, 0, 0))
    carried = pl.BlockSpec((128, rows), lambda j, order: (j, 0))
    stats_shape = array((pairs, 8, rows), jnp.float32)
    if last:
        outs = [
            (column, array((rows, width))),
            (carried, array((width, rows))),
            (column, array((rows, width), jnp.float32)),
            (stats, stats_shape),
        ]
    else:
        outs = [(stats, stats_shape), (carried, array((width, rows), jnp.float32))]
    return call(
        body,
        order,
        (pairs,),
        [
            pl.BlockSpec(memory_space=pltpu.SMEM),
            pl.BlockSpec((rows, 128), lambda j, order: (0, order[j])),
            pl.BlockSpec((rows, 256), lambda j, order: (0, order[j])),
        ]
        + ([] if first else [stats, carried]),
        outs,
        (valid, queries, both, *(() if first else state)),
        f"attend{block}",
        256 * rows * rows * width,
        transcendentals=16 * rows * rows,
    )


def attend_back(order, valid, block, held, last, queries, both, go, attended, lse, cosine, sine):
    rows, width = queries.shape
    pairs = width // 128
    scale = 1.0 / math.sqrt(HD)
    first = held is None

    def body(order_ref, valid_ref, q_ref, kv_ref, go_ref, o_ref, lse_ref, cos_ref, sin_ref, *refs):
        dq_ref, dkv_ref = refs[-2:]
        keys = kv_ref[:, :128]
        values = kv_ref[:, 128:]
        go_all = go_ref[...]
        q_parts = head_parts(q_ref[...])
        go_parts = head_parts(go_all)
        crossed = (go_all.astype(jnp.float32) * o_ref[...]).T
        flipped = keys.T
        dk = jnp.zeros((rows, 128), jnp.float32)
        dv = jnp.zeros((rows, 128), jnp.float32)
        dq = []
        for head in range(2):
            delta = jnp.sum(crossed[head * HD : (head + 1) * HD, :], axis=0, keepdims=True)
            scores = nt(keys, q_parts[head])
            seat = lax.broadcasted_iota(jnp.int32, scores.shape, 0)
            scores = jnp.where(seat < valid_ref[block], scores, masked_score)
            probs = jnp.exp(scores - lse_ref[0, head : head + 1, :])
            grad_probs = nt(values, go_parts[head])
            grad_scores = (probs * (grad_probs - delta)).astype(BF)
            dv = dv + jnp.dot(probs.astype(BF), go_parts[head], preferred_element_type=jnp.float32)
            dk = dk + jnp.dot(grad_scores, q_parts[head], preferred_element_type=jnp.float32)
            dq.append(
                jnp.dot(
                    flipped[head * HD : (head + 1) * HD, :],
                    grad_scores,
                    preferred_element_type=jnp.float32,
                )
            )
        dkv_ref[:, :128] = turn(dk, cos_ref[...], -sin_ref[...]).astype(BF)
        dkv_ref[:, 128:] = dv.astype(BF)
        found = jnp.concatenate(dq, axis=0)
        if not first:
            found = found + refs[0][...]
        if last:
            dq_ref[...] = turn(found.T * scale, cos_ref[...], -sin_ref[...]).astype(BF)
        else:
            dq_ref[...] = found

    column = pl.BlockSpec((rows, 128), lambda j, order: (0, j))
    natural = pl.BlockSpec((rows, 128), lambda j, order: (0, order[j]))
    natural_both = pl.BlockSpec((rows, 256), lambda j, order: (0, order[j]))
    carried = pl.BlockSpec((128, rows), lambda j, order: (j, 0))
    table = pl.BlockSpec((rows, 128), lambda j, order: (block, 0))
    return call(
        body,
        order,
        (pairs,),
        [
            pl.BlockSpec(memory_space=pltpu.SMEM),
            natural,
            natural_both,
            column,
            column,
            pl.BlockSpec((1, 8, rows), lambda j, order: (j, 0, 0)),
            table,
            table,
        ]
        + ([] if first else [carried]),
        [
            (natural, array((rows, width))) if last else (carried, array((width, rows), jnp.float32)),
            (natural_both, array((rows, 2 * width))),
        ],
        (valid, queries, both, go, attended, lse, cosine, sine, *(() if first else (held,))),
        f"attend_back{block}",
        40 * rows * rows * width,
        transcendentals=16 * rows * rows,
    )


def middle(order, attended, mixed, tokens, cols):
    rows, width = tokens.shape
    count = len(mixed)
    last = mixed[0].shape[1] // width - 1
    chunk = math.gcd(rows, 256)

    def body(order_ref, o_ref, x_ref, cols_ref, *refs):
        weights = refs[:count]
        resid_ref, two_ref, flipped_ref, held = refs[count:]
        found = x_ref[...].astype(jnp.float32) + by_pieces(o_ref, weights)
        resid_ref[...] = found
        spread(order_ref, resid_ref, held, slice(None))
        two = layer_norm(held[...], cols_ref[2:3, :], cols_ref[3:4, :]).astype(BF)
        two_ref[...] = two
        flipped_ref[...] = two.T

    line = pl.BlockSpec((chunk, width), lambda i, order: (i, 0))
    return call(
        body,
        order,
        (rows // chunk,),
        [line, line, whole((8, width))]
        + [pl.BlockSpec((piece.shape[0], width), lambda i, order: (0, last)) for piece in mixed],
        [
            (line, array((rows, width), jnp.float32)),
            (line, array((rows, width))),
            (pl.BlockSpec((width, chunk), lambda i, order: (0, i)), array((width, rows))),
        ],
        (attended, tokens, cols, *mixed),
        "middle",
        2 * rows * width * width,
        scratch=[pltpu.VMEM((chunk, width), jnp.float32)],
    )


def feed(order, two, pair):
    rows, width = two.shape
    blocks = order.shape[0]
    hidden = (pair[0].shape[1] - width) // 2
    part = hidden // blocks
    count = len(pair)

    def body(order_ref, two_ref, *refs):
        gate_ref, up_ref, hidden_ref, flipped_ref = refs[count:]
        found = by_pieces(two_ref, refs[:count])
        gate, up = found[:, :part], found[:, part:]
        made = (gate / (1.0 + jnp.exp(-gate)) * up).astype(BF)
        gate_ref[...] = gate.astype(BF)
        up_ref[...] = up.astype(BF)
        hidden_ref[...] = made
        flipped_ref[...] = made.T

    tile = pl.BlockSpec((rows, part), lambda j, order: (0, j))
    shape = array((rows, hidden))
    return call(
        body,
        order,
        (blocks,),
        [whole((rows, width))]
        + [
            pl.BlockSpec((piece.shape[0], 2 * part), lambda j, order: (0, order[j]))
            for piece in pair
        ],
        [
            (tile, shape),
            (tile, shape),
            (tile, shape),
            (pl.BlockSpec((part, rows), lambda j, order: (j, 0)), array((hidden, rows))),
        ],
        (two, *pair),
        "feed",
        4 * rows * width * hidden,
        transcendentals=rows * hidden,
    )


def feed_back(order, upstream, gate, up, made, resid, pair, down):
    rows, width = upstream.shape
    blocks = order.shape[0]
    hidden = gate.shape[1]
    part = hidden // blocks
    count, downs = len(pair), len(down)
    each = blocks // downs

    def body(order_ref, m_ref, gate_ref, up_ref, made_ref, resid_ref, *refs):
        pairs, lows = refs[:count], refs[count : count + downs]
        out_ref, grads_ref, two_ref, total, result = refs[count + downs :]
        at = pl.program_id(0)

        @pl.when(at == 0)
        def _():
            total[...] = jnp.zeros_like(total)
            result[...] = resid_ref[...]

        def one(low):
            gate_all = gate_ref[...].astype(jnp.float32)
            up_all = up_ref[...].astype(jnp.float32)
            sigma = 1.0 / (1.0 + jnp.exp(-gate_all))
            made_grad = nt(m_ref[...], low[...])
            result[...] += jnp.dot(made_ref[...], low[...], preferred_element_type=jnp.float32)
            gate_grad = made_grad * up_all * sigma * (1.0 + gate_all * (1.0 - sigma))
            grads_ref[:, :part] = gate_grad.astype(BF)
            grads_ref[:, part:] = (made_grad * gate_all * sigma).astype(BF)

        for i in range(downs):

            @pl.when((at >= i * each) & (at < (i + 1) * each))
            def _(i=i):
                one(lows[i])

        grads = grads_ref[...]
        low = 0
        for piece in pairs:
            high = low + piece.shape[0]
            total[:, low:high] += nt(grads, piece[...])
            low = high

        @pl.when(at == blocks - 1)
        def _():
            out_ref[...] = result[...].astype(BF)
            collect(order_ref, total, two_ref)

    tile = pl.BlockSpec((rows, part), lambda j, order: (0, j))
    return call(
        body,
        order,
        (blocks,),
        [whole((rows, width)), tile, tile, tile, whole((rows, width))]
        + [
            pl.BlockSpec((piece.shape[0], 2 * part), lambda j, order: (0, order[j]))
            for piece in pair
        ]
        + [
            pl.BlockSpec(
                (part, width), lambda j, order, i=i: (jnp.clip(j - i * each, 0, each - 1), 0)
            )
            for i in range(downs)
        ],
        [
            (whole((rows, width)), array((rows, width))),
            (
                pl.BlockSpec((rows, 2 * part), lambda j, order: (0, order[j])),
                array((rows, 2 * hidden)),
            ),
            (whole((rows, width)), array((rows, width), jnp.float32)),
        ],
        (upstream, gate, up, made, resid, *pair, *down),
        "feed_back",
        8 * rows * width * hidden,
        scratch=[pltpu.VMEM((rows, width), jnp.float32), pltpu.VMEM((rows, width), jnp.float32)],
        transcendentals=rows * hidden,
    )


def norm_back(values, grads, gain):
    centre = values - jnp.mean(values, axis=-1, keepdims=True)
    scale = lax.rsqrt(jnp.mean(centre * centre, axis=-1, keepdims=True) + epsilon)
    normed = centre * scale
    scaled = grads * gain
    inner = jnp.mean(scaled * normed, axis=-1, keepdims=True)
    found = (scaled - jnp.mean(scaled, axis=-1, keepdims=True) - normed * inner) * scale
    return (
        found,
        jnp.sum(grads * normed, axis=0, keepdims=True),
        jnp.sum(grads, axis=0, keepdims=True),
    )


def middle_back(order, grads, resid, upstream, mixed, gain):
    rows, width = resid.shape
    count = len(mixed)
    last = mixed[0].shape[1] // width - 1
    chunk = math.gcd(rows, 256)

    def body(order_ref, grads_ref, resid_ref, m_ref, gain_ref, *refs):
        weights = refs[:count]
        y_ref, a_ref, go_ref, edge_ref = refs[count:]

        @pl.when(pl.program_id(0) == 0)
        def _():
            edge_ref[...] = jnp.zeros_like(edge_ref)

        found, gain_grad, shift_grad = norm_back(resid_ref[...], grads_ref[...], gain_ref[...])
        found = m_ref[...].astype(jnp.float32) + found
        edge_ref[0:1, :] += gain_grad
        edge_ref[1:2, :] += shift_grad
        y_ref[...] = found
        a_ref[...] = found.astype(BF)
        low = 0
        for weight in weights:
            high = low + weight.shape[0]
            go_ref[:, low:high] = nt(a_ref[...], weight[...]).astype(BF)
            low = high

    line = pl.BlockSpec((chunk, width), lambda i, order: (i, 0))
    return call(
        body,
        order,
        (rows // chunk,),
        [line, line, line, whole((1, width))]
        + [pl.BlockSpec((piece.shape[0], width), lambda i, order: (0, last)) for piece in mixed],
        [
            (line, array((rows, width), jnp.float32)),
            (line, array((rows, width))),
            (line, array((rows, width))),
            (whole((8, width)), array((8, width), jnp.float32)),
        ],
        (grads, resid, upstream, gain[None, :], *mixed),
        "middle_back",
        2 * rows * width * width,
    )


def pull(order, dq, both, mixed, block):
    rows, width = both.shape[0], both.shape[1] // 2
    tile = 512
    tiles = width // tile
    count = len(mixed)
    skip = 0 if block == 0 else tiles
    steps = 3 * tiles - skip
    dtype = BF if block else jnp.float32

    def body(order_ref, *refs):
        lefts = refs[: 1 if block else 2]
        weights = refs[len(lefts) : len(lefts) + count]
        out_ref, total = refs[len(lefts) + count :]
        at = pl.program_id(0)

        @pl.when(at == 0)
        def _():
            total[...] = jnp.zeros_like(total)

        def one(left):
            low = 0
            for weight in weights:
                high = low + weight.shape[0]
                total[:, low:high] += nt(left[...], weight[...])
                low = high

        if block:
            one(lefts[0])
        else:

            @pl.when(at < tiles)
            def _():
                one(lefts[0])

            @pl.when(at >= tiles)
            def _():
                one(lefts[1])

        @pl.when(at == steps - 1)
        def _():
            out_ref[...] = total[...].astype(dtype)

    lefts = [] if block else [pl.BlockSpec((rows, tile), lambda j, order: (0, jnp.minimum(j, tiles - 1)))]
    lefts.append(pl.BlockSpec((rows, tile), lambda j, order: (0, jnp.maximum(j + skip - tiles, 0))))
    return call(
        body,
        order,
        (steps,),
        lefts
        + [
            pl.BlockSpec((piece.shape[0], tile), lambda j, order: (0, j + skip)) for piece in mixed
        ],
        [(whole((rows, width)), array((rows, width), dtype))],
        ((both,) if block else (dq, both)) + tuple(mixed),
        f"pull{block}",
        rows * width * (1 if block else 96 * width),
        scratch=[pltpu.VMEM((rows, width), jnp.float32)],
    )[0]


def end_back(order, parts, tokens, grads, gain):
    rows, width = tokens.shape
    count = len(parts)
    chunk = math.gcd(rows, 256)

    def body(order_ref, x_ref, y_ref, gain_ref, *refs):
        sources = refs[:count]
        out_ref, edge_ref, held, total = refs[count:]

        @pl.when(pl.program_id(0) == 0)
        def _():
            edge_ref[...] = jnp.zeros_like(edge_ref)

        held[...] = sum(source[...].astype(jnp.float32) for source in sources)
        collect(order_ref, held, total)
        found, gain_grad, shift_grad = norm_back(
            x_ref[...].astype(jnp.float32), total[...], gain_ref[...]
        )
        edge_ref[0:1, :] += gain_grad
        edge_ref[1:2, :] += shift_grad
        out_ref[...] = (y_ref[...] + found).astype(BF)

    line = pl.BlockSpec((chunk, width), lambda i, order: (i, 0))
    return call(
        body,
        order,
        (rows // chunk,),
        [line, line, whole((1, width))] + [line] * count,
        [(line, array((rows, width))), (whole((8, width)), array((8, width), jnp.float32))],
        (tokens, grads, gain[None, :], *parts),
        "end_back",
        0,
        scratch=[pltpu.VMEM((chunk, width), jnp.float32), pltpu.VMEM((chunk, width), jnp.float32)],
    )


def join(first, second, part):
    rows, width = first.shape
    stacked = jnp.stack([first.reshape(rows, -1, part), second.reshape(rows, -1, part)], axis=2)
    return stacked.reshape(rows, 2 * width)


def part_ways(both, part):
    rows, width = both.shape
    cut = both.reshape(rows, -1, 2, part)
    return cut[:, :, 0].reshape(rows, width // 2), cut[:, :, 1].reshape(rows, width // 2)


def shards(
    plan,
    tokens,
    lengths,
    cotangent,
    query_weight,
    key_weight,
    value_weight,
    output_weight,
    gate_weight,
    up_weight,
    down_weight,
    attention_gain,
    attention_shift,
    feed_gain,
    feed_shift,
):
    slots = plan.slots()
    windows, local_len, width = tokens.shape
    rows = windows * local_len
    hidden = gate_weight.shape[1]
    place = lax.axis_index("ctx")
    exact = (width // plan.dp) % 128 == 0
    order = slots if exact else jnp.arange(8, dtype=jnp.int32)
    part = hidden // order.shape[0]

    def pieces_of(chain, shard):
        if exact:
            return chain.value
        return [assemble(slots, chain.value, shard.shape[0] * plan.ctx)]

    def in_slots(flipped):
        if exact:
            return flipped
        cut = flipped.reshape(plan.dp, -1, flipped.shape[1])
        return jnp.take(cut, slots, axis=0).reshape(flipped.shape)

    edge = jnp.stack([attention_gain, attention_shift, feed_gain, feed_shift], axis=1)
    edge = jnp.pad(edge, ((0, 0), (0, 124)))
    both = join(key_weight, value_weight, 128)
    mixed = jnp.concatenate([query_weight, both, edge], axis=1)
    mix = Chain(gather_steps(plan, mixed))

    seats = jnp.arange(local_len, dtype=jnp.int32)
    starts = jnp.asarray(plan.blocks)[place] * local_len
    valid = jnp.clip(lengths[0] - starts, 0, local_len)
    cosine, sine = rotary_tables((starts[:, None] + seats[None, :]).reshape(-1))
    real = (place * local_len + seats < lengths[0])[:, None]
    upstream = jnp.where(real, cotangent.reshape(rows, width), 0)
    own = tokens.reshape(rows, width)

    pair_own = jnp.concatenate([join(gate_weight, up_weight, part), output_weight], axis=1)
    early = (pair_own, cosine, sine, upstream)
    pair_own, cosine, sine, upstream = step(early, mix)
    pair = Chain(gather_steps(plan, pair_own, line=True))
    own = step(own, mix, pair)
    own = step(own, mix, pair)
    came = {}
    own, window = begin(own, window_steps(plan, own, came))
    own = finish(own, mix)
    mixed_w = pieces_of(mix, mixed)
    back = jnp.asarray(plan.back)[lax.axis_index("dp")] if exact else order

    flipped, both = {}, {}
    cols = None
    flipped[0], queries, both[0], cols = project(order, own, cols, mixed_w, cosine, sine, 0)
    both[0] = step(both[0], pair)
    state = attend(order, valid, 0, None, plan.ctx == 1, queries, both[0])
    down = None
    for k in range(1, plan.ctx):
        while k not in came:
            state = step(state, window)
        if k == min(3, plan.ctx - 1):
            down_own, state = tie(down_weight, state)
            down = Chain(gather_steps(plan, down_own))
        flipped[k], both[k] = project(order, came[k], cols, mixed_w, cosine, sine, k)
        if k in (1, plan.ctx - 1):
            both[k] = step(both[k], pair)
        state = attend(order, valid, k, state, k == plan.ctx - 1, queries, both[k])
    state = step(state, pair, down)
    state = finish(state, pair)
    pair_w = pieces_of(pair, pair_own)
    natural = cols[:4].reshape(4, order.shape[0], -1)[:, back].reshape(4, width)
    low, low_flipped, attended, lse = state
    resid, two, two_flipped = middle(order, low, pair_w, own, cols)
    two = step(two, down)
    gate, up, made, made_flipped = feed(order, two, pair_w)
    product = product_of(plan, [[(in_slots(made_flipped), upstream)]])
    first = product(plan.dp // 2, plan.dp)
    made, first = finish((made, first), down)
    made, down_sum = begin(made, sum_steps(plan, product, first))
    down_w = pieces_of(down, down_weight)
    output, pair_grads, two_grads = feed_back(
        order, upstream, gate, up, made, resid, pair_w, down_w
    )
    output = output.reshape(windows, local_len, width)

    product = product_of(plan, [[(in_slots(two_flipped), pair_grads)]])
    first = product(plan.dp // 2, plan.dp)
    first, two_grads = wait((first, two_grads), down_sum)
    two_grads, pair_sum = begin(two_grads, sum_steps(plan, product, first))
    two_grads = go_on(two_grads, down_sum)
    y_grads, low_grads, go, edge_two = middle_back(
        order, two_grads, resid, upstream, pair_w, natural[2]
    )
    go = step(go, pair_sum)
    go, output_sum = begin(
        go, sum_steps(plan, product_of(plan, [[(in_slots(low_flipped), low_grads)]]))
    )
    held, back_way = None, None
    grads, parts = {}, {}
    flipped = {k: in_slots(flipped[k]) for k in flipped}
    for k in reversed(range(plan.ctx)):
        held, grads[k] = attend_back(
            order, valid, k, held, k == 0, queries, both[k], go, attended, lse, cosine, sine
        )
        if k:
            if k == plan.ctx - 1:
                held = step(held, down_sum, output_sum)
            else:
                held = step(held, pair_sum)
                if plan.line:
                    held = wait(held, back_way)
            held, grads[k] = tie(held, grads[k])
            parts[k] = pull(order, held, grads[k], mixed_w, k)
            held, parts[k] = tie(held, parts[k])
            if plan.line:
                if back_way is None:
                    held, back_way = begin(held, return_steps(plan, parts))
                else:
                    held = go_on(held, back_way)
            if k < plan.ctx - 1:
                held = step(held, down_sum, output_sum)
    finals = [down_sum, output_sum, pair_sum]
    held = wait(held, *finals)
    groups = [[(flipped[0], held)], [(flipped[k], grads[k]) for k in range(plan.ctx)]]
    held, last_sum = begin(held, sum_steps(plan, product_of(plan, groups)))
    held = go_on(held, down_sum, output_sum)
    held = step(held, last_sum)
    held = go_on(held, pair_sum)
    part_grads = pull(order, held, grads[0], mixed_w, 0)
    part_grads = finish(part_grads, down_sum, output_sum, *([back_way] if plan.line else []))
    part_grads = step(part_grads, last_sum)
    if plan.line:
        sends = back_way.value
    else:
        sends = [lax.ppermute(parts[k], AXES, plan.across[k]) for k in range(1, plan.ctx)]
    tokens_grad, edge_one = end_back(
        order, [part_grads, *sends], own, y_grads, natural[0]
    )
    edge_one = step(edge_one, pair_sum)
    edge_one = step(edge_one, last_sum)
    vectors = sum_vectors(plan, (edge_one[0], edge_one[1], edge_two[0], edge_two[1]))
    finish((), pair_sum)
    pair_grads = pair_sum.value
    for _ in range(plan.ctx_bits - 1):
        pair_grads = step(pair_grads, last_sum)
    finish((), last_sum)
    gate_grad, up_grad = part_ways(pair_grads, part)
    key_grad, value_grad = part_ways(last_sum.value[:, width:], 128)
    return (
        output,
        tokens_grad.reshape(windows, local_len, width),
        last_sum.value[:, :width],
        key_grad,
        value_grad,
        output_sum.value,
        gate_grad,
        up_grad,
        down_sum.value,
        *vectors,
    )


def solution(mesh):
    return jax.shard_map(
        functools.partial(shards, Plan(mesh)),
        mesh=mesh,
        in_specs=(
            P("dp", "ctx", None),
            P("dp"),
            P("dp", "ctx", None),
            P(("dp", "ctx"), None),
            P(("dp", "ctx"), None),
            P(("dp", "ctx"), None),
            P(("dp", "ctx"), None),
            P(("dp", "ctx"), None),
            P(("dp", "ctx"), None),
            P(("dp", "ctx"), None),
            P(("dp", "ctx")),
            P(("dp", "ctx")),
            P(("dp", "ctx")),
            P(("dp", "ctx")),
        ),
        out_specs=(
            P("dp", "ctx", None),
            P("dp", "ctx", None),
            P(("dp", "ctx"), None),
            P(("dp", "ctx"), None),
            P(("dp", "ctx"), None),
            P(("dp", "ctx"), None),
            P(("dp", "ctx"), None),
            P(("dp", "ctx"), None),
            P(("dp", "ctx"), None),
            P(("dp", "ctx")),
            P(("dp", "ctx")),
            P(("dp", "ctx")),
            P(("dp", "ctx")),
        ),
        check_vma=False,
    )
```
